128 devices in a mesh: dp: 8 (over x, core), mem: 16 (over z, y).
Axes of the slice: x: 4, y: 4, z: 4, core: 2. Of those that a mesh axis runs over, the one named last changes fastest.
Arguments:
- tokens: bfloat16 [16384, 2048], P(('dp', 'mem')), may hold values from -60 to 60
- norm_gain: float32 [2048], replicated, may hold values from 0.1 to 1.9
- query_weight: bfloat16 [2048, 2048], P(None, 'dp'), may hold values from -0.125 to 0.125
- values: bfloat16 [131072, 2048], P(('dp', 'mem')), may hold values from -6 to 6
- blocks: int32 [16384, 2], P(('dp', 'mem')), may hold values from 0 to 2047, as said below
- weights: float32 [16384, 2], P(('dp', 'mem')), may hold values from 0.25 to 1
- out_cotangent: bfloat16 [16384, 2048], P(('dp', 'mem')), may hold values from -6 to 6
Outputs:
- layer_out: float32 [16384, 2048], P(('dp', 'mem'))
- grad_tokens: float32 [16384, 2048], P(('dp', 'mem'))
- grad_values: bfloat16 [131072, 2048], P(('dp', 'mem'))
The draws below stay inside these ranges and needn't reach their ends.
Inputs may be any that keep to these rules, and one draw needn't show every extreme that they name: Block b is held by device b // 16, devices counted as the tokens are (dp major, mem minor). The 2 blocks of one token differ. The tokens of one device make at most 4 lookups (repeats counted) into the blocks held by any one device, and in every draw some devices receive exactly 4 lookups from the tokens of every device.
All inputs are finite; a program needn't handle non-finite values.
Results may differ from the reference program's by a relative error of at most 0.012.
Values may be sent and summed in bfloat16 or wider, within the bound.
No kernel may reach another device: no remote copies, remote signals or barrier semaphores. Data moves between devices by JAX's collectives and lax.ppermute only.
A program may use at most 128 MiB of HBM per device.

```python
import math
import jax
import jax.numpy as jnp
from jax import lax

D = 2048
BLOCK = 64
TOPK = 2
TOK = 128
BLK_DEV = 16
VALUES = 131072
TOKENS = 16384
N_DP = 8
N_MEM = 16


def draw_tokens(key, part):
    key_rows, key_cols, key_noise = jax.random.split(key, 3)
    row_scale = jnp.exp(jax.random.uniform(key_rows, (TOKENS, 1), jnp.float32) * math.log(10.0))
    noise = jnp.clip(jax.random.normal(key_noise, (TOKENS, D), jnp.float32), -6.0, 6.0)
    col_scale = jnp.exp(jax.random.uniform(key_cols, (1, D), jnp.float32) * math.log(10.0))
    return (noise * row_scale * col_scale * 0.1).astype(jnp.bfloat16)


def draw_blocks(key, part):
    owner_count = N_DP * N_MEM
    pair_count = TOK * TOPK
    capacity = 2 * pair_count // owner_count
    hot_count = owner_count // 8
    cold_count = owner_count - hot_count
    rest_count = pair_count - hot_count * capacity
    base_count = rest_count // cold_count
    extra_count = rest_count % cold_count
    shuffle_order = jax.random.permutation(jax.random.fold_in(key, 11), owner_count)
    order_rank = jnp.argsort(shuffle_order, stable=True).astype(jnp.int32)

    def one_source(source):
        source_key = jax.random.fold_in(jax.random.fold_in(key, 23), source)
        key_extra, key_shuffle, key_local = jax.random.split(source_key, 3)
        lucky_rank = jax.random.permutation(key_extra, cold_count)
        chosen = jnp.take(lucky_rank, jnp.clip(order_rank - hot_count, 0, cold_count - 1)) < extra_count
        per_owner = jnp.where(order_rank < hot_count, capacity, base_count + chosen.astype(jnp.int32))
        bounds = jnp.cumsum(per_owner)
        owners_of = jnp.searchsorted(bounds, jnp.arange(pair_count, dtype=jnp.int32), side='right').astype(jnp.int32)
        owners_of = owners_of[jax.random.permutation(key_shuffle, pair_count)]
        local_block = jax.random.randint(key_local, (TOK, TOPK), 0, BLK_DEV // TOPK) * TOPK + jnp.arange(TOPK, dtype=jnp.int32)[None, :]
        return owners_of.reshape(TOK, TOPK) * BLK_DEV + local_block
    drawn = jax.vmap(one_source)(jnp.arange(owner_count, dtype=jnp.int32))
    return drawn.reshape(owner_count * TOK, TOPK).astype(jnp.int32)


def levels(key, extent, cuts, least, top_value):
    factor_of = 1.0
    for axis_at, blocks in cuts:
        heights = jax.random.uniform(jax.random.fold_in(jax.random.fold_in(key, 6), axis_at), (blocks,), jnp.float32, least / len(cuts), top_value / len(cuts))
        factor_of = factor_of * jnp.repeat(jnp.exp(heights), extent[axis_at] // blocks).reshape((-1,) + (1,) * (len(extent) - 1 - axis_at))
    return factor_of


def centred(own_key, extent, width, most, cuts=(), kind=jnp.bfloat16):
    values = jax.random.normal(own_key, extent, jnp.float32) * width
    if len(cuts) > 0:
        values = levels(own_key, extent, cuts, -0.22, 0.18) * values
    return jnp.clip(values, min=-most, max=most).astype(kind)


def setup_inputs(seed: int = 0) -> dict:
    key_of = jax.random.split(jax.random.key(seed), 8)
    tokens = draw_tokens(jax.random.fold_in(key_of[7], 71), 0)
    norm_gain = jnp.clip(1.0 + 0.18 * jax.random.normal(key_of[1], (D,), jnp.float32), 0.1, 1.9)
    query_weight = centred(key_of[2], (D, D), D ** -0.5, 0.125, ((1, 8),))
    values = centred(key_of[3], (VALUES, D), 1.0, 6.0, ((0, 128),))
    blocks = draw_blocks(jax.random.fold_in(key_of[7], 71), 0)
    weights = jnp.clip(jnp.exp(math.log(1.0) - 1.3862944 * jax.random.uniform(key_of[5], (TOKENS, TOPK), jnp.float32) ** levels(key_of[5], (TOKENS, TOPK), ((0, 128),), -0.2, 0.2)), 0.25, 1.0)
    out_cotangent = centred(key_of[6], (TOKENS, D), 1.0, 6.0, ((0, 128),))
    return {"tokens": tokens, "norm_gain": norm_gain, "query_weight": query_weight, "values": values, "blocks": blocks, "weights": weights, "out_cotangent": out_cotangent}


def reference(tokens, norm_gain, query_weight, values, blocks, weights, out_cotangent):
    score_scale = float(D) ** (-0.5)
    exact_tokens = tokens.astype(jnp.float32)
    rms_rows = lax.rsqrt(lax.optimization_barrier(jnp.mean(exact_tokens * exact_tokens, axis=1, keepdims=True)) + 1e-06)
    unit_rows = exact_tokens * rms_rows
    normed = (unit_rows * norm_gain).astype(jnp.bfloat16)
    queries = jnp.dot(normed, query_weight, preferred_element_type=jnp.float32).astype(jnp.bfloat16)
    offsets = jnp.arange(BLOCK, dtype=jnp.int32)
    group_count = TOKENS // TOK

    def scan_step(grad_rows, group_index):
        start = (group_index * TOK).astype(jnp.int32)
        query_block = lax.dynamic_slice_in_dim(queries, start, TOK, 0)
        token_block = lax.dynamic_slice_in_dim(exact_tokens, start, TOK, 0)
        cot_block = lax.dynamic_slice_in_dim(out_cotangent, start, TOK, 0).astype(jnp.float32)
        block_ids = lax.dynamic_slice_in_dim(blocks, start, TOK, 0).astype(jnp.int32)
        weight_block = lax.dynamic_slice_in_dim(weights, start, TOK, 0)
        row_ids = (block_ids[:, :, None] * BLOCK + offsets[None, None, :]).astype(jnp.int32)
        gathered = jnp.take(values, row_ids.reshape(-1), axis=0).reshape(TOK, TOPK, BLOCK, D).astype(jnp.float32)
        query_exact = query_block.astype(jnp.float32)
        scores = jnp.einsum('cd,ckjd->ckj', query_exact, gathered) * score_scale
        sigmoid_of = jax.nn.sigmoid(scores)
        gate_values = sigmoid_of.astype(jnp.bfloat16)
        block_parts = jnp.einsum('ckj,ckjd->ckd', gate_values.astype(jnp.float32), gathered).astype(jnp.bfloat16)
        mixed = lax.optimization_barrier(jnp.sum(weight_block[:, :, None] * block_parts.astype(jnp.float32), axis=1))
        out_block = token_block + mixed
        scaled_cot = (weight_block[:, :, None] * cot_block[:, None, :]).astype(jnp.bfloat16)
        cot_scores = jnp.einsum('ckd,ckjd->ckj', scaled_cot.astype(jnp.float32), gathered)
        score_grads = (cot_scores * sigmoid_of * (1.0 - sigmoid_of) * score_scale).astype(jnp.bfloat16)
        query_parts = jnp.einsum('ckj,ckjd->ckd', score_grads.astype(jnp.float32), gathered).astype(jnp.bfloat16)
        query_grad = lax.optimization_barrier(jnp.sum(query_parts.astype(jnp.float32), axis=1)).astype(jnp.bfloat16)
        contrib = gate_values.astype(jnp.float32)[:, :, :, None] * scaled_cot.astype(jnp.float32)[:, :, None, :]
        contrib = contrib + score_grads.astype(jnp.float32)[:, :, :, None] * query_exact[:, None, None, :]
        grad_rows = grad_rows.at[row_ids.reshape(-1)].add(contrib.reshape(-1, D))
        return (grad_rows, (out_block, query_grad))
    grad_rows, (out_blocks, query_grads) = lax.scan(scan_step, jnp.zeros((VALUES, D), jnp.float32), jnp.arange(group_count, dtype=jnp.int32))
    layer_out = out_blocks.reshape(TOKENS, D)
    query_grad = query_grads.reshape(TOKENS, D)
    normed_grad = jnp.dot(query_grad, query_weight.T, preferred_element_type=jnp.float32)
    unit_grad = normed_grad * norm_gain
    grad_tokens = out_cotangent.astype(jnp.float32) + rms_rows * (unit_grad - unit_rows * lax.optimization_barrier(jnp.mean(unit_grad * unit_rows, axis=1, keepdims=True)))
    return (layer_out, grad_tokens, grad_rows.astype(jnp.bfloat16))
```

```python
import functools

import jax
import jax.numpy as jnp
import numpy as np
from jax import lax
from jax.experimental import pallas as pl
from jax.experimental.pallas import tpu as pltpu
from jax.sharding import Mesh
from jax.sharding import PartitionSpec as P

BLOCK = 64
SLOTS = 4
CHUNK = 2 * SLOTS
LANES = 128
ALL = ("x", "core", "z", "y")
BF = jnp.bfloat16
F32 = jnp.float32


def params(megabytes):
    return pltpu.CompilerParams(vmem_limit_bytes=megabytes << 20)


def cost(flops, bytes_accessed):
    return pl.CostEstimate(
        flops=int(flops), bytes_accessed=int(bytes_accessed), transcendentals=0
    )


def whole(shape):
    return pl.BlockSpec(shape, lambda *_: (0,) * len(shape))


def nt(left, right):
    return lax.dot_general(left, right, (((1,), (1,)), ((), ())), preferred_element_type=F32)


def nn(left, right):
    return jnp.dot(left, right, preferred_element_type=F32)


def send_kernel(span, tok_ref, gain_ref, blk_ref, wgt_ref, cot_ref, x_ref, tgt_ref, rows_ref, route_ref):
    step = pl.program_id(0)
    count, features = tok_ref.shape
    step_rows = x_ref.shape[0]

    @pl.when(step == 0)
    def _():
        exact = tok_ref[...].astype(F32)
        rms = lax.rsqrt(jnp.mean(exact * exact, axis=1, keepdims=True) + 1e-06)
        rows_ref[:count, :] = ((exact * rms) * gain_ref[...]).astype(BF)
        rows_ref[count:, :] = cot_ref[...]
        square = (count, count)
        sub = lax.broadcasted_iota(jnp.int32, square, 0)
        lane = lax.broadcasted_iota(jnp.int32, square, 1)
        blocks = blk_ref[...]
        weights = wgt_ref[...]
        col = [jnp.broadcast_to(blocks[:, k : k + 1], square) for k in range(2)]
        row = [c.astype(F32).T.astype(jnp.int32) for c in col]
        wrow = [jnp.broadcast_to(weights[:, k : k + 1], square).T for k in range(2)]
        own_col = [c // span for c in col]
        own_row = [r // span for r in row]
        one = lambda hit: jnp.where(hit, 1, 0)
        before = [
            [one((own_col[0] == own_row[0]) & (sub < lane))],
            [one(own_col[0] == own_row[1]), one((own_col[1] == own_row[1]) & (sub < lane))],
        ]
        before_t = [
            [one((own_row[0] == own_col[0]) & (lane < sub))],
            [one(own_row[0] == own_col[1]), one((own_row[1] == own_col[1]) & (lane < sub))],
        ]
        for k in range(2):
            slot_row = sum(jnp.sum(e, axis=0, keepdims=True) for e in before[k])
            slot_col = sum(jnp.sum(e, axis=1, keepdims=True) for e in before_t[k])
            target = own_row[k][:1, :] * CHUNK + slot_row
            route_ref[k : k + 1, :] = target.astype(F32)
            route_ref[2 + k : 3 + k, :] = (row[k][:1, :] % span).astype(F32) + 1.0
            route_ref[4 + k : 5 + k, :] = wrow[k][:1, :]
            tgt_ref[:, k : k + 1] = own_col[k][:, :1] * CHUNK + slot_col

    route = route_ref[...]
    shape = (step_rows, count)
    number = (lax.broadcasted_iota(jnp.int32, shape, 0) + step * step_rows).astype(F32)
    t0, t1 = route[0:1, :], route[1:2, :]
    n0, n1 = number == t0, number == t1
    c0, c1 = number == t0 + SLOTS, number == t1 + SLOTS
    scale = jnp.sum(jnp.where(c0, route[4:5, :], 0.0) + jnp.where(c1, route[5:6, :], 0.0), axis=1, keepdims=True)
    ident = jnp.sum(
        jnp.where(n0 | c0, route[2:3, :], 0.0) + jnp.where(n1 | c1, route[3:4, :], 0.0),
        axis=1,
        keepdims=True,
    )
    is_cot = (lax.broadcasted_iota(jnp.int32, (step_rows, 1), 0) % CHUNK) >= SLOTS
    scale = jnp.where(is_cot, scale, 1.0)
    pick = jnp.concatenate(
        [jnp.where(n0 | n1, 1.0, 0.0), jnp.where(c0 | c1, 1.0, 0.0)], axis=1
    ).astype(BF)
    width = 512
    for at in range(0, features, width):
        rows = nn(pick, rows_ref[:, at : at + width])
        x_ref[:, at : at + width] = (rows * scale).astype(BF)
    x_ref[:, features:] = jnp.broadcast_to(ident - 1.0, (step_rows, LANES)).astype(BF)


def build_payload(tokens, gain, blocks, weights, cot, owners, span):
    count, features = tokens.shape
    rows = owners * CHUNK
    steps = 4
    return pl.pallas_call(
        functools.partial(send_kernel, span),
        out_shape=(
            jax.ShapeDtypeStruct((rows, features + LANES), BF),
            jax.ShapeDtypeStruct((count, 2), jnp.int32),
        ),
        grid=(steps,),
        in_specs=[
            whole((count, features)),
            whole((1, features)),
            whole((count, 2)),
            whole((count, 2)),
            whole((count, features)),
        ],
        out_specs=(
            pl.BlockSpec((rows // steps, features + LANES), lambda i: (i, 0)),
            whole((count, 2)),
        ),
        scratch_shapes=[pltpu.VMEM((2 * count, features), BF), pltpu.VMEM((8, count), F32)],
        compiler_params=params(24),
        cost_estimate=cost(2 * rows * 2 * count * features, 6 << 20),
    )(tokens, gain, blocks, weights, cot)


def slice_at(step, core, half):
    return jnp.where(step < half, 2 * step + core, 2 * (step - half) + 1 - core)


def slice_specs(half, features, width):
    return [
        pl.BlockSpec((1, features, width), lambda a, core: (jnp.minimum(a, half - 1), 0, 0)),
        pl.BlockSpec((1, features, width), lambda a, core: (jnp.maximum(a - half, 0), 0, 0)),
    ]


def with_slice(half, own_ref, sib_ref, use):
    step = pl.program_id(0)

    @pl.when(step < half)
    def _():
        use(own_ref)

    @pl.when(step >= half)
    def _():
        use(sib_ref)


def fold_kernel(half, core_ref, own_ref, sib_ref, val_ref, out_ref, acc_ref):
    step = pl.program_id(0)
    features = acc_ref.shape[0]
    tile = 256

    def use(w_ref):
        val = val_ref[...]

        @pl.loop(0, features // tile)
        def _(i):
            at = pl.ds(pl.multiple_of(i * tile, tile), tile)
            part = nt(w_ref[0, at, :], val)

            @pl.when(step == 0)
            def _():
                acc_ref[at, :] = part

            @pl.when(step > 0)
            def _():
                acc_ref[at, :] += part

            @pl.when(step == 2 * half - 1)
            def _():
                out_ref[at, :] = acc_ref[at, :].astype(BF)

    with_slice(half, own_ref, sib_ref, use)


def fold_weight(core, own, sib, values):
    half, features, width = own.shape
    value_rows = values.shape[0]
    return pl.pallas_call(
        functools.partial(fold_kernel, half),
        out_shape=jax.ShapeDtypeStruct((features, value_rows), BF),
        grid_spec=pltpu.PrefetchScalarGridSpec(
            num_scalar_prefetch=1,
            grid=(2 * half,),
            in_specs=slice_specs(half, features, width)
            + [pl.BlockSpec((value_rows, width), lambda a, core: (0, slice_at(a, core[0], half)))],
            out_specs=whole((features, value_rows)),
            scratch_shapes=[pltpu.VMEM((features, value_rows), F32)],
        ),
        compiler_params=params(32),
        cost_estimate=cost(2 * features * features * value_rows, 16 << 20),
    )(core, own, sib, values)


def serve_kernel(scale, x_hbm, fold_hbm, val_hbm, y_hbm, g_hbm,
                 x_buf, fold_buf, val_buf, n_buf, c_buf, id_buf, g_buf, y_buf, x_sem, f_sem, v_sem, y_sem, g_sem):
    rows = x_buf.shape[0]
    features = n_buf.shape[1]
    value_rows = val_buf.shape[0]
    parts = x_sem.shape[0]
    step_rows = rows // parts
    step_cols = value_rows // parts
    slots = rows // 2

    def x_copy(i):
        at = pl.ds(pl.multiple_of(i * step_rows, step_rows), step_rows)
        return pltpu.make_async_copy(x_hbm.at[at, :], x_buf.at[at, :], x_sem.at[i])

    def f_copy(i):
        return pltpu.make_async_copy(
            fold_hbm.at[:, pl.ds(pl.multiple_of(i * step_cols, step_cols), step_cols)],
            fold_buf.at[i],
            f_sem.at[i],
        )

    def v_copy(i):
        at = pl.ds(pl.multiple_of(i * step_cols, step_cols), step_cols)
        return pltpu.make_async_copy(val_hbm.at[at, :], val_buf.at[at, :], v_sem.at[i])

    for i in range(parts):
        x_copy(i).start()
    for i in range(parts):
        f_copy(i).start()
        v_copy(i).start()

    take = 32
    low = lax.broadcasted_iota(jnp.int32, (take // 16, 8, 1), 1) < SLOTS

    def split(x):
        pairs = x.astype(F32).reshape(take // 16, 16, x.shape[1])
        first, second = pairs[:, :8], pairs[:, 8:]
        upper = jnp.where(low, first, pltpu.roll(second, 4, 1))
        lower = jnp.where(low, pltpu.roll(first, 4, 1), second)
        return upper.reshape(take // 2, x.shape[1]), lower.reshape(take // 2, x.shape[1])

    for i in range(parts):
        x_copy(i).wait()

        @pl.loop(i * step_rows // take, (i + 1) * step_rows // take)
        def _(r):
            src = pl.ds(pl.multiple_of(r * take, take), take)
            dst = pl.ds(pl.multiple_of(r * (take // 2), take // 2), take // 2)
            upper, lower = split(x_buf[src, :features])
            n_buf[dst, :] = upper.astype(BF)
            c_buf[dst, :] = lower.astype(BF)
            ident, _ = split(x_buf[src, features:])
            id_buf[dst, :] = ident

    lows = lax.broadcasted_iota(jnp.int32, (slots // 8, 8, 1), 1) < SLOTS

    @pl.loop(0, parts)
    def _(j):
        f_copy(j).wait()
        v_copy(j).wait()
        at = pl.ds(pl.multiple_of(j * step_cols, step_cols), step_cols)
        scores = nn(n_buf[...], fold_buf[j]) * scale
        sig = 1.0 / (1.0 + jnp.exp(-scores))
        cot_scores = nt(c_buf[...], val_buf[at, :])
        block_of = (lax.broadcasted_iota(jnp.int32, (1, step_cols), 1) // BLOCK + j * (step_cols // BLOCK)).astype(F32)
        mine = id_buf[:, :1] == block_of
        gates = jnp.where(mine, sig, 0.0).reshape(slots // 8, 8, step_cols)
        grads = jnp.where(mine, cot_scores * sig * (1.0 - sig) * scale, 0.0).reshape(slots // 8, 8, step_cols)
        first = jnp.where(lows, gates, pltpu.roll(grads, 4, 1))
        second = jnp.where(lows, pltpu.roll(gates, 4, 1), grads)
        mixed = jnp.concatenate([first, second], axis=1).reshape(rows, step_cols).astype(BF)
        g_buf[j] = mixed

    def g_copy(i):
        return pltpu.make_async_copy(
            g_buf.at[i], g_hbm.at[:, pl.ds(i * step_cols, step_cols)], g_sem.at[i]
        )

    for i in range(parts):
        g_copy(i).start()

    tiles = y_sem.shape[0]
    width = features // tiles

    def y_copy(i):
        at = pl.ds(pl.multiple_of(i * width, width), width)
        return pltpu.make_async_copy(y_buf.at[i], y_hbm.at[:, at], y_sem.at[i])

    @pl.loop(0, tiles)
    def _(i):
        at = pl.ds(pl.multiple_of(i * width, width), width)
        total = nn(g_buf[0], val_buf[0:step_cols, at])
        for j in range(1, parts):
            total += nn(g_buf[j], val_buf[j * step_cols : (j + 1) * step_cols, at])
        y_buf[i] = total.astype(BF)
        y_copy(i).start()

    for i in range(parts):
        g_copy(i).wait()
    for i in range(tiles):
        y_copy(i).wait()


def serve(x, fold, values, features):
    rows = x.shape[0]
    value_rows = values.shape[0]
    parts, tiles = 4, 8
    step_cols = value_rows // parts
    any_spec = pl.BlockSpec(memory_space=pl.ANY)
    return pl.pallas_call(
        functools.partial(serve_kernel, float(features) ** (-0.5)),
        out_shape=(
            jax.ShapeDtypeStruct((rows, features), BF),
            jax.ShapeDtypeStruct((rows, value_rows), BF),
        ),
        in_specs=[any_spec] * 3,
        out_specs=(any_spec, any_spec),
        scratch_shapes=[
            pltpu.VMEM(x.shape, BF),
            pltpu.VMEM((parts, features, step_cols), BF),
            pltpu.VMEM(values.shape, BF),
            pltpu.VMEM((rows // 2, features), BF),
            pltpu.VMEM((rows // 2, features), BF),
            pltpu.VMEM((rows // 2, LANES), F32),
            pltpu.VMEM((parts, rows, step_cols), BF),
            pltpu.VMEM((tiles, rows, features // tiles), BF),
            pltpu.SemaphoreType.DMA((parts,)),
            pltpu.SemaphoreType.DMA((parts,)),
            pltpu.SemaphoreType.DMA((parts,)),
            pltpu.SemaphoreType.DMA((tiles,)),
            pltpu.SemaphoreType.DMA((parts,)),
        ],
        compiler_params=params(48),
        cost_estimate=cost(4 * rows * value_rows * features, 20 << 20),
    )(x, fold, values)


def grad_kernel(half, core_ref, own_ref, sib_ref, x_ref, part_ref, g_ref, out_ref, gt_ref):
    step = pl.program_id(0)
    rows = x_ref.shape[0]
    tile = 256

    @pl.when(step == 0)
    def _():
        for i in range(0, rows, tile):
            gt_ref[:, i : i + tile] = g_ref[i : i + tile, :].T

    def use(w_ref):
        features = w_ref.shape[1]
        width = w_ref.shape[2]
        low = lax.broadcasted_iota(jnp.int32, (tile // 8, 8, 1), 1) < SLOTS
        pieces = []
        for i in range(0, rows, tile):
            queries = nn(x_ref[i : i + tile, :features], w_ref[0]).reshape(tile // 8, 8, width)
            sent = part_ref[i : i + tile, :].astype(F32).reshape(tile // 8, 8, width)
            other = jnp.where(low, pltpu.roll(sent, 4, 1), pltpu.roll(queries, 4, 1))
            pieces.append(other.reshape(tile, width).astype(BF))
        other = jnp.concatenate(pieces, axis=0)
        for i in range(0, out_ref.shape[0], tile):
            out_ref[i : i + tile, :] = nn(gt_ref[i : i + tile, :], other).astype(BF)

    with_slice(half, own_ref, sib_ref, use)


def value_grads(core, own, sib, x, g):
    half, features, width = own.shape
    rows, value_rows = g.shape
    return pl.pallas_call(
        functools.partial(grad_kernel, half),
        out_shape=jax.ShapeDtypeStruct((value_rows, features), BF),
        grid_spec=pltpu.PrefetchScalarGridSpec(
            num_scalar_prefetch=1,
            grid=(2 * half,),
            in_specs=slice_specs(half, features, width)
            + [
                whole(x.shape),
                pl.BlockSpec((rows, width), lambda a, core: (0, slice_at(a, core[0], half))),
                whole(g.shape),
            ],
            out_specs=pl.BlockSpec((value_rows, width), lambda a, core: (0, slice_at(a, core[0], half))),
            scratch_shapes=[pltpu.VMEM((value_rows, rows), BF)],
        ),
        compiler_params=params(40),
        cost_estimate=cost(6 * rows * value_rows * features, 24 << 20),
    )(core, own, sib, x, x, g)


def home_kernel(half, core_ref, own_ref, sib_ref, back_ref, tgt_ref, wgt_ref, tok_ref, cot_ref, gain_ref,
                out_ref, grad_ref, query_ref, acc_ref):
    step = pl.program_id(0)
    count, features = tok_ref.shape
    rows = back_ref.shape[0]
    width = query_ref.shape[2]

    @pl.when(step == 0)
    def _():
        number = lax.broadcasted_iota(jnp.int32, (count, rows), 1)
        targets = tgt_ref[...]
        weights = wgt_ref[...]
        t0, t1 = targets[:, :1], targets[:, 1:]
        one = lambda hit: jnp.where(hit, 1.0, 0.0).astype(BF)
        pick = jnp.concatenate(
            [
                one(number == t0),
                one(number == t1),
                one((number == t0 + SLOTS) | (number == t1 + SLOTS)),
            ],
            axis=0,
        )
        for i in range(2 * half):
            at = slice(i * width, (i + 1) * width)
            got = nn(pick, back_ref[:, at])
            out_ref[:, at] = tok_ref[:, at].astype(F32) + (
                weights[:, :1] * got[:count] + weights[:, 1:] * got[count : 2 * count]
            )
            query_ref[i] = got[2 * count :].astype(BF)
        acc_ref[...] = jnp.zeros_like(acc_ref)

    at = slice_at(step, core_ref[0], half)

    def use(w_ref):
        acc_ref[...] += nt(query_ref[at], w_ref[0])

    with_slice(half, own_ref, sib_ref, use)

    @pl.when(step == 2 * half - 1)
    def _():
        exact = tok_ref[...].astype(F32)
        rms = lax.rsqrt(jnp.mean(exact * exact, axis=1, keepdims=True) + 1e-06)
        unit = exact * rms
        unit_grad = acc_ref[...] * gain_ref[...]
        mean = jnp.mean(unit_grad * unit, axis=1, keepdims=True)
        grad_ref[...] = cot_ref[...].astype(F32) + rms * (unit_grad - unit * mean)


def finish(core, own, sib, back, targets, weights, tokens, cot, gain):
    half, features, width = own.shape
    count = tokens.shape[0]
    return pl.pallas_call(
        functools.partial(home_kernel, half),
        out_shape=(
            jax.ShapeDtypeStruct((count, features), F32),
            jax.ShapeDtypeStruct((count, features), F32),
        ),
        grid_spec=pltpu.PrefetchScalarGridSpec(
            num_scalar_prefetch=1,
            grid=(2 * half,),
            in_specs=slice_specs(half, features, width)
            + [
                whole(back.shape),
                whole((count, 2)),
                whole((count, 2)),
                whole(tokens.shape),
                whole(cot.shape),
                whole((1, features)),
            ],
            out_specs=(whole((count, features)), whole((count, features))),
            scratch_shapes=[
                pltpu.VMEM((2 * half, count, width), BF),
                pltpu.VMEM((count, features), F32),
            ],
        ),
        compiler_params=params(40),
        cost_estimate=cost(4 * count * features * features, 14 << 20),
    )(core, own, sib, back, targets, weights, tokens, cot, gain)


def gather_weight(query_weight):
    own = lax.all_gather(query_weight, "x", axis=0, tiled=False)
    sib = lax.ppermute(own, "core", [(0, 1), (1, 0)])
    return own, sib


def exchange(rows):
    return lax.all_to_all(rows, ALL, split_axis=0, concat_axis=0, tiled=True)


def body(tokens, norm_gain, query_weight, values, blocks, weights, out_cotangent):
    features = tokens.shape[1]
    owners = lax.axis_size(ALL)
    core = lax.axis_index("core").astype(jnp.int32).reshape(1)
    gain = norm_gain.reshape(1, features)
    own, sib = gather_weight(query_weight)
    payload, targets = build_payload(
        tokens, gain, blocks, weights, out_cotangent, owners, values.shape[0] // BLOCK
    )
    got = exchange(payload)
    fold = fold_weight(core, own, sib, values)
    answers, mixed = serve(got, fold, values, features)
    back = exchange(answers)
    grad_values = value_grads(core, own, sib, got, mixed)
    layer_out, grad_tokens = finish(
        core, own, sib, back, targets, weights, tokens, out_cotangent, gain
    )
    return layer_out, grad_tokens, grad_values


def solution(mesh):
    fine = Mesh(np.asarray(mesh.devices).reshape(4, 2, 4, 4), ALL)
    rows = P(ALL, None)
    return jax.shard_map(
        body,
        mesh=fine,
        in_specs=(rows, P(), P(None, ("x", "core")), rows, rows, rows, rows),
        out_specs=(rows, rows, rows),
        check_vma=False,
    )
```

```python
import functools

import jax
import jax.numpy as jnp
import numpy as np
from jax import lax
from jax.experimental import pallas as pl
from jax.experimental.pallas import tpu as pltpu
from jax.sharding import Mesh
from jax.sharding import PartitionSpec as P

BLOCK = 64
SLOTS = 4
CHUNK = 2 * SLOTS
LANES = 128
ALL = ("x", "core", "z", "y")
BF = jnp.bfloat16
F32 = jnp.float32
MB = 60


def params(megabytes):
    return pltpu.CompilerParams(vmem_limit_bytes=megabytes << 20)


def cost(flops, bytes_accessed):
    return pl.CostEstimate(
        flops=int(flops), bytes_accessed=int(bytes_accessed), transcendentals=0
    )


def whole(shape):
    return pl.BlockSpec(shape, lambda *_: (0,) * len(shape))


def nt(left, right):
    return lax.dot_general(left, right, (((1,), (1,)), ((), ())), preferred_element_type=F32)


def nn(left, right):
    return jnp.dot(left, right, preferred_element_type=F32)


def send_kernel(span, tok_ref, gain_ref, blk_ref, wgt_ref, cot_ref, x_ref, tgt_ref, rows_ref, route_ref):
    step = pl.program_id(0)
    count, features = tok_ref.shape
    step_rows = x_ref.shape[0]

    @pl.when(step == 0)
    def _():
        exact = tok_ref[...].astype(F32)
        rms = lax.rsqrt(jnp.mean(exact * exact, axis=1, keepdims=True) + 1e-06)
        rows_ref[:count, :] = ((exact * rms) * gain_ref[...]).astype(BF)
        rows_ref[count:, :] = cot_ref[...]
        square = (count, count)
        sub = lax.broadcasted_iota(jnp.int32, square, 0)
        lane = lax.broadcasted_iota(jnp.int32, square, 1)
        blocks = blk_ref[...]
        weights = wgt_ref[...]
        col = [jnp.broadcast_to(blocks[:, k : k + 1], square) for k in range(2)]
        row = [c.astype(F32).T.astype(jnp.int32) for c in col]
        wrow = [jnp.broadcast_to(weights[:, k : k + 1], square).T for k in range(2)]
        own_col = [c // span for c in col]
        own_row = [r // span for r in row]
        one = lambda hit: jnp.where(hit, 1, 0)
        before = [
            [one((own_col[0] == own_row[0]) & (sub < lane))],
            [one(own_col[0] == own_row[1]), one((own_col[1] == own_row[1]) & (sub < lane))],
        ]
        before_t = [
            [one((own_row[0] == own_col[0]) & (lane < sub))],
            [one(own_row[0] == own_col[1]), one((own_row[1] == own_col[1]) & (lane < sub))],
        ]
        for k in range(2):
            slot_row = sum(jnp.sum(e, axis=0, keepdims=True) for e in before[k])
            slot_col = sum(jnp.sum(e, axis=1, keepdims=True) for e in before_t[k])
            target = own_row[k][:1, :] * CHUNK + slot_row
            route_ref[k : k + 1, :] = target.astype(F32)
            route_ref[2 + k : 3 + k, :] = (row[k][:1, :] % span).astype(F32) + 1.0
            route_ref[4 + k : 5 + k, :] = wrow[k][:1, :]
            tgt_ref[:, k : k + 1] = own_col[k][:, :1] * CHUNK + slot_col

    route = route_ref[...]
    shape = (step_rows, count)
    number = (lax.broadcasted_iota(jnp.int32, shape, 0) + step * step_rows).astype(F32)
    t0, t1 = route[0:1, :], route[1:2, :]
    n0, n1 = number == t0, number == t1
    c0, c1 = number == t0 + SLOTS, number == t1 + SLOTS
    scale = jnp.sum(jnp.where(c0, route[4:5, :], 0.0) + jnp.where(c1, route[5:6, :], 0.0), axis=1, keepdims=True)
    ident = jnp.sum(
        jnp.where(n0 | c0, route[2:3, :], 0.0) + jnp.where(n1 | c1, route[3:4, :], 0.0),
        axis=1,
        keepdims=True,
    )
    is_cot = (lax.broadcasted_iota(jnp.int32, (step_rows, 1), 0) % CHUNK) >= SLOTS
    scale = jnp.where(is_cot, scale, 1.0)
    pick = jnp.concatenate(
        [jnp.where(n0 | n1, 1.0, 0.0), jnp.where(c0 | c1, 1.0, 0.0)], axis=1
    ).astype(BF)
    width = 512
    for at in range(0, features, width):
        rows = nn(pick, rows_ref[:, at : at + width])
        x_ref[:, at : at + width] = (rows * scale).astype(BF)
    x_ref[:, features:] = jnp.broadcast_to(ident - 1.0, (step_rows, LANES)).astype(BF)


def build_payload(tokens, gain, blocks, weights, cot, owners, span):
    count, features = tokens.shape
    rows = owners * CHUNK
    steps = 4
    return pl.pallas_call(
        functools.partial(send_kernel, span),
        out_shape=(
            jax.ShapeDtypeStruct((rows, features + LANES), BF),
            jax.ShapeDtypeStruct((count, 2), jnp.int32),
        ),
        grid=(steps,),
        in_specs=[
            whole((count, features)),
            whole((1, features)),
            whole((count, 2)),
            whole((count, 2)),
            whole((count, features)),
        ],
        out_specs=(
            pl.BlockSpec((rows // steps, features + LANES), lambda i: (i, 0)),
            whole((count, 2)),
        ),
        scratch_shapes=[pltpu.VMEM((2 * count, features), BF), pltpu.VMEM((8, count), F32)],
        compiler_params=params(MB),
        cost_estimate=cost(2 * rows * 2 * count * features, 6 << 20),
    )(tokens, gain, blocks, weights, cot)


def ring(axis, size, by):
    return lambda rows: lax.ppermute(rows, axis, [(i, (i + by) % size) for i in range(size)])


def both_ways(axis, size, piece):
    up, down = ring(axis, size, 1), ring(axis, size, -1)
    half = piece.shape[0] // 2
    before, after = up(piece), down(piece)
    return before, after, up(before[:half]), down(after[half:])


def assemble_kernel(at_ref, w_ref, *refs):
    pieces, out_ref, sems = refs[:-2], refs[-2], refs[-1]
    x, z, y = at_ref[0], at_ref[1], at_ref[2]
    width = w_ref.shape[1]
    half_rows = w_ref.shape[0] // 2
    columns = [lax.rem(x + d, 4) for d in (3, 1, 2)]
    copies = []

    def add(src, row, column, rows):
        copies.append(
            pltpu.make_async_copy(
                src,
                out_ref.at[
                    pl.ds(pl.multiple_of(row, 128), rows),
                    pl.ds(pl.multiple_of(column * width, width), width),
                ],
                sems.at[len(copies)],
            )
        )

    add(w_ref, 0, x, w_ref.shape[0])
    for part, me in ((0, y), (1, z)):
        mine, before, after, top, bottom = pieces[5 * part : 5 * part + 5]
        rows = mine.shape[0]
        base = part * half_rows
        across = lax.rem(me + 2, 4) * rows
        places = [
            (mine, me * rows),
            (before, lax.rem(me + 3, 4) * rows),
            (after, lax.rem(me + 1, 4) * rows),
            (top, across),
            (bottom, across + rows // 2),
        ]
        for piece, row in places:
            for k, column in enumerate(columns):
                add(
                    piece.at[:, k * width : (k + 1) * width],
                    base + row,
                    column,
                    piece.shape[0],
                )
    for copy in copies:
        copy.start()
    for copy in copies:
        copy.wait()


def gather_own(weight, after_this):
    features, width = weight.shape
    half, rows = features // 2, features // 8
    x, z, y = (lax.axis_index(n).astype(jnp.int32) for n in ("x", "z", "y"))
    mine = jnp.concatenate(
        [
            lax.dynamic_slice(weight, (y * rows, 0), (rows, width)),
            lax.dynamic_slice(weight, (half + z * rows, 0), (rows, width)),
        ],
        axis=0,
    )
    up, down = ring("x", 4, 1), ring("x", 4, -1)
    before, after = up(mine), down(mine)
    before, after, after_this = lax.optimization_barrier((before, after, after_this))
    across_y, across_z = up(before[:rows]), down(after[rows:])
    set_y = jnp.concatenate([before[:rows], after[:rows], across_y], axis=1)
    set_z = jnp.concatenate([before[rows:], after[rows:], across_z], axis=1)
    pieces = (set_y, *both_ways("y", 4, set_y), set_z, *both_ways("z", 4, set_z))
    any_spec = pl.BlockSpec(memory_space=pl.ANY)
    return pl.pallas_call(
        assemble_kernel,
        out_shape=jax.ShapeDtypeStruct((features, 4 * width), BF),
        in_specs=[pl.BlockSpec(memory_space=pltpu.SMEM)] + [any_spec] * 11,
        out_specs=any_spec,
        scratch_shapes=[pltpu.SemaphoreType.DMA((31,))],
        compiler_params=params(MB),
        cost_estimate=cost(1, 1),
    )(jnp.stack([x, z, y]), weight, *pieces)


def slice_at(step, core, half):
    return jnp.where(step < half, 2 * step + core, 2 * (step - half) + 1 - core)


def slice_specs(half, features, width):
    return [
        pl.BlockSpec((features, width), lambda a, core: (0, jnp.minimum(a, half - 1))),
        pl.BlockSpec((features, width), lambda a, core: (0, jnp.maximum(a - half, 0))),
    ]


def with_slice(half, own_ref, sib_ref, use):
    step = pl.program_id(0)

    @pl.when(step < half)
    def _():
        use(own_ref)

    @pl.when(step >= half)
    def _():
        use(sib_ref)


def fold_kernel(core_ref, own_ref, sib_ref, val_ref, out_ref, vt_own, vt_sib):
    width = own_ref.shape[1] // 4
    tile = 256

    @pl.when(pl.program_id(0) == 0)
    def _():
        core = core_ref[0]
        for x in range(4):
            to = slice(x * width, (x + 1) * width)
            for vt, c in ((vt_own, core), (vt_sib, 1 - core)):
                at = pl.ds(pl.multiple_of((2 * x + c) * width, width), width)
                vt[to, :] = val_ref[:, at].T

    for i in range(0, out_ref.shape[1], tile):
        at = slice(i, i + tile)
        total = nn(own_ref[...], vt_own[:, at]) + nn(sib_ref[...], vt_sib[:, at])
        out_ref[:, at] = total.astype(BF)


def fold_weight(core, own, sib, values):
    value_rows, features = values.shape
    steps = 4
    rows, half = features // steps, features // 2
    block = pl.BlockSpec((rows, half), lambda i, core: (i, 0))
    return pl.pallas_call(
        fold_kernel,
        out_shape=jax.ShapeDtypeStruct((features, value_rows), BF),
        grid_spec=pltpu.PrefetchScalarGridSpec(
            num_scalar_prefetch=1,
            grid=(steps,),
            in_specs=[block, block, whole(values.shape)],
            out_specs=pl.BlockSpec((rows, value_rows), lambda i, core: (i, 0)),
            scratch_shapes=[pltpu.VMEM((half, value_rows), BF), pltpu.VMEM((half, value_rows), BF)],
        ),
        compiler_params=params(MB),
        cost_estimate=cost(1, 1),
    )(core.reshape(1), own, sib, values)


def serve_kernel(scale, x_hbm, fold_hbm, val_hbm, y_hbm, n_hbm, c_hbm, g_hbm, s_hbm,
                 x_buf, fold_buf, val_buf, n_buf, c_buf, id_buf, g_buf, s_buf, y_buf,
                 x_sem, f_sem, v_sem, y_sem, o_sem):
    rows = x_buf.shape[0]
    features = n_buf.shape[1]
    value_rows = val_buf.shape[0]
    parts = x_sem.shape[0]
    step_rows = rows // parts
    step_cols = value_rows // parts
    slots = rows // 2

    def x_copy(i):
        at = pl.ds(i * step_rows, step_rows)
        return pltpu.make_async_copy(x_hbm.at[at, :], x_buf.at[at, :], x_sem.at[i])

    def f_copy(i):
        return pltpu.make_async_copy(
            fold_hbm.at[:, pl.ds(i * step_cols, step_cols)], fold_buf.at[i], f_sem.at[i]
        )

    def v_copy(i):
        at = pl.ds(i * step_cols, step_cols)
        return pltpu.make_async_copy(val_hbm.at[at, :], val_buf.at[at, :], v_sem.at[i])

    for i in range(parts):
        x_copy(i).start()
    for i in range(parts):
        f_copy(i).start()
        v_copy(i).start()

    take = 32
    low = lax.broadcasted_iota(jnp.int32, (take // 16, 8, 1), 1) < SLOTS

    def split(x):
        pairs = x.astype(F32).reshape(take // 16, 16, x.shape[1])
        first, second = pairs[:, :8], pairs[:, 8:]
        upper = jnp.where(low, first, pltpu.roll(second, 4, 1))
        lower = jnp.where(low, pltpu.roll(first, 4, 1), second)
        return upper.reshape(take // 2, x.shape[1]), lower.reshape(take // 2, x.shape[1])

    for i in range(parts):
        x_copy(i).wait()

        @pl.loop(i * step_rows // take, (i + 1) * step_rows // take)
        def _(r):
            src = pl.ds(pl.multiple_of(r * take, take), take)
            dst = pl.ds(pl.multiple_of(r * (take // 2), take // 2), take // 2)
            upper, lower = split(x_buf[src, :features])
            n_buf[dst, :] = upper.astype(BF)
            c_buf[dst, :] = lower.astype(BF)
            ident, _ = split(x_buf[src, features:])
            id_buf[dst, :] = ident

    kept = [pltpu.make_async_copy(n_buf, n_hbm, o_sem.at[0]), pltpu.make_async_copy(c_buf, c_hbm, o_sem.at[1])]
    for copy in kept:
        copy.start()

    for j in range(parts):
        f_copy(j).wait()
        v_copy(j).wait()
        scores = nn(n_buf[...], fold_buf[j]) * scale
        cot_scores = nt(c_buf[...], val_buf[j * step_cols : (j + 1) * step_cols, :])
        sig = 1.0 / (1.0 + jnp.exp(-scores))
        block_of = (lax.broadcasted_iota(jnp.int32, (1, step_cols), 1) // BLOCK + j * (step_cols // BLOCK)).astype(F32)
        mine = id_buf[:, :1] == block_of
        g_buf[j] = jnp.where(mine, sig, 0.0).astype(BF)
        s_buf[j] = jnp.where(mine, cot_scores * sig * (1.0 - sig) * scale, 0.0).astype(BF)
        at = pl.ds(j * step_cols, step_cols)
        kept.append(pltpu.make_async_copy(g_buf.at[j], g_hbm.at[:, at], o_sem.at[2 + j]))
        kept.append(pltpu.make_async_copy(s_buf.at[j], s_hbm.at[:, at], o_sem.at[2 + parts + j]))
        kept[-2].start()
        kept[-1].start()

    tiles = y_sem.shape[0]
    width = features // tiles
    lows = lax.broadcasted_iota(jnp.int32, (slots // 8, 8, 1), 1) < SLOTS

    def y_copy(i):
        at = pl.ds(pl.multiple_of(i * width, width), width)
        return pltpu.make_async_copy(y_buf.at[i], y_hbm.at[:, at], y_sem.at[i])

    @pl.loop(0, tiles)
    def _(i):
        at = pl.ds(pl.multiple_of(i * width, width), width)
        read = nn(g_buf[0], val_buf[0:step_cols, at])
        grad = nt(s_buf[0], fold_buf[0, at, :])
        for j in range(1, parts):
            read += nn(g_buf[j], val_buf[j * step_cols : (j + 1) * step_cols, at])
            grad += nt(s_buf[j], fold_buf[j, at, :])
        read = read.reshape(slots // 8, 8, width)
        grad = grad.reshape(slots // 8, 8, width)
        first = jnp.where(lows, read, pltpu.roll(grad, 4, 1))
        second = jnp.where(lows, pltpu.roll(read, 4, 1), grad)
        y_buf[i] = jnp.concatenate([first, second], axis=1).reshape(rows, width).astype(BF)
        y_copy(i).start()

    for copy in kept:
        copy.wait()
    for i in range(tiles):
        y_copy(i).wait()


def serve(x, fold, values, features):
    rows = x.shape[0]
    slots = rows // 2
    value_rows = values.shape[0]
    parts, tiles = 4, 8
    step_cols = value_rows // parts
    any_spec = pl.BlockSpec(memory_space=pl.ANY)
    return pl.pallas_call(
        functools.partial(serve_kernel, float(features) ** (-0.5)),
        out_shape=(
            jax.ShapeDtypeStruct((rows, features), BF),
            jax.ShapeDtypeStruct((slots, features), BF),
            jax.ShapeDtypeStruct((slots, features), BF),
            jax.ShapeDtypeStruct((slots, value_rows), BF),
            jax.ShapeDtypeStruct((slots, value_rows), BF),
        ),
        in_specs=[any_spec] * 3,
        out_specs=(any_spec,) * 5,
        scratch_shapes=[
            pltpu.VMEM(x.shape, BF),
            pltpu.VMEM((parts, features, step_cols), BF),
            pltpu.VMEM(values.shape, BF),
            pltpu.VMEM((slots, features), BF),
            pltpu.VMEM((slots, features), BF),
            pltpu.VMEM((slots, LANES), F32),
            pltpu.VMEM((parts, slots, step_cols), BF),
            pltpu.VMEM((parts, slots, step_cols), BF),
            pltpu.VMEM((tiles, rows, features // tiles), BF),
            pltpu.SemaphoreType.DMA((parts,)),
            pltpu.SemaphoreType.DMA((parts,)),
            pltpu.SemaphoreType.DMA((parts,)),
            pltpu.SemaphoreType.DMA((tiles,)),
            pltpu.SemaphoreType.DMA((2 + 2 * parts,)),
        ],
        compiler_params=params(MB),
        cost_estimate=cost(4 * rows * value_rows * features, 20 << 20),
    )(x, fold, values)


def grad_kernel(half, core_ref, own_ref, sib_ref, n_ref, c_ref, g_ref, s_ref, out_ref, gt_ref, st_ref):
    slots = n_ref.shape[0]
    tile = 256

    @pl.when(pl.program_id(0) == 0)
    def _():
        for i in range(0, slots, tile):
            gt_ref[:, i : i + tile] = g_ref[i : i + tile, :].T
            st_ref[:, i : i + tile] = s_ref[i : i + tile, :].T

    def use(w_ref):
        queries = nn(n_ref[...], w_ref[...]).astype(BF)
        for i in range(0, out_ref.shape[0], tile):
            total = nn(gt_ref[i : i + tile, :], c_ref[...]) + nn(st_ref[i : i + tile, :], queries)
            out_ref[i : i + tile, :] = total.astype(BF)

    with_slice(half, own_ref, sib_ref, use)


def value_grads(core, own, sib, n, c, g, s):
    half = 4
    features, width = own.shape[0], own.shape[1] // half
    slots, value_rows = g.shape
    return pl.pallas_call(
        functools.partial(grad_kernel, half),
        out_shape=jax.ShapeDtypeStruct((value_rows, features), BF),
        grid_spec=pltpu.PrefetchScalarGridSpec(
            num_scalar_prefetch=1,
            grid=(2 * half,),
            in_specs=slice_specs(half, features, width)
            + [
                whole(n.shape),
                pl.BlockSpec((slots, width), lambda a, core: (0, slice_at(a, core[0], half))),
                whole(g.shape),
                whole(s.shape),
            ],
            out_specs=pl.BlockSpec((value_rows, width), lambda a, core: (0, slice_at(a, core[0], half))),
            scratch_shapes=[pltpu.VMEM((value_rows, slots), BF), pltpu.VMEM((value_rows, slots), BF)],
        ),
        compiler_params=params(MB),
        cost_estimate=cost(6 * slots * value_rows * features, 24 << 20),
    )(core, own, sib, n, c, g, s)


def home_kernel(back_ref, tgt_ref, wgt_ref, tok_ref, cot_ref, gain_ref, out_ref, grad_ref, pick_ref, acc_ref, rms_ref, sum_ref):
    step = pl.program_id(0)
    count, features = tok_ref.shape
    rows, width = back_ref.shape

    @pl.when(step == 0)
    def _():
        number = lax.broadcasted_iota(jnp.int32, (count, rows), 1)
        targets = tgt_ref[...]
        t0, t1 = targets[:, :1], targets[:, 1:]
        one = lambda hit: jnp.where(hit, 1.0, 0.0).astype(BF)
        pick_ref[:count, :] = one(number == t0)
        pick_ref[count : 2 * count, :] = one(number == t1)
        pick_ref[2 * count :, :] = one((number == t0 + SLOTS) | (number == t1 + SLOTS))
        exact = tok_ref[...].astype(F32)
        rms_ref[...] = lax.rsqrt(jnp.mean(exact * exact, axis=1, keepdims=True) + 1e-06)
        sum_ref[...] = jnp.zeros_like(sum_ref)

    at = pl.ds(pl.multiple_of(step * width, width), width)
    weights = wgt_ref[...]
    got = nn(pick_ref[...], back_ref[...])
    exact = tok_ref[:, at].astype(F32)
    out_ref[...] = exact + (weights[:, :1] * got[:count] + weights[:, 1:] * got[count : 2 * count])
    unit_grad = got[2 * count :] * gain_ref[:, at]
    acc_ref[:, at] = unit_grad
    rms = rms_ref[...]
    sum_ref[...] += jnp.sum(unit_grad * (exact * rms), axis=1, keepdims=True)

    @pl.when(step == pl.num_programs(0) - 1)
    def _():
        mean = sum_ref[...] * (1.0 / features)
        for i in range(0, features, width):
            cols = slice(i, i + width)
            unit = tok_ref[:, cols].astype(F32) * rms
            grad_ref[:, cols] = cot_ref[:, cols].astype(F32) + rms * (acc_ref[:, cols] - unit * mean)


def finish(back, targets, weights, tokens, cot, gain):
    count, features = tokens.shape
    rows = back.shape[0]
    steps = 4
    width = features // steps
    return pl.pallas_call(
        home_kernel,
        out_shape=(
            jax.ShapeDtypeStruct((count, features), F32),
            jax.ShapeDtypeStruct((count, features), F32),
        ),
        grid=(steps,),
        in_specs=[
            pl.BlockSpec((rows, width), lambda i: (0, i)),
            whole((count, 2)),
            whole((count, 2)),
            whole(tokens.shape),
            whole(cot.shape),
            whole((1, features)),
        ],
        out_specs=(pl.BlockSpec((count, width), lambda i: (0, i)), whole((count, features))),
        scratch_shapes=[
            pltpu.VMEM((3 * count, rows), BF),
            pltpu.VMEM((count, features), F32),
            pltpu.VMEM((count, 1), F32),
            pltpu.VMEM((count, 1), F32),
        ],
        compiler_params=params(MB),
        cost_estimate=cost(6 * count * rows * features, 10 << 20),
    )(back, targets, weights, tokens, cot, gain)


def exchange(rows):
    return lax.all_to_all(rows, ALL, split_axis=0, concat_axis=0, tiled=True)


def body(tokens, norm_gain, query_weight, values, blocks, weights, out_cotangent):
    features = tokens.shape[1]
    owners = lax.axis_size(ALL)
    core = lax.axis_index("core").astype(jnp.int32)
    gain = norm_gain.reshape(1, features)
    payload, targets = build_payload(
        tokens, gain, blocks, weights, out_cotangent, owners, values.shape[0] // BLOCK
    )
    got = exchange(payload)
    own = gather_own(query_weight, targets)
    sib = lax.ppermute(own, "core", [(0, 1), (1, 0)])
    fold = fold_weight(core, own, sib, values)
    answers, n, c, g, s = serve(got, fold, values, features)
    back = exchange(answers)
    grad_values = value_grads(core.reshape(1), own, sib, n, c, g, s)
    layer_out, grad_tokens = finish(back, targets, weights, tokens, out_cotangent, gain)
    return layer_out, grad_tokens, grad_values


def solution(mesh):
    fine = Mesh(np.asarray(mesh.devices).reshape(4, 2, 4, 4), ALL)
    rows = P(ALL, None)
    return jax.shard_map(
        body,
        mesh=fine,
        in_specs=(rows, P(), P(None, ("x", "core")), rows, rows, rows, rows),
        out_specs=(rows, rows, rows),
        check_vma=False,
    )
```

```python
import functools

import jax
import jax.numpy as jnp
import numpy as np
from jax import lax
from jax.experimental import pallas as pl
from jax.experimental.pallas import tpu as pltpu
from jax.sharding import Mesh
from jax.sharding import PartitionSpec as P

BLOCK = 64
SLOTS = 4
CHUNK = 2 * SLOTS
LANES = 128
ALL = ("x", "core", "z", "y")
BF = jnp.bfloat16
F32 = jnp.float32
MB = 60


def params(megabytes):
    return pltpu.CompilerParams(vmem_limit_bytes=megabytes << 20)


def cost(flops, bytes_accessed):
    return pl.CostEstimate(
        flops=int(flops), bytes_accessed=int(bytes_accessed), transcendentals=0
    )


def whole(shape):
    return pl.BlockSpec(shape, lambda *_: (0,) * len(shape))


def nt(left, right):
    return lax.dot_general(left, right, (((1,), (1,)), ((), ())), preferred_element_type=F32)


def nn(left, right):
    return jnp.dot(left, right, preferred_element_type=F32)


def send_kernel(span, tok_ref, gain_ref, blk_ref, wgt_ref, cot_ref, x_ref, tgt_ref, rows_ref, route_ref):
    step = pl.program_id(0)
    count, features = tok_ref.shape
    step_rows = x_ref.shape[0]

    @pl.when(step == 0)
    def _():
        exact = tok_ref[...].astype(F32)
        rms = lax.rsqrt(jnp.mean(exact * exact, axis=1, keepdims=True) + 1e-06)
        rows_ref[:count, :] = ((exact * rms) * gain_ref[...]).astype(BF)
        rows_ref[count:, :] = cot_ref[...]
        square = (count, count)
        sub = lax.broadcasted_iota(jnp.int32, square, 0)
        lane = lax.broadcasted_iota(jnp.int32, square, 1)
        blocks = blk_ref[...]
        weights = wgt_ref[...]
        col = [jnp.broadcast_to(blocks[:, k : k + 1], square) for k in range(2)]
        row = [c.astype(F32).T.astype(jnp.int32) for c in col]
        wrow = [jnp.broadcast_to(weights[:, k : k + 1], square).T for k in range(2)]
        own_col = [c // span for c in col]
        own_row = [r // span for r in row]
        one = lambda hit: jnp.where(hit, 1, 0)
        before = [
            [one((own_col[0] == own_row[0]) & (sub < lane))],
            [one(own_col[0] == own_row[1]), one((own_col[1] == own_row[1]) & (sub < lane))],
        ]
        before_t = [
            [one((own_row[0] == own_col[0]) & (lane < sub))],
            [one(own_row[0] == own_col[1]), one((own_row[1] == own_col[1]) & (lane < sub))],
        ]
        for k in range(2):
            slot_row = sum(jnp.sum(e, axis=0, keepdims=True) for e in before[k])
            slot_col = sum(jnp.sum(e, axis=1, keepdims=True) for e in before_t[k])
            target = own_row[k][:1, :] * CHUNK + slot_row
            route_ref[k : k + 1, :] = target.astype(F32)
            route_ref[2 + k : 3 + k, :] = (row[k][:1, :] % span).astype(F32) + 1.0
            route_ref[4 + k : 5 + k, :] = wrow[k][:1, :]
            tgt_ref[:, k : k + 1] = own_col[k][:, :1] * CHUNK + slot_col

    route = route_ref[...]
    shape = (step_rows, count)
    number = (lax.broadcasted_iota(jnp.int32, shape, 0) + step * step_rows).astype(F32)
    t0, t1 = route[0:1, :], route[1:2, :]
    n0, n1 = number == t0, number == t1
    c0, c1 = number == t0 + SLOTS, number == t1 + SLOTS
    scale = jnp.sum(jnp.where(c0, route[4:5, :], 0.0) + jnp.where(c1, route[5:6, :], 0.0), axis=1, keepdims=True)
    ident = jnp.sum(
        jnp.where(n0 | c0, route[2:3, :], 0.0) + jnp.where(n1 | c1, route[3:4, :], 0.0),
        axis=1,
        keepdims=True,
    )
    is_cot = (lax.broadcasted_iota(jnp.int32, (step_rows, 1), 0) % CHUNK) >= SLOTS
    scale = jnp.where(is_cot, scale, 1.0)
    pick = jnp.concatenate(
        [jnp.where(n0 | n1, 1.0, 0.0), jnp.where(c0 | c1, 1.0, 0.0)], axis=1
    ).astype(BF)
    width = 512
    for at in range(0, features, width):
        rows = nn(pick, rows_ref[:, at : at + width])
        x_ref[:, at : at + width] = (rows * scale).astype(BF)
    x_ref[:, features:] = jnp.broadcast_to(ident - 1.0, (step_rows, LANES)).astype(BF)


def build_payload(tokens, gain, blocks, weights, cot, owners, span):
    count, features = tokens.shape
    rows = owners * CHUNK
    steps = 4
    return pl.pallas_call(
        functools.partial(send_kernel, span),
        out_shape=(
            jax.ShapeDtypeStruct((rows, features + LANES), BF),
            jax.ShapeDtypeStruct((count, 2), jnp.int32),
        ),
        grid=(steps,),
        in_specs=[
            whole((count, features)),
            whole((1, features)),
            whole((count, 2)),
            whole((count, 2)),
            whole((count, features)),
        ],
        out_specs=(
            pl.BlockSpec((rows // steps, features + LANES), lambda i: (i, 0)),
            whole((count, 2)),
        ),
        scratch_shapes=[pltpu.VMEM((2 * count, features), BF), pltpu.VMEM((8, count), F32)],
        compiler_params=params(MB),
        cost_estimate=cost(2 * rows * 2 * count * features, 6 << 20),
    )(tokens, gain, blocks, weights, cot)


def shifted(rows, by):
    return lax.ppermute(rows, "x", [(i, (i + by) % 4) for i in range(4)])


def gather_weight(weight):
    own = jnp.stack([weight, shifted(weight, 1), shifted(weight, 3), shifted(weight, 2)])
    return own, lax.ppermute(own, "core", [(0, 1), (1, 0)])


def slice_at(step, at):
    turn = jnp.where(step % 4 == 0, 0, jnp.where(step % 4 == 1, 3, step % 4 - 1))
    return 2 * ((at[0] + turn) % 4) + jnp.where(step < 4, at[1], 1 - at[1])


def fold_kernel(at_ref, own_ref, sib_ref, val_ref, out_ref, vt_ref, left_ref):
    half, _, width = own_ref.shape
    tile = 256

    @pl.when(pl.program_id(0) == 0)
    def _():
        for a in range(2 * half):
            turn = (0, 3, 1, 2)[a % half]
            parity = at_ref[1] if a < half else 1 - at_ref[1]
            column = 2 * lax.rem(at_ref[0] + turn, 4) + parity
            at = pl.ds(pl.multiple_of(column * width, width), width)
            vt_ref[a * width : (a + 1) * width, :] = val_ref[:, at].T

    for a in range(half):
        left_ref[:, a * width : (a + 1) * width] = own_ref[a]
        left_ref[:, (half + a) * width : (half + a + 1) * width] = sib_ref[a]
    for i in range(0, out_ref.shape[1], tile):
        at = slice(i, i + tile)
        out_ref[:, at] = nn(left_ref[...], vt_ref[:, at]).astype(BF)


def fold_weight(at, own, sib, values):
    value_rows, features = values.shape
    half, _, width = own.shape
    steps = 4
    rows = features // steps
    block = pl.BlockSpec((half, rows, width), lambda i, at: (0, i, 0))
    return pl.pallas_call(
        fold_kernel,
        out_shape=jax.ShapeDtypeStruct((features, value_rows), BF),
        grid_spec=pltpu.PrefetchScalarGridSpec(
            num_scalar_prefetch=1,
            grid=(steps,),
            in_specs=[block, block, whole(values.shape)],
            out_specs=pl.BlockSpec((rows, value_rows), lambda i, at: (i, 0)),
            scratch_shapes=[pltpu.VMEM((features, value_rows), BF), pltpu.VMEM((rows, features), BF)],
        ),
        compiler_params=params(MB),
        cost_estimate=cost(1, 1),
    )(at, own, sib, values)


def serve_kernel(scale, x_hbm, fold_hbm, val_hbm, y_hbm, n_hbm, c_hbm, g_hbm, s_hbm,
                 x_buf, fold_buf, val_buf, n_buf, c_buf, id_buf, g_buf, s_buf, y_buf,
                 x_sem, f_sem, v_sem, y_sem, o_sem):
    rows = x_buf.shape[0]
    features = n_buf.shape[1]
    value_rows = val_buf.shape[0]
    parts = x_sem.shape[0]
    step_rows = rows // parts
    step_cols = value_rows // parts
    slots = rows // 2

    def x_copy(i):
        at = pl.ds(i * step_rows, step_rows)
        return pltpu.make_async_copy(x_hbm.at[at, :], x_buf.at[at, :], x_sem.at[i])

    def f_copy(i):
        return pltpu.make_async_copy(
            fold_hbm.at[:, pl.ds(i * step_cols, step_cols)], fold_buf.at[i], f_sem.at[i]
        )

    def v_copy(i):
        at = pl.ds(i * step_cols, step_cols)
        return pltpu.make_async_copy(val_hbm.at[at, :], val_buf.at[at, :], v_sem.at[i])

    for i in range(parts):
        x_copy(i).start()
    for i in range(parts):
        f_copy(i).start()
        v_copy(i).start()

    take = 32
    low = lax.broadcasted_iota(jnp.int32, (take // 16, 8, 1), 1) < SLOTS

    def split(x):
        pairs = x.astype(F32).reshape(take // 16, 16, x.shape[1])
        first, second = pairs[:, :8], pairs[:, 8:]
        upper = jnp.where(low, first, pltpu.roll(second, 4, 1))
        lower = jnp.where(low, pltpu.roll(first, 4, 1), second)
        return upper.reshape(take // 2, x.shape[1]), lower.reshape(take // 2, x.shape[1])

    for i in range(parts):
        x_copy(i).wait()

        @pl.loop(i * step_rows // take, (i + 1) * step_rows // take)
        def _(r):
            src = pl.ds(pl.multiple_of(r * take, take), take)
            dst = pl.ds(pl.multiple_of(r * (take // 2), take // 2), take // 2)
            upper, lower = split(x_buf[src, :features])
            n_buf[dst, :] = upper.astype(BF)
            c_buf[dst, :] = lower.astype(BF)
            ident, _ = split(x_buf[src, features:])
            id_buf[dst, :] = ident

    kept = [pltpu.make_async_copy(n_buf, n_hbm, o_sem.at[0]), pltpu.make_async_copy(c_buf, c_hbm, o_sem.at[1])]
    for copy in kept:
        copy.start()

    for j in range(parts):
        f_copy(j).wait()
        v_copy(j).wait()
        scores = nn(n_buf[...], fold_buf[j]) * scale
        cot_scores = nt(c_buf[...], val_buf[j * step_cols : (j + 1) * step_cols, :])
        sig = 1.0 / (1.0 + jnp.exp(-scores))
        block_of = (lax.broadcasted_iota(jnp.int32, (1, step_cols), 1) // BLOCK + j * (step_cols // BLOCK)).astype(F32)
        mine = id_buf[:, :1] == block_of
        g_buf[j] = jnp.where(mine, sig, 0.0).astype(BF)
        s_buf[j] = jnp.where(mine, cot_scores * sig * (1.0 - sig) * scale, 0.0).astype(BF)
        at = pl.ds(j * step_cols, step_cols)
        kept.append(pltpu.make_async_copy(g_buf.at[j], g_hbm.at[:, at], o_sem.at[2 + j]))
        kept.append(pltpu.make_async_copy(s_buf.at[j], s_hbm.at[:, at], o_sem.at[2 + parts + j]))
        kept[-2].start()
        kept[-1].start()

    tiles = y_sem.shape[0]
    width = features // tiles
    lows = lax.broadcasted_iota(jnp.int32, (slots // 8, 8, 1), 1) < SLOTS

    def y_copy(i):
        at = pl.ds(pl.multiple_of(i * width, width), width)
        return pltpu.make_async_copy(y_buf.at[i], y_hbm.at[:, at], y_sem.at[i])

    @pl.loop(0, tiles)
    def _(i):
        at = pl.ds(pl.multiple_of(i * width, width), width)
        read = nn(g_buf[0], val_buf[0:step_cols, at])
        grad = nt(s_buf[0], fold_buf[0, at, :])
        for j in range(1, parts):
            read += nn(g_buf[j], val_buf[j * step_cols : (j + 1) * step_cols, at])
            grad += nt(s_buf[j], fold_buf[j, at, :])
        read = read.reshape(slots // 8, 8, width)
        grad = grad.reshape(slots // 8, 8, width)
        first = jnp.where(lows, read, pltpu.roll(grad, 4, 1))
        second = jnp.where(lows, pltpu.roll(read, 4, 1), grad)
        y_buf[i] = jnp.concatenate([first, second], axis=1).reshape(rows, width).astype(BF)
        y_copy(i).start()

    for copy in kept:
        copy.wait()
    for i in range(tiles):
        y_copy(i).wait()


def serve(x, fold, values, features):
    rows = x.shape[0]
    slots = rows // 2
    value_rows = values.shape[0]
    parts, tiles = 4, 8
    step_cols = value_rows // parts
    any_spec = pl.BlockSpec(memory_space=pl.ANY)
    return pl.pallas_call(
        functools.partial(serve_kernel, float(features) ** (-0.5)),
        out_shape=(
            jax.ShapeDtypeStruct((rows, features), BF),
            jax.ShapeDtypeStruct((slots, features), BF),
            jax.ShapeDtypeStruct((slots, features), BF),
            jax.ShapeDtypeStruct((slots, value_rows), BF),
            jax.ShapeDtypeStruct((slots, value_rows), BF),
        ),
        in_specs=[any_spec] * 3,
        out_specs=(any_spec,) * 5,
        scratch_shapes=[
            pltpu.VMEM(x.shape, BF),
            pltpu.VMEM((parts, features, step_cols), BF),
            pltpu.VMEM(values.shape, BF),
            pltpu.VMEM((slots, features), BF),
            pltpu.VMEM((slots, features), BF),
            pltpu.VMEM((slots, LANES), F32),
            pltpu.VMEM((parts, slots, step_cols), BF),
            pltpu.VMEM((parts, slots, step_cols), BF),
            pltpu.VMEM((tiles, rows, features // tiles), BF),
            pltpu.SemaphoreType.DMA((parts,)),
            pltpu.SemaphoreType.DMA((parts,)),
            pltpu.SemaphoreType.DMA((parts,)),
            pltpu.SemaphoreType.DMA((tiles,)),
            pltpu.SemaphoreType.DMA((2 + 2 * parts,)),
        ],
        compiler_params=params(MB),
        cost_estimate=cost(4 * rows * value_rows * features, 20 << 20),
    )(x, fold, values)


def grad_kernel(at_ref, own_ref, sib_ref, n_ref, c_ref, g_ref, s_ref, out_ref, gt_ref, st_ref):
    slots = n_ref.shape[0]
    tile = 256

    @pl.when(pl.program_id(0) == 0)
    def _():
        for i in range(0, slots, tile):
            gt_ref[:, i : i + tile] = g_ref[i : i + tile, :].T
            st_ref[:, i : i + tile] = s_ref[i : i + tile, :].T

    weight = jnp.where(pl.program_id(0) < 4, own_ref[0], sib_ref[0])
    queries = nn(n_ref[...], weight).astype(BF)
    for i in range(0, out_ref.shape[0], tile):
        total = nn(gt_ref[i : i + tile, :], c_ref[...]) + nn(st_ref[i : i + tile, :], queries)
        out_ref[i : i + tile, :] = total.astype(BF)


def value_grads(at, own, sib, n, c, g, s):
    half, features, width = own.shape
    slots, value_rows = g.shape
    return pl.pallas_call(
        grad_kernel,
        out_shape=jax.ShapeDtypeStruct((value_rows, features), BF),
        grid_spec=pltpu.PrefetchScalarGridSpec(
            num_scalar_prefetch=1,
            grid=(2 * half,),
            in_specs=[
                pl.BlockSpec((1, features, width), lambda a, x: (jnp.minimum(a, half - 1), 0, 0)),
                pl.BlockSpec((1, features, width), lambda a, x: (jnp.maximum(a - half, 0), 0, 0)),
                whole(n.shape),
                pl.BlockSpec((slots, width), lambda a, x: (0, slice_at(a, x))),
                whole(g.shape),
                whole(s.shape),
            ],
            out_specs=pl.BlockSpec((value_rows, width), lambda a, x: (0, slice_at(a, x))),
            scratch_shapes=[pltpu.VMEM((value_rows, slots), BF), pltpu.VMEM((value_rows, slots), BF)],
        ),
        compiler_params=params(MB),
        cost_estimate=cost(6 * slots * value_rows * features, 24 << 20),
    )(at, own, sib, n, c, g, s)


def home_kernel(back_ref, tgt_ref, wgt_ref, tok_ref, cot_ref, gain_ref, out_ref, grad_ref, pick_ref, acc_ref, rms_ref, sum_ref):
    step = pl.program_id(0)
    count, features = tok_ref.shape
    rows, width = back_ref.shape

    @pl.when(step == 0)
    def _():
        number = lax.broadcasted_iota(jnp.int32, (count, rows), 1)
        targets = tgt_ref[...]
        t0, t1 = targets[:, :1], targets[:, 1:]
        one = lambda hit: jnp.where(hit, 1.0, 0.0).astype(BF)
        pick_ref[:count, :] = one(number == t0)
        pick_ref[count : 2 * count, :] = one(number == t1)
        pick_ref[2 * count :, :] = one((number == t0 + SLOTS) | (number == t1 + SLOTS))
        exact = tok_ref[...].astype(F32)
        rms_ref[...] = lax.rsqrt(jnp.mean(exact * exact, axis=1, keepdims=True) + 1e-06)
        sum_ref[...] = jnp.zeros_like(sum_ref)

    at = pl.ds(pl.multiple_of(step * width, width), width)
    weights = wgt_ref[...]
    got = nn(pick_ref[...], back_ref[...])
    exact = tok_ref[:, at].astype(F32)
    out_ref[...] = exact + (weights[:, :1] * got[:count] + weights[:, 1:] * got[count : 2 * count])
    unit_grad = got[2 * count :] * gain_ref[:, at]
    acc_ref[:, at] = unit_grad
    rms = rms_ref[...]
    sum_ref[...] += jnp.sum(unit_grad * (exact * rms), axis=1, keepdims=True)

    @pl.when(step == pl.num_programs(0) - 1)
    def _():
        mean = sum_ref[...] * (1.0 / features)
        for i in range(0, features, width):
            cols = slice(i, i + width)
            unit = tok_ref[:, cols].astype(F32) * rms
            grad_ref[:, cols] = cot_ref[:, cols].astype(F32) + rms * (acc_ref[:, cols] - unit * mean)


def finish(back, targets, weights, tokens, cot, gain):
    count, features = tokens.shape
    rows = back.shape[0]
    steps = 4
    width = features // steps
    return pl.pallas_call(
        home_kernel,
        out_shape=(
            jax.ShapeDtypeStruct((count, features), F32),
            jax.ShapeDtypeStruct((count, features), F32),
        ),
        grid=(steps,),
        in_specs=[
            pl.BlockSpec((rows, width), lambda i: (0, i)),
            whole((count, 2)),
            whole((count, 2)),
            whole(tokens.shape),
            whole(cot.shape),
            whole((1, features)),
        ],
        out_specs=(pl.BlockSpec((count, width), lambda i: (0, i)), whole((count, features))),
        scratch_shapes=[
            pltpu.VMEM((3 * count, rows), BF),
            pltpu.VMEM((count, features), F32),
            pltpu.VMEM((count, 1), F32),
            pltpu.VMEM((count, 1), F32),
        ],
        compiler_params=params(MB),
        cost_estimate=cost(6 * count * rows * features, 10 << 20),
    )(back, targets, weights, tokens, cot, gain)


def exchange(rows):
    return lax.all_to_all(rows, ALL, split_axis=0, concat_axis=0, tiled=True)


def body(tokens, norm_gain, query_weight, values, blocks, weights, out_cotangent):
    features = tokens.shape[1]
    owners = lax.axis_size(ALL)
    at = jnp.stack([lax.axis_index("x"), lax.axis_index("core")]).astype(jnp.int32)
    gain = norm_gain.reshape(1, features)
    payload, targets = build_payload(
        tokens, gain, blocks, weights, out_cotangent, owners, values.shape[0] // BLOCK
    )
    own, sib = gather_weight(query_weight)
    got = exchange(payload)
    fold = fold_weight(at, own, sib, values)
    answers, n, c, g, s = serve(got, fold, values, features)
    back = exchange(answers)
    grad_values = value_grads(at, own, sib, n, c, g, s)
    layer_out, grad_tokens = finish(back, targets, weights, tokens, out_cotangent, gain)
    return layer_out, grad_tokens, grad_values


def solution(mesh):
    fine = Mesh(np.asarray(mesh.devices).reshape(4, 2, 4, 4), ALL)
    rows = P(ALL, None)
    return jax.shard_map(
        body,
        mesh=fine,
        in_specs=(rows, P(), P(None, ("x", "core")), rows, rows, rows, rows),
        out_specs=(rows, rows, rows),
        check_vma=False,
    )
```

```python
import functools

import jax
import jax.numpy as jnp
import numpy as np
from jax import lax
from jax.experimental import pallas as pl
from jax.experimental.pallas import tpu as pltpu
from jax.sharding import Mesh
from jax.sharding import PartitionSpec as P

BLOCK = 64
SLOTS = 4
CHUNK = 2 * SLOTS
LANES = 128
ALL = ("x", "core", "z", "y")
BF = jnp.bfloat16
F32 = jnp.float32
MB = 60
HINT = 1


def params(megabytes):
    return pltpu.CompilerParams(vmem_limit_bytes=megabytes << 20)


def cost(flops, bytes_accessed):
    return pl.CostEstimate(
        flops=int(flops), bytes_accessed=int(bytes_accessed), transcendentals=0
    )


def whole(shape):
    return pl.BlockSpec(shape, lambda *_: (0,) * len(shape))


def nt(left, right):
    return lax.dot_general(left, right, (((1,), (1,)), ((), ())), preferred_element_type=F32)


def nn(left, right):
    return jnp.dot(left, right, preferred_element_type=F32)


def send_kernel(span, tok_ref, gain_ref, blk_ref, wgt_ref, cot_ref, x_ref, tgt_ref, rows_ref, route_ref):
    step = pl.program_id(0)
    count, features = tok_ref.shape
    step_rows = x_ref.shape[0]

    @pl.when(step == 0)
    def _():
        exact = tok_ref[...].astype(F32)
        rms = lax.rsqrt(jnp.mean(exact * exact, axis=1, keepdims=True) + 1e-06)
        rows_ref[:count, :] = ((exact * rms) * gain_ref[...]).astype(BF)
        rows_ref[count:, :] = cot_ref[...]
        square = (count, count)
        sub = lax.broadcasted_iota(jnp.int32, square, 0)
        lane = lax.broadcasted_iota(jnp.int32, square, 1)
        blocks = blk_ref[...]
        weights = wgt_ref[...]
        col = [jnp.broadcast_to(blocks[:, k : k + 1], square) for k in range(2)]
        row = [c.astype(F32).T.astype(jnp.int32) for c in col]
        wrow = [jnp.broadcast_to(weights[:, k : k + 1], square).T for k in range(2)]
        own_col = [c // span for c in col]
        own_row = [r // span for r in row]
        one = lambda hit: jnp.where(hit, 1, 0)
        before = [
            [one((own_col[0] == own_row[0]) & (sub < lane))],
            [one(own_col[0] == own_row[1]), one((own_col[1] == own_row[1]) & (sub < lane))],
        ]
        before_t = [
            [one((own_row[0] == own_col[0]) & (lane < sub))],
            [one(own_row[0] == own_col[1]), one((own_row[1] == own_col[1]) & (lane < sub))],
        ]
        for k in range(2):
            slot_row = sum(jnp.sum(e, axis=0, keepdims=True) for e in before[k])
            slot_col = sum(jnp.sum(e, axis=1, keepdims=True) for e in before_t[k])
            target = own_row[k][:1, :] * CHUNK + slot_row
            route_ref[k : k + 1, :] = target.astype(F32)
            route_ref[2 + k : 3 + k, :] = (row[k][:1, :] % span).astype(F32) + 1.0
            route_ref[4 + k : 5 + k, :] = wrow[k][:1, :]
            tgt_ref[:, k : k + 1] = own_col[k][:, :1] * CHUNK + slot_col

    route = route_ref[...]
    shape = (step_rows, count)
    number = (lax.broadcasted_iota(jnp.int32, shape, 0) + step * step_rows).astype(F32)
    t0, t1 = route[0:1, :], route[1:2, :]
    n0, n1 = number == t0, number == t1
    c0, c1 = number == t0 + SLOTS, number == t1 + SLOTS
    scale = jnp.sum(jnp.where(c0, route[4:5, :], 0.0) + jnp.where(c1, route[5:6, :], 0.0), axis=1, keepdims=True)
    ident = jnp.sum(
        jnp.where(n0 | c0, route[2:3, :], 0.0) + jnp.where(n1 | c1, route[3:4, :], 0.0),
        axis=1,
        keepdims=True,
    )
    is_cot = (lax.broadcasted_iota(jnp.int32, (step_rows, 1), 0) % CHUNK) >= SLOTS
    scale = jnp.where(is_cot, scale, 1.0)
    pick = jnp.concatenate(
        [jnp.where(n0 | n1, 1.0, 0.0), jnp.where(c0 | c1, 1.0, 0.0)], axis=1
    ).astype(BF)
    width = 512
    for at in range(0, features, width):
        rows = nn(pick, rows_ref[:, at : at + width])
        x_ref[:, at : at + width] = (rows * scale).astype(BF)
    x_ref[:, features:] = jnp.broadcast_to(ident - 1.0, (step_rows, LANES)).astype(BF)


def build_payload(tokens, gain, blocks, weights, cot, owners, span):
    count, features = tokens.shape
    rows = owners * CHUNK
    steps = 4
    return pl.pallas_call(
        functools.partial(send_kernel, span),
        out_shape=(
            jax.ShapeDtypeStruct((rows, features + LANES), BF),
            jax.ShapeDtypeStruct((count, 2), jnp.int32),
        ),
        grid=(steps,),
        in_specs=[
            whole((count, features)),
            whole((1, features)),
            whole((count, 2)),
            whole((count, 2)),
            whole((count, features)),
        ],
        out_specs=(
            pl.BlockSpec((rows // steps, features + LANES), lambda i: (i, 0)),
            whole((count, 2)),
        ),
        scratch_shapes=[pltpu.VMEM((2 * count, features), BF), pltpu.VMEM((8, count), F32)],
        compiler_params=params(MB),
        cost_estimate=cost(2 * rows * 2 * count * features, 6 << 20),
    )(tokens, gain, blocks, weights, cot)


PART = 256
SHIFTS = (1, 3, 2)


def shifted(rows, axis):
    return [lax.ppermute(rows, axis, [(i, (i + by) % 4) for i in range(4)]) for by in SHIFTS]


def assemble_kernel(at_ref, w_ref, *refs):
    part, along_y, along_z, out_ref = refs[:3], refs[3:6], refs[6:9], refs[9]
    width = w_ref.shape[1]
    out_ref[0] = w_ref[...]
    for side, lines in ((0, along_y), (1, along_z)):
        base = side * 4 * PART
        me = at_ref[side]
        rows = pl.ds(pl.multiple_of(base + me * PART, 64), PART)
        for k in range(3):
            out_ref[k + 1, rows, :] = part[k][side * PART : (side + 1) * PART, :]
        for line, by in zip(lines, SHIFTS):
            rows = pl.ds(pl.multiple_of(base + lax.rem(me + 4 - by, 4) * PART, 64), PART)
            for k in range(3):
                out_ref[k + 1, rows, :] = line[:, k * width : (k + 1) * width]


def assemble(weight, part, along_y, along_z):
    features, width = weight.shape
    places = jnp.stack([lax.axis_index("y"), lax.axis_index("z")]).astype(jnp.int32)
    arrays = [weight, *part, *along_y, *along_z]
    return pl.pallas_call(
        assemble_kernel,
        out_shape=jax.ShapeDtypeStruct((4, features, width), BF),
        in_specs=[pl.BlockSpec(memory_space=pltpu.SMEM)]
        + [pl.BlockSpec(memory_space=pltpu.VMEM)] * len(arrays),
        out_specs=pl.BlockSpec(memory_space=pltpu.VMEM),
        compiler_params=params(24),
        cost_estimate=cost(1, HINT),
    )(places, *arrays)


def own_part(weight):
    y, z = lax.axis_index("y"), lax.axis_index("z")
    width = weight.shape[1]
    return jnp.concatenate(
        [
            lax.dynamic_slice(weight, (y * PART, 0), (PART, width)),
            lax.dynamic_slice(weight, (4 * PART + z * PART, 0), (PART, width)),
        ],
        axis=0,
    )


def slice_at(step, at):
    turn = jnp.where(step % 4 == 0, 0, jnp.where(step % 4 == 1, 3, step % 4 - 1))
    return 2 * ((at[0] + turn) % 4) + jnp.where(step < 4, at[1], 1 - at[1])


def fold_kernel(at_ref, own_ref, sib_ref, val_ref, out_ref, vt_ref, left_ref):
    half, _, width = own_ref.shape
    tile = 256

    @pl.when(pl.program_id(0) == 0)
    def _():
        for a in range(2 * half):
            turn = (0, 3, 1, 2)[a % half]
            parity = at_ref[1] if a < half else 1 - at_ref[1]
            column = 2 * lax.rem(at_ref[0] + turn, 4) + parity
            at = pl.ds(pl.multiple_of(column * width, width), width)
            vt_ref[a * width : (a + 1) * width, :] = val_ref[:, at].T

    for a in range(half):
        left_ref[:, a * width : (a + 1) * width] = own_ref[a]
        left_ref[:, (half + a) * width : (half + a + 1) * width] = sib_ref[a]
    for i in range(0, out_ref.shape[1], tile):
        at = slice(i, i + tile)
        out_ref[:, at] = nn(left_ref[...], vt_ref[:, at]).astype(BF)


def fold_weight(at, own, sib, values):
    value_rows, features = values.shape
    half, _, width = own.shape
    steps = 4
    rows = features // steps
    block = pl.BlockSpec((half, rows, width), lambda i, at: (0, i, 0))
    return pl.pallas_call(
        fold_kernel,
        out_shape=jax.ShapeDtypeStruct((features, value_rows), BF),
        grid_spec=pltpu.PrefetchScalarGridSpec(
            num_scalar_prefetch=1,
            grid=(steps,),
            in_specs=[block, block, whole(values.shape)],
            out_specs=pl.BlockSpec((rows, value_rows), lambda i, at: (i, 0)),
            scratch_shapes=[pltpu.VMEM((features, value_rows), BF), pltpu.VMEM((rows, features), BF)],
        ),
        compiler_params=params(MB),
        cost_estimate=cost(1, 1),
    )(at, own, sib, values)


def serve_kernel(scale, x_hbm, fold_hbm, val_hbm, y_hbm, n_hbm, c_hbm, g_hbm, s_hbm,
                 x_buf, fold_buf, val_buf, n_buf, c_buf, id_buf, g_buf, s_buf, y_buf,
                 x_sem, f_sem, v_sem, y_sem, o_sem):
    rows = x_buf.shape[0]
    features = n_buf.shape[1]
    value_rows = val_buf.shape[0]
    parts = x_sem.shape[0]
    step_rows = rows // parts
    step_cols = value_rows // parts
    slots = rows // 2

    def x_copy(i):
        at = pl.ds(i * step_rows, step_rows)
        return pltpu.make_async_copy(x_hbm.at[at, :], x_buf.at[at, :], x_sem.at[i])

    def f_copy(i):
        return pltpu.make_async_copy(
            fold_hbm.at[:, pl.ds(i * step_cols, step_cols)], fold_buf.at[i], f_sem.at[i]
        )

    def v_copy(i):
        at = pl.ds(i * step_cols, step_cols)
        return pltpu.make_async_copy(val_hbm.at[at, :], val_buf.at[at, :], v_sem.at[i])

    for i in range(parts):
        x_copy(i).start()
    for i in range(parts):
        f_copy(i).start()
        v_copy(i).start()

    take = 32
    low = lax.broadcasted_iota(jnp.int32, (take // 16, 8, 1), 1) < SLOTS

    def split(x):
        pairs = x.astype(F32).reshape(take // 16, 16, x.shape[1])
        first, second = pairs[:, :8], pairs[:, 8:]
        upper = jnp.where(low, first, pltpu.roll(second, 4, 1))
        lower = jnp.where(low, pltpu.roll(first, 4, 1), second)
        return upper.reshape(take // 2, x.shape[1]), lower.reshape(take // 2, x.shape[1])

    for i in range(parts):
        x_copy(i).wait()

        @pl.loop(i * step_rows // take, (i + 1) * step_rows // take)
        def _(r):
            src = pl.ds(pl.multiple_of(r * take, take), take)
            dst = pl.ds(pl.multiple_of(r * (take // 2), take // 2), take // 2)
            upper, lower = split(x_buf[src, :features])
            n_buf[dst, :] = upper.astype(BF)
            c_buf[dst, :] = lower.astype(BF)
            ident, _ = split(x_buf[src, features:])
            id_buf[dst, :] = ident

    kept = [pltpu.make_async_copy(n_buf, n_hbm, o_sem.at[0]), pltpu.make_async_copy(c_buf, c_hbm, o_sem.at[1])]
    for copy in kept:
        copy.start()

    for j in range(parts):
        f_copy(j).wait()
        v_copy(j).wait()
        scores = nn(n_buf[...], fold_buf[j]) * scale
        cot_scores = nt(c_buf[...], val_buf[j * step_cols : (j + 1) * step_cols, :])
        sig = 1.0 / (1.0 + jnp.exp(-scores))
        block_of = (lax.broadcasted_iota(jnp.int32, (1, step_cols), 1) // BLOCK + j * (step_cols // BLOCK)).astype(F32)
        mine = id_buf[:, :1] == block_of
        g_buf[j] = jnp.where(mine, sig, 0.0).astype(BF)
        s_buf[j] = jnp.where(mine, cot_scores * sig * (1.0 - sig) * scale, 0.0).astype(BF)
        at = pl.ds(j * step_cols, step_cols)
        kept.append(pltpu.make_async_copy(g_buf.at[j], g_hbm.at[:, at], o_sem.at[2 + j]))
        kept.append(pltpu.make_async_copy(s_buf.at[j], s_hbm.at[:, at], o_sem.at[2 + parts + j]))
        kept[-2].start()
        kept[-1].start()

    tiles = y_sem.shape[0]
    width = features // tiles
    lows = lax.broadcasted_iota(jnp.int32, (slots // 8, 8, 1), 1) < SLOTS

    def y_copy(i):
        at = pl.ds(pl.multiple_of(i * width, width), width)
        return pltpu.make_async_copy(y_buf.at[i], y_hbm.at[:, at], y_sem.at[i])

    @pl.loop(0, tiles)
    def _(i):
        at = pl.ds(pl.multiple_of(i * width, width), width)
        read = nn(g_buf[0], val_buf[0:step_cols, at])
        grad = nt(s_buf[0], fold_buf[0, at, :])
        for j in range(1, parts):
            read += nn(g_buf[j], val_buf[j * step_cols : (j + 1) * step_cols, at])
            grad += nt(s_buf[j], fold_buf[j, at, :])
        read = read.reshape(slots // 8, 8, width)
        grad = grad.reshape(slots // 8, 8, width)
        first = jnp.where(lows, read, pltpu.roll(grad, 4, 1))
        second = jnp.where(lows, pltpu.roll(read, 4, 1), grad)
        y_buf[i] = jnp.concatenate([first, second], axis=1).reshape(rows, width).astype(BF)
        y_copy(i).start()

    for copy in kept:
        copy.wait()
    for i in range(tiles):
        y_copy(i).wait()


def serve(x, fold, values, features):
    rows = x.shape[0]
    slots = rows // 2
    value_rows = values.shape[0]
    parts, tiles = 4, 8
    step_cols = value_rows // parts
    any_spec = pl.BlockSpec(memory_space=pl.ANY)
    return pl.pallas_call(
        functools.partial(serve_kernel, float(features) ** (-0.5)),
        out_shape=(
            jax.ShapeDtypeStruct((rows, features), BF),
            jax.ShapeDtypeStruct((slots, features), BF),
            jax.ShapeDtypeStruct((slots, features), BF),
            jax.ShapeDtypeStruct((slots, value_rows), BF),
            jax.ShapeDtypeStruct((slots, value_rows), BF),
        ),
        in_specs=[any_spec] * 3,
        out_specs=(any_spec,) * 5,
        scratch_shapes=[
            pltpu.VMEM(x.shape, BF),
            pltpu.VMEM((parts, features, step_cols), BF),
            pltpu.VMEM(values.shape, BF),
            pltpu.VMEM((slots, features), BF),
            pltpu.VMEM((slots, features), BF),
            pltpu.VMEM((slots, LANES), F32),
            pltpu.VMEM((parts, slots, step_cols), BF),
            pltpu.VMEM((parts, slots, step_cols), BF),
            pltpu.VMEM((tiles, rows, features // tiles), BF),
            pltpu.SemaphoreType.DMA((parts,)),
            pltpu.SemaphoreType.DMA((parts,)),
            pltpu.SemaphoreType.DMA((parts,)),
            pltpu.SemaphoreType.DMA((tiles,)),
            pltpu.SemaphoreType.DMA((2 + 2 * parts,)),
        ],
        compiler_params=params(MB),
        cost_estimate=cost(4 * rows * value_rows * features, 20 << 20),
    )(x, fold, values)


def grad_kernel(at_ref, own_ref, sib_ref, n_ref, c_ref, g_ref, s_ref, out_ref, gt_ref, st_ref):
    slots = n_ref.shape[0]
    tile = 256

    @pl.when(pl.program_id(0) == 0)
    def _():
        for i in range(0, slots, tile):
            gt_ref[:, i : i + tile] = g_ref[i : i + tile, :].T
            st_ref[:, i : i + tile] = s_ref[i : i + tile, :].T

    weight = jnp.where(pl.program_id(0) < 4, own_ref[0], sib_ref[0])
    queries = nn(n_ref[...], weight).astype(BF)
    for i in range(0, out_ref.shape[0], tile):
        total = nn(gt_ref[i : i + tile, :], c_ref[...]) + nn(st_ref[i : i + tile, :], queries)
        out_ref[i : i + tile, :] = total.astype(BF)


def value_grads(at, own, sib, n, c, g, s):
    half, features, width = own.shape
    slots, value_rows = g.shape
    return pl.pallas_call(
        grad_kernel,
        out_shape=jax.ShapeDtypeStruct((value_rows, features), BF),
        grid_spec=pltpu.PrefetchScalarGridSpec(
            num_scalar_prefetch=1,
            grid=(2 * half,),
            in_specs=[
                pl.BlockSpec((1, features, width), lambda a, x: (jnp.minimum(a, half - 1), 0, 0)),
                pl.BlockSpec((1, features, width), lambda a, x: (jnp.maximum(a - half, 0), 0, 0)),
                whole(n.shape),
                pl.BlockSpec((slots, width), lambda a, x: (0, slice_at(a, x))),
                whole(g.shape),
                whole(s.shape),
            ],
            out_specs=pl.BlockSpec((value_rows, width), lambda a, x: (0, slice_at(a, x))),
            scratch_shapes=[pltpu.VMEM((value_rows, slots), BF), pltpu.VMEM((value_rows, slots), BF)],
        ),
        compiler_params=params(MB),
        cost_estimate=cost(6 * slots * value_rows * features, 24 << 20),
    )(at, own, sib, n, c, g, s)


def home_kernel(back_ref, tgt_ref, wgt_ref, tok_ref, cot_ref, gain_ref, out_ref, grad_ref, pick_ref, acc_ref, rms_ref, sum_ref):
    step = pl.program_id(0)
    count, features = tok_ref.shape
    rows, width = back_ref.shape

    @pl.when(step == 0)
    def _():
        number = lax.broadcasted_iota(jnp.int32, (count, rows), 1)
        targets = tgt_ref[...]
        t0, t1 = targets[:, :1], targets[:, 1:]
        one = lambda hit: jnp.where(hit, 1.0, 0.0).astype(BF)
        pick_ref[:count, :] = one(number == t0)
        pick_ref[count : 2 * count, :] = one(number == t1)
        pick_ref[2 * count :, :] = one((number == t0 + SLOTS) | (number == t1 + SLOTS))
        exact = tok_ref[...].astype(F32)
        rms_ref[...] = lax.rsqrt(jnp.mean(exact * exact, axis=1, keepdims=True) + 1e-06)
        sum_ref[...] = jnp.zeros_like(sum_ref)

    at = pl.ds(pl.multiple_of(step * width, width), width)
    weights = wgt_ref[...]
    got = nn(pick_ref[...], back_ref[...])
    exact = tok_ref[:, at].astype(F32)
    out_ref[...] = exact + (weights[:, :1] * got[:count] + weights[:, 1:] * got[count : 2 * count])
    unit_grad = got[2 * count :] * gain_ref[:, at]
    acc_ref[:, at] = unit_grad
    rms = rms_ref[...]
    sum_ref[...] += jnp.sum(unit_grad * (exact * rms), axis=1, keepdims=True)

    @pl.when(step == pl.num_programs(0) - 1)
    def _():
        mean = sum_ref[...] * (1.0 / features)
        for i in range(0, features, width):
            cols = slice(i, i + width)
            unit = tok_ref[:, cols].astype(F32) * rms
            grad_ref[:, cols] = cot_ref[:, cols].astype(F32) + rms * (acc_ref[:, cols] - unit * mean)


def finish(back, targets, weights, tokens, cot, gain):
    count, features = tokens.shape
    rows = back.shape[0]
    steps = 4
    width = features // steps
    return pl.pallas_call(
        home_kernel,
        out_shape=(
            jax.ShapeDtypeStruct((count, features), F32),
            jax.ShapeDtypeStruct((count, features), F32),
        ),
        grid=(steps,),
        in_specs=[
            pl.BlockSpec((rows, width), lambda i: (0, i)),
            whole((count, 2)),
            whole((count, 2)),
            whole(tokens.shape),
            whole(cot.shape),
            whole((1, features)),
        ],
        out_specs=(pl.BlockSpec((count, width), lambda i: (0, i)), whole((count, features))),
        scratch_shapes=[
            pltpu.VMEM((3 * count, rows), BF),
            pltpu.VMEM((count, features), F32),
            pltpu.VMEM((count, 1), F32),
            pltpu.VMEM((count, 1), F32),
        ],
        compiler_params=params(MB),
        cost_estimate=cost(6 * count * rows * features, 10 << 20),
    )(back, targets, weights, tokens, cot, gain)


def exchange(rows):
    return lax.all_to_all(rows, ALL, split_axis=0, concat_axis=0, tiled=True)


def body(tokens, norm_gain, query_weight, values, blocks, weights, out_cotangent):
    features = tokens.shape[1]
    owners = lax.axis_size(ALL)
    at = jnp.stack([lax.axis_index("x"), lax.axis_index("core")]).astype(jnp.int32)
    gain = norm_gain.reshape(1, features)
    part = shifted(own_part(query_weight), "x")
    payload, targets = build_payload(
        tokens, gain, blocks, weights, out_cotangent, owners, values.shape[0] // BLOCK
    )
    set_y = jnp.concatenate([p[:PART] for p in part], axis=1)
    set_z = jnp.concatenate([p[PART:] for p in part], axis=1)
    set_y, set_z, payload = lax.optimization_barrier((set_y, set_z, payload))
    own = assemble(query_weight, part, shifted(set_y, "y"), shifted(set_z, "z"))
    sib = lax.ppermute(own, "core", [(0, 1), (1, 0)])
    got = exchange(payload)
    fold = fold_weight(at, own, sib, values)
    answers, n, c, g, s = serve(got, fold, values, features)
    back = exchange(answers)
    grad_values = value_grads(at, own, sib, n, c, g, s)
    layer_out, grad_tokens = finish(back, targets, weights, tokens, out_cotangent, gain)
    return layer_out, grad_tokens, grad_values


def solution(mesh):
    fine = Mesh(np.asarray(mesh.devices).reshape(4, 2, 4, 4), ALL)
    rows = P(ALL, None)
    return jax.shard_map(
        body,
        mesh=fine,
        in_specs=(rows, P(), P(None, ("x", "core")), rows, rows, rows, rows),
        out_specs=(rows, rows, rows),
        check_vma=False,
    )
```

```python
import functools

import jax
import jax.numpy as jnp
import numpy as np
from jax import lax
from jax.experimental import pallas as pl
from jax.experimental.pallas import tpu as pltpu
from jax.sharding import Mesh
from jax.sharding import PartitionSpec as P

BLOCK = 64
SLOTS = 4
CHUNK = 2 * SLOTS
LANES = 128
ALL = ("x", "core", "z", "y")
BF = jnp.bfloat16
F32 = jnp.float32
MB = 60
HINT = 1


def params(megabytes):
    return pltpu.CompilerParams(vmem_limit_bytes=megabytes << 20)


def cost(flops, bytes_accessed):
    return pl.CostEstimate(
        flops=int(flops), bytes_accessed=int(bytes_accessed), transcendentals=0
    )


def whole(shape):
    return pl.BlockSpec(shape, lambda *_: (0,) * len(shape))


def nt(left, right):
    return lax.dot_general(left, right, (((1,), (1,)), ((), ())), preferred_element_type=F32)


def nn(left, right):
    return jnp.dot(left, right, preferred_element_type=F32)


def send_kernel(span, tok_ref, gain_ref, blk_ref, wgt_ref, cot_ref, x_ref, tgt_ref, rows_ref, route_ref):
    step = pl.program_id(0)
    count, features = tok_ref.shape
    step_rows = x_ref.shape[0]

    @pl.when(step == 0)
    def _():
        exact = tok_ref[...].astype(F32)
        rms = lax.rsqrt(jnp.mean(exact * exact, axis=1, keepdims=True) + 1e-06)
        rows_ref[:count, :] = ((exact * rms) * gain_ref[...]).astype(BF)
        rows_ref[count:, :] = cot_ref[...]
        square = (count, count)
        sub = lax.broadcasted_iota(jnp.int32, square, 0)
        lane = lax.broadcasted_iota(jnp.int32, square, 1)
        blocks = blk_ref[...]
        weights = wgt_ref[...]
        col = [jnp.broadcast_to(blocks[:, k : k + 1], square) for k in range(2)]
        row = [c.astype(F32).T.astype(jnp.int32) for c in col]
        wrow = [jnp.broadcast_to(weights[:, k : k + 1], square).T for k in range(2)]
        own_col = [c // span for c in col]
        own_row = [r // span for r in row]
        one = lambda hit: jnp.where(hit, 1, 0)
        before = [
            [one((own_col[0] == own_row[0]) & (sub < lane))],
            [one(own_col[0] == own_row[1]), one((own_col[1] == own_row[1]) & (sub < lane))],
        ]
        before_t = [
            [one((own_row[0] == own_col[0]) & (lane < sub))],
            [one(own_row[0] == own_col[1]), one((own_row[1] == own_col[1]) & (lane < sub))],
        ]
        for k in range(2):
            slot_row = sum(jnp.sum(e, axis=0, keepdims=True) for e in before[k])
            slot_col = sum(jnp.sum(e, axis=1, keepdims=True) for e in before_t[k])
            target = own_row[k][:1, :] * CHUNK + slot_row
            route_ref[k : k + 1, :] = target.astype(F32)
            route_ref[2 + k : 3 + k, :] = (row[k][:1, :] % span).astype(F32) + 1.0
            route_ref[4 + k : 5 + k, :] = wrow[k][:1, :]
            tgt_ref[:, k : k + 1] = own_col[k][:, :1] * CHUNK + slot_col

    route = route_ref[...]
    shape = (step_rows, count)
    number = (lax.broadcasted_iota(jnp.int32, shape, 0) + step * step_rows).astype(F32)
    t0, t1 = route[0:1, :], route[1:2, :]
    n0, n1 = number == t0, number == t1
    c0, c1 = number == t0 + SLOTS, number == t1 + SLOTS
    scale = jnp.sum(jnp.where(c0, route[4:5, :], 0.0) + jnp.where(c1, route[5:6, :], 0.0), axis=1, keepdims=True)
    ident = jnp.sum(
        jnp.where(n0 | c0, route[2:3, :], 0.0) + jnp.where(n1 | c1, route[3:4, :], 0.0),
        axis=1,
        keepdims=True,
    )
    is_cot = (lax.broadcasted_iota(jnp.int32, (step_rows, 1), 0) % CHUNK) >= SLOTS
    scale = jnp.where(is_cot, scale, 1.0)
    pick = jnp.concatenate(
        [jnp.where(n0 | n1, 1.0, 0.0), jnp.where(c0 | c1, 1.0, 0.0)], axis=1
    ).astype(BF)
    width = 512
    for at in range(0, features, width):
        rows = nn(pick, rows_ref[:, at : at + width])
        x_ref[:, at : at + width] = (rows * scale).astype(BF)
    x_ref[:, features:] = jnp.broadcast_to(ident - 1.0, (step_rows, LANES)).astype(BF)


def build_payload(tokens, gain, blocks, weights, cot, owners, span):
    count, features = tokens.shape
    rows = owners * CHUNK
    steps = 4
    return pl.pallas_call(
        functools.partial(send_kernel, span),
        out_shape=(
            jax.ShapeDtypeStruct((rows, features + LANES), BF),
            jax.ShapeDtypeStruct((count, 2), jnp.int32),
        ),
        grid=(steps,),
        in_specs=[
            whole((count, features)),
            whole((1, features)),
            whole((count, 2)),
            whole((count, 2)),
            whole((count, features)),
        ],
        out_specs=(
            pl.BlockSpec((rows // steps, features + LANES), lambda i: (i, 0)),
            whole((count, 2)),
        ),
        scratch_shapes=[pltpu.VMEM((2 * count, features), BF), pltpu.VMEM((8, count), F32)],
        compiler_params=params(MB),
        cost_estimate=cost(2 * rows * 2 * count * features, 6 << 20),
    )(tokens, gain, blocks, weights, cot)


DIRECT = 1024
SHIFTS = (1, 3, 2)


def shifted(rows, axis):
    return [lax.ppermute(rows, axis, [(i, (i + by) % 4) for i in range(4)]) for by in SHIFTS]


def assemble_kernel(at_ref, w_ref, *refs):
    direct, part, along_y, out_ref = refs[:3], refs[3:6], refs[6:9], refs[9]
    width = w_ref.shape[1]
    count = part[0].shape[0]
    me = at_ref[0]
    out_ref[0] = w_ref[...]
    rows = pl.ds(pl.multiple_of(DIRECT + me * count, 64), count)
    for k in range(3):
        out_ref[k + 1, :DIRECT, :] = direct[k][...]
        out_ref[k + 1, rows, :] = part[k][...]
    for line, by in zip(along_y, SHIFTS):
        rows = pl.ds(pl.multiple_of(DIRECT + lax.rem(me + 4 - by, 4) * count, 64), count)
        for k in range(3):
            out_ref[k + 1, rows, :] = line[:, k * width : (k + 1) * width]


def assemble(weight, direct, part, along_y):
    features, width = weight.shape
    place = lax.axis_index("y").astype(jnp.int32).reshape(1)
    arrays = [weight, *direct, *part, *along_y]
    return pl.pallas_call(
        assemble_kernel,
        out_shape=jax.ShapeDtypeStruct((4, features, width), BF),
        in_specs=[pl.BlockSpec(memory_space=pltpu.SMEM)]
        + [pl.BlockSpec(memory_space=pltpu.VMEM)] * len(arrays),
        out_specs=pl.BlockSpec(memory_space=pltpu.VMEM),
        compiler_params=params(24),
        cost_estimate=cost(1, HINT),
    )(place, *arrays)


def slice_at(step, at):
    turn = jnp.where(step % 4 == 0, 0, jnp.where(step % 4 == 1, 3, step % 4 - 1))
    return 2 * ((at[0] + turn) % 4) + jnp.where(step < 4, at[1], 1 - at[1])


def fold_kernel(at_ref, own_ref, sib_ref, val_ref, out_ref, vt_ref, left_ref):
    half, _, width = own_ref.shape
    tile = 256

    @pl.when(pl.program_id(0) == 0)
    def _():
        for a in range(2 * half):
            turn = (0, 3, 1, 2)[a % half]
            parity = at_ref[1] if a < half else 1 - at_ref[1]
            column = 2 * lax.rem(at_ref[0] + turn, 4) + parity
            at = pl.ds(pl.multiple_of(column * width, width), width)
            vt_ref[a * width : (a + 1) * width, :] = val_ref[:, at].T

    for a in range(half):
        left_ref[:, a * width : (a + 1) * width] = own_ref[a]
        left_ref[:, (half + a) * width : (half + a + 1) * width] = sib_ref[a]
    for i in range(0, out_ref.shape[1], tile):
        at = slice(i, i + tile)
        out_ref[:, at] = nn(left_ref[...], vt_ref[:, at]).astype(BF)


def fold_weight(at, own, sib, values):
    value_rows, features = values.shape
    half, _, width = own.shape
    steps = 4
    rows = features // steps
    block = pl.BlockSpec((half, rows, width), lambda i, at: (0, i, 0))
    return pl.pallas_call(
        fold_kernel,
        out_shape=jax.ShapeDtypeStruct((features, value_rows), BF),
        grid_spec=pltpu.PrefetchScalarGridSpec(
            num_scalar_prefetch=1,
            grid=(steps,),
            in_specs=[block, block, whole(values.shape)],
            out_specs=pl.BlockSpec((rows, value_rows), lambda i, at: (i, 0)),
            scratch_shapes=[pltpu.VMEM((features, value_rows), BF), pltpu.VMEM((rows, features), BF)],
        ),
        compiler_params=params(MB),
        cost_estimate=cost(1, 1),
    )(at, own, sib, values)


def serve_kernel(scale, x_hbm, fold_hbm, val_hbm, y_hbm, n_hbm, c_hbm, g_hbm, s_hbm,
                 x_buf, fold_buf, val_buf, n_buf, c_buf, id_buf, g_buf, s_buf, y_buf,
                 x_sem, f_sem, v_sem, y_sem, o_sem):
    rows = x_buf.shape[0]
    features = n_buf.shape[1]
    value_rows = val_buf.shape[0]
    parts = x_sem.shape[0]
    step_rows = rows // parts
    step_cols = value_rows // parts
    slots = rows // 2

    def x_copy(i):
        at = pl.ds(i * step_rows, step_rows)
        return pltpu.make_async_copy(x_hbm.at[at, :], x_buf.at[at, :], x_sem.at[i])

    def f_copy(i):
        return pltpu.make_async_copy(
            fold_hbm.at[:, pl.ds(i * step_cols, step_cols)], fold_buf.at[i], f_sem.at[i]
        )

    def v_copy(i):
        at = pl.ds(i * step_cols, step_cols)
        return pltpu.make_async_copy(val_hbm.at[at, :], val_buf.at[at, :], v_sem.at[i])

    for i in range(parts):
        x_copy(i).start()
    for i in range(parts):
        f_copy(i).start()
        v_copy(i).start()

    take = 32
    low = lax.broadcasted_iota(jnp.int32, (take // 16, 8, 1), 1) < SLOTS

    def split(x):
        pairs = x.astype(F32).reshape(take // 16, 16, x.shape[1])
        first, second = pairs[:, :8], pairs[:, 8:]
        upper = jnp.where(low, first, pltpu.roll(second, 4, 1))
        lower = jnp.where(low, pltpu.roll(first, 4, 1), second)
        return upper.reshape(take // 2, x.shape[1]), lower.reshape(take // 2, x.shape[1])

    for i in range(parts):
        x_copy(i).wait()

        @pl.loop(i * step_rows // take, (i + 1) * step_rows // take)
        def _(r):
            src = pl.ds(pl.multiple_of(r * take, take), take)
            dst = pl.ds(pl.multiple_of(r * (take // 2), take // 2), take // 2)
            upper, lower = split(x_buf[src, :features])
            n_buf[dst, :] = upper.astype(BF)
            c_buf[dst, :] = lower.astype(BF)
            ident, _ = split(x_buf[src, features:])
            id_buf[dst, :] = ident

    kept = [pltpu.make_async_copy(n_buf, n_hbm, o_sem.at[0]), pltpu.make_async_copy(c_buf, c_hbm, o_sem.at[1])]
    for copy in kept:
        copy.start()

    for j in range(parts):
        f_copy(j).wait()
        v_copy(j).wait()
        scores = nn(n_buf[...], fold_buf[j]) * scale
        cot_scores = nt(c_buf[...], val_buf[j * step_cols : (j + 1) * step_cols, :])
        sig = 1.0 / (1.0 + jnp.exp(-scores))
        block_of = (lax.broadcasted_iota(jnp.int32, (1, step_cols), 1) // BLOCK + j * (step_cols // BLOCK)).astype(F32)
        mine = id_buf[:, :1] == block_of
        g_buf[j] = jnp.where(mine, sig, 0.0).astype(BF)
        s_buf[j] = jnp.where(mine, cot_scores * sig * (1.0 - sig) * scale, 0.0).astype(BF)
        at = pl.ds(j * step_cols, step_cols)
        kept.append(pltpu.make_async_copy(g_buf.at[j], g_hbm.at[:, at], o_sem.at[2 + j]))
        kept.append(pltpu.make_async_copy(s_buf.at[j], s_hbm.at[:, at], o_sem.at[2 + parts + j]))
        kept[-2].start()
        kept[-1].start()

    tiles = y_sem.shape[0]
    width = features // tiles
    lows = lax.broadcasted_iota(jnp.int32, (slots // 8, 8, 1), 1) < SLOTS

    def y_copy(i):
        at = pl.ds(pl.multiple_of(i * width, width), width)
        return pltpu.make_async_copy(y_buf.at[i], y_hbm.at[:, at], y_sem.at[i])

    @pl.loop(0, tiles)
    def _(i):
        at = pl.ds(pl.multiple_of(i * width, width), width)
        read = nn(g_buf[0], val_buf[0:step_cols, at])
        grad = nt(s_buf[0], fold_buf[0, at, :])
        for j in range(1, parts):
            read += nn(g_buf[j], val_buf[j * step_cols : (j + 1) * step_cols, at])
            grad += nt(s_buf[j], fold_buf[j, at, :])
        read = read.reshape(slots // 8, 8, width)
        grad = grad.reshape(slots // 8, 8, width)
        first = jnp.where(lows, read, pltpu.roll(grad, 4, 1))
        second = jnp.where(lows, pltpu.roll(read, 4, 1), grad)
        y_buf[i] = jnp.concatenate([first, second], axis=1).reshape(rows, width).astype(BF)
        y_copy(i).start()

    for copy in kept:
        copy.wait()
    for i in range(tiles):
        y_copy(i).wait()


def serve(x, fold, values, features):
    rows = x.shape[0]
    slots = rows // 2
    value_rows = values.shape[0]
    parts, tiles = 4, 8
    step_cols = value_rows // parts
    any_spec = pl.BlockSpec(memory_space=pl.ANY)
    return pl.pallas_call(
        functools.partial(serve_kernel, float(features) ** (-0.5)),
        out_shape=(
            jax.ShapeDtypeStruct((rows, features), BF),
            jax.ShapeDtypeStruct((slots, features), BF),
            jax.ShapeDtypeStruct((slots, features), BF),
            jax.ShapeDtypeStruct((slots, value_rows), BF),
            jax.ShapeDtypeStruct((slots, value_rows), BF),
        ),
        in_specs=[any_spec] * 3,
        out_specs=(any_spec,) * 5,
        scratch_shapes=[
            pltpu.VMEM(x.shape, BF),
            pltpu.VMEM((parts, features, step_cols), BF),
            pltpu.VMEM(values.shape, BF),
            pltpu.VMEM((slots, features), BF),
            pltpu.VMEM((slots, features), BF),
            pltpu.VMEM((slots, LANES), F32),
            pltpu.VMEM((parts, slots, step_cols), BF),
            pltpu.VMEM((parts, slots, step_cols), BF),
            pltpu.VMEM((tiles, rows, features // tiles), BF),
            pltpu.SemaphoreType.DMA((parts,)),
            pltpu.SemaphoreType.DMA((parts,)),
            pltpu.SemaphoreType.DMA((parts,)),
            pltpu.SemaphoreType.DMA((tiles,)),
            pltpu.SemaphoreType.DMA((2 + 2 * parts,)),
        ],
        compiler_params=params(MB),
        cost_estimate=cost(4 * rows * value_rows * features, 20 << 20),
    )(x, fold, values)


def grad_kernel(at_ref, own_ref, sib_ref, n_ref, c_ref, g_ref, s_ref, out_ref, gt_ref, st_ref):
    slots = n_ref.shape[0]
    tile = 256

    @pl.when(pl.program_id(0) == 0)
    def _():
        for i in range(0, slots, tile):
            gt_ref[:, i : i + tile] = g_ref[i : i + tile, :].T
            st_ref[:, i : i + tile] = s_ref[i : i + tile, :].T

    weight = jnp.where(pl.program_id(0) < 4, own_ref[0], sib_ref[0])
    queries = nn(n_ref[...], weight).astype(BF)
    for i in range(0, out_ref.shape[0], tile):
        total = nn(gt_ref[i : i + tile, :], c_ref[...]) + nn(st_ref[i : i + tile, :], queries)
        out_ref[i : i + tile, :] = total.astype(BF)


def value_grads(at, own, sib, n, c, g, s):
    half, features, width = own.shape
    slots, value_rows = g.shape
    return pl.pallas_call(
        grad_kernel,
        out_shape=jax.ShapeDtypeStruct((value_rows, features), BF),
        grid_spec=pltpu.PrefetchScalarGridSpec(
            num_scalar_prefetch=1,
            grid=(2 * half,),
            in_specs=[
                pl.BlockSpec((1, features, width), lambda a, x: (jnp.minimum(a, half - 1), 0, 0)),
                pl.BlockSpec((1, features, width), lambda a, x: (jnp.maximum(a - half, 0), 0, 0)),
                whole(n.shape),
                pl.BlockSpec((slots, width), lambda a, x: (0, slice_at(a, x))),
                whole(g.shape),
                whole(s.shape),
            ],
            out_specs=pl.BlockSpec((value_rows, width), lambda a, x: (0, slice_at(a, x))),
            scratch_shapes=[pltpu.VMEM((value_rows, slots), BF), pltpu.VMEM((value_rows, slots), BF)],
        ),
        compiler_params=params(MB),
        cost_estimate=cost(6 * slots * value_rows * features, 24 << 20),
    )(at, own, sib, n, c, g, s)


def home_kernel(back_ref, tgt_ref, wgt_ref, tok_ref, cot_ref, gain_ref, out_ref, grad_ref, pick_ref, acc_ref, rms_ref, sum_ref):
    step = pl.program_id(0)
    count, features = tok_ref.shape
    rows, width = back_ref.shape

    @pl.when(step == 0)
    def _():
        number = lax.broadcasted_iota(jnp.int32, (count, rows), 1)
        targets = tgt_ref[...]
        t0, t1 = targets[:, :1], targets[:, 1:]
        one = lambda hit: jnp.where(hit, 1.0, 0.0).astype(BF)
        pick_ref[:count, :] = one(number == t0)
        pick_ref[count : 2 * count, :] = one(number == t1)
        pick_ref[2 * count :, :] = one((number == t0 + SLOTS) | (number == t1 + SLOTS))
        exact = tok_ref[...].astype(F32)
        rms_ref[...] = lax.rsqrt(jnp.mean(exact * exact, axis=1, keepdims=True) + 1e-06)
        sum_ref[...] = jnp.zeros_like(sum_ref)

    at = pl.ds(pl.multiple_of(step * width, width), width)
    weights = wgt_ref[...]
    got = nn(pick_ref[...], back_ref[...])
    exact = tok_ref[:, at].astype(F32)
    out_ref[...] = exact + (weights[:, :1] * got[:count] + weights[:, 1:] * got[count : 2 * count])
    unit_grad = got[2 * count :] * gain_ref[:, at]
    acc_ref[:, at] = unit_grad
    rms = rms_ref[...]
    sum_ref[...] += jnp.sum(unit_grad * (exact * rms), axis=1, keepdims=True)

    @pl.when(step == pl.num_programs(0) - 1)
    def _():
        mean = sum_ref[...] * (1.0 / features)
        for i in range(0, features, width):
            cols = slice(i, i + width)
            unit = tok_ref[:, cols].astype(F32) * rms
            grad_ref[:, cols] = cot_ref[:, cols].astype(F32) + rms * (acc_ref[:, cols] - unit * mean)


def finish(back, targets, weights, tokens, cot, gain):
    count, features = tokens.shape
    rows = back.shape[0]
    steps = 4
    width = features // steps
    return pl.pallas_call(
        home_kernel,
        out_shape=(
            jax.ShapeDtypeStruct((count, features), F32),
            jax.ShapeDtypeStruct((count, features), F32),
        ),
        grid=(steps,),
        in_specs=[
            pl.BlockSpec((rows, width), lambda i: (0, i)),
            whole((count, 2)),
            whole((count, 2)),
            whole(tokens.shape),
            whole(cot.shape),
            whole((1, features)),
        ],
        out_specs=(pl.BlockSpec((count, width), lambda i: (0, i)), whole((count, features))),
        scratch_shapes=[
            pltpu.VMEM((3 * count, rows), BF),
            pltpu.VMEM((count, features), F32),
            pltpu.VMEM((count, 1), F32),
            pltpu.VMEM((count, 1), F32),
        ],
        compiler_params=params(MB),
        cost_estimate=cost(6 * count * rows * features, 10 << 20),
    )(back, targets, weights, tokens, cot, gain)


def exchange(rows):
    return lax.all_to_all(rows, ALL, split_axis=0, concat_axis=0, tiled=True)


def body(tokens, norm_gain, query_weight, values, blocks, weights, out_cotangent):
    features = tokens.shape[1]
    owners = lax.axis_size(ALL)
    at = jnp.stack([lax.axis_index("x"), lax.axis_index("core")]).astype(jnp.int32)
    gain = norm_gain.reshape(1, features)
    features, width = query_weight.shape
    rows = (features - DIRECT) // 4
    mine = lax.dynamic_slice(query_weight, (DIRECT + lax.axis_index("y") * rows, 0), (rows, width))
    part = shifted(mine, "x")
    direct = shifted(query_weight[:DIRECT], "x")
    payload, targets = build_payload(
        tokens, gain, blocks, weights, out_cotangent, owners, values.shape[0] // BLOCK
    )
    set_y = jnp.concatenate(part, axis=1)
    set_y, payload = lax.optimization_barrier((set_y, payload))
    own = assemble(query_weight, direct, part, shifted(set_y, "y"))
    sib = lax.ppermute(own, "core", [(0, 1), (1, 0)])
    got = exchange(payload)
    fold = fold_weight(at, own, sib, values)
    answers, n, c, g, s = serve(got, fold, values, features)
    back = exchange(answers)
    grad_values = value_grads(at, own, sib, n, c, g, s)
    layer_out, grad_tokens = finish(back, targets, weights, tokens, out_cotangent, gain)
    return layer_out, grad_tokens, grad_values


def solution(mesh):
    fine = Mesh(np.asarray(mesh.devices).reshape(4, 2, 4, 4), ALL)
    rows = P(ALL, None)
    return jax.shard_map(
        body,
        mesh=fine,
        in_specs=(rows, P(), P(None, ("x", "core")), rows, rows, rows, rows),
        out_specs=(rows, rows, rows),
        check_vma=False,
    )
```

```python
import functools

import jax
import jax.numpy as jnp
import numpy as np
from jax import lax
from jax.experimental import pallas as pl
from jax.experimental.pallas import tpu as pltpu
from jax.sharding import Mesh
from jax.sharding import PartitionSpec as P

BLOCK = 64
SLOTS = 4
CHUNK = 2 * SLOTS
LANES = 128
ALL = ("x", "core", "z", "y")
BF = jnp.bfloat16
F32 = jnp.float32
MB = 60
HINT = 1


def params(megabytes):
    return pltpu.CompilerParams(vmem_limit_bytes=megabytes << 20)


def cost(flops, bytes_accessed):
    return pl.CostEstimate(
        flops=int(flops), bytes_accessed=int(bytes_accessed), transcendentals=0
    )


def whole(shape):
    return pl.BlockSpec(shape, lambda *_: (0,) * len(shape))


def nt(left, right):
    return lax.dot_general(left, right, (((1,), (1,)), ((), ())), preferred_element_type=F32)


def nn(left, right):
    return jnp.dot(left, right, preferred_element_type=F32)


def send_kernel(span, tok_ref, gain_ref, blk_ref, wgt_ref, cot_ref, x_ref, tgt_ref, rows_ref, route_ref):
    step = pl.program_id(0)
    count, features = tok_ref.shape
    step_rows = x_ref.shape[0]

    @pl.when(step == 0)
    def _():
        exact = tok_ref[...].astype(F32)
        rms = lax.rsqrt(jnp.mean(exact * exact, axis=1, keepdims=True) + 1e-06)
        rows_ref[:count, :] = ((exact * rms) * gain_ref[...]).astype(BF)
        rows_ref[count:, :] = cot_ref[...]
        square = (count, count)
        sub = lax.broadcasted_iota(jnp.int32, square, 0)
        lane = lax.broadcasted_iota(jnp.int32, square, 1)
        blocks = blk_ref[...]
        weights = wgt_ref[...]
        col = [jnp.broadcast_to(blocks[:, k : k + 1], square) for k in range(2)]
        row = [c.astype(F32).T.astype(jnp.int32) for c in col]
        wrow = [jnp.broadcast_to(weights[:, k : k + 1], square).T for k in range(2)]
        own_col = [c // span for c in col]
        own_row = [r // span for r in row]
        one = lambda hit: jnp.where(hit, 1, 0)
        before = [
            [one((own_col[0] == own_row[0]) & (sub < lane))],
            [one(own_col[0] == own_row[1]), one((own_col[1] == own_row[1]) & (sub < lane))],
        ]
        before_t = [
            [one((own_row[0] == own_col[0]) & (lane < sub))],
            [one(own_row[0] == own_col[1]), one((own_row[1] == own_col[1]) & (lane < sub))],
        ]
        for k in range(2):
            slot_row = sum(jnp.sum(e, axis=0, keepdims=True) for e in before[k])
            slot_col = sum(jnp.sum(e, axis=1, keepdims=True) for e in before_t[k])
            target = own_row[k][:1, :] * CHUNK + slot_row
            route_ref[k : k + 1, :] = target.astype(F32)
            route_ref[2 + k : 3 + k, :] = (row[k][:1, :] % span).astype(F32) + 1.0
            route_ref[4 + k : 5 + k, :] = wrow[k][:1, :]
            tgt_ref[:, k : k + 1] = own_col[k][:, :1] * CHUNK + slot_col

    route = route_ref[...]
    shape = (step_rows, count)
    number = (lax.broadcasted_iota(jnp.int32, shape, 0) + step * step_rows).astype(F32)
    t0, t1 = route[0:1, :], route[1:2, :]
    n0, n1 = number == t0, number == t1
    c0, c1 = number == t0 + SLOTS, number == t1 + SLOTS
    scale = jnp.sum(jnp.where(c0, route[4:5, :], 0.0) + jnp.where(c1, route[5:6, :], 0.0), axis=1, keepdims=True)
    ident = jnp.sum(
        jnp.where(n0 | c0, route[2:3, :], 0.0) + jnp.where(n1 | c1, route[3:4, :], 0.0),
        axis=1,
        keepdims=True,
    )
    is_cot = (lax.broadcasted_iota(jnp.int32, (step_rows, 1), 0) % CHUNK) >= SLOTS
    scale = jnp.where(is_cot, scale, 1.0)
    pick = jnp.concatenate(
        [jnp.where(n0 | n1, 1.0, 0.0), jnp.where(c0 | c1, 1.0, 0.0)], axis=1
    ).astype(BF)
    width = 512
    for at in range(0, features, width):
        rows = nn(pick, rows_ref[:, at : at + width])
        x_ref[:, at : at + width] = (rows * scale).astype(BF)
    x_ref[:, features:] = jnp.broadcast_to(ident - 1.0, (step_rows, LANES)).astype(BF)


def build_payload(tokens, gain, blocks, weights, cot, owners, span):
    count, features = tokens.shape
    rows = owners * CHUNK
    steps = 4
    return pl.pallas_call(
        functools.partial(send_kernel, span),
        out_shape=(
            jax.ShapeDtypeStruct((rows, features + LANES), BF),
            jax.ShapeDtypeStruct((count, 2), jnp.int32),
        ),
        grid=(steps,),
        in_specs=[
            whole((count, features)),
            whole((1, features)),
            whole((count, 2)),
            whole((count, 2)),
            whole((count, features)),
        ],
        out_specs=(
            pl.BlockSpec((rows // steps, features + LANES), lambda i: (i, 0)),
            whole((count, 2)),
        ),
        scratch_shapes=[pltpu.VMEM((2 * count, features), BF), pltpu.VMEM((8, count), F32)],
        compiler_params=params(MB),
        cost_estimate=cost(2 * rows * 2 * count * features, 6 << 20),
    )(tokens, gain, blocks, weights, cot)


SHIFTS = (1, 3, 2)


def along_x(rows):
    return [lax.ppermute(rows, "x", [(i, (i + by) % 4) for i in range(4)]) for by in SHIFTS]


def line_step(by):
    pairs = []
    for x in range(4):
        for z in range(4):
            for y in range(4):
                at = lambda c, z, y: ((2 * x + c) * 4 + z % 4) * 4 + y % 4
                pairs.append((at(0, z, y), at(0, z, y + by)))
                pairs.append((at(1, z, y), at(1, z + by, y)))
    return pairs


def along_line(rows):
    return [lax.ppermute(rows, ALL, line_step(by)) for by in SHIFTS]


def line_place():
    return jnp.where(lax.axis_index("core") == 0, lax.axis_index("y"), lax.axis_index("z")).astype(jnp.int32)


def assemble_kernel(at_ref, w_ref, *refs):
    part, line, out_ref = refs[:3], refs[3:6], refs[6]
    width = w_ref.shape[1]
    count = part[0].shape[0]
    me = at_ref[0]
    out_ref[0] = w_ref[...]
    rows = pl.ds(pl.multiple_of(me * count, count), count)
    for k in range(3):
        out_ref[k + 1, rows, :] = part[k][...]
    for other, by in zip(line, SHIFTS):
        rows = pl.ds(pl.multiple_of(lax.rem(me + 4 - by, 4) * count, count), count)
        for k in range(3):
            out_ref[k + 1, rows, :] = other[:, k * width : (k + 1) * width]


def assemble(place, weight, part, line):
    features, width = weight.shape
    arrays = [weight, *part, *line]
    return pl.pallas_call(
        assemble_kernel,
        out_shape=jax.ShapeDtypeStruct((4, features, width), BF),
        in_specs=[pl.BlockSpec(memory_space=pltpu.SMEM)]
        + [pl.BlockSpec(memory_space=pltpu.VMEM)] * len(arrays),
        out_specs=pl.BlockSpec(memory_space=pltpu.VMEM),
        compiler_params=params(24),
        cost_estimate=cost(1, HINT),
    )(place.reshape(1), *arrays)


def slice_at(step, at):
    turn = jnp.where(step % 4 == 0, 0, jnp.where(step % 4 == 1, 3, step % 4 - 1))
    return 2 * ((at[0] + turn) % 4) + jnp.where(step < 4, at[1], 1 - at[1])


def fold_kernel(at_ref, own_ref, sib_ref, val_ref, out_ref, vt_ref, left_ref):
    half, _, width = own_ref.shape
    tile = 256

    @pl.when(pl.program_id(0) == 0)
    def _():
        for a in range(2 * half):
            turn = (0, 3, 1, 2)[a % half]
            parity = at_ref[1] if a < half else 1 - at_ref[1]
            column = 2 * lax.rem(at_ref[0] + turn, 4) + parity
            at = pl.ds(pl.multiple_of(column * width, width), width)
            vt_ref[a * width : (a + 1) * width, :] = val_ref[:, at].T

    for a in range(half):
        left_ref[:, a * width : (a + 1) * width] = own_ref[a]
        left_ref[:, (half + a) * width : (half + a + 1) * width] = sib_ref[a]
    for i in range(0, out_ref.shape[1], tile):
        at = slice(i, i + tile)
        out_ref[:, at] = nn(left_ref[...], vt_ref[:, at]).astype(BF)


def fold_weight(at, own, sib, values):
    value_rows, features = values.shape
    half, _, width = own.shape
    steps = 4
    rows = features // steps
    block = pl.BlockSpec((half, rows, width), lambda i, at: (0, i, 0))
    return pl.pallas_call(
        fold_kernel,
        out_shape=jax.ShapeDtypeStruct((features, value_rows), BF),
        grid_spec=pltpu.PrefetchScalarGridSpec(
            num_scalar_prefetch=1,
            grid=(steps,),
            in_specs=[block, block, whole(values.shape)],
            out_specs=pl.BlockSpec((rows, value_rows), lambda i, at: (i, 0)),
            scratch_shapes=[pltpu.VMEM((features, value_rows), BF), pltpu.VMEM((rows, features), BF)],
        ),
        compiler_params=params(MB),
        cost_estimate=cost(1, 1),
    )(at, own, sib, values)


def serve_kernel(scale, x_hbm, fold_hbm, val_hbm, y_hbm, n_hbm, c_hbm, g_hbm, s_hbm,
                 x_buf, fold_buf, val_buf, n_buf, c_buf, id_buf, g_buf, s_buf, y_buf,
                 x_sem, f_sem, v_sem, y_sem, o_sem):
    rows = x_buf.shape[0]
    features = n_buf.shape[1]
    value_rows = val_buf.shape[0]
    parts = x_sem.shape[0]
    step_rows = rows // parts
    step_cols = value_rows // parts
    slots = rows // 2

    def x_copy(i):
        at = pl.ds(i * step_rows, step_rows)
        return pltpu.make_async_copy(x_hbm.at[at, :], x_buf.at[at, :], x_sem.at[i])

    def f_copy(i):
        return pltpu.make_async_copy(
            fold_hbm.at[:, pl.ds(i * step_cols, step_cols)], fold_buf.at[i], f_sem.at[i]
        )

    def v_copy(i):
        at = pl.ds(i * step_cols, step_cols)
        return pltpu.make_async_copy(val_hbm.at[at, :], val_buf.at[at, :], v_sem.at[i])

    for i in range(parts):
        x_copy(i).start()
    for i in range(parts):
        f_copy(i).start()
        v_copy(i).start()

    take = 32
    low = lax.broadcasted_iota(jnp.int32, (take // 16, 8, 1), 1) < SLOTS

    def split(x):
        pairs = x.astype(F32).reshape(take // 16, 16, x.shape[1])
        first, second = pairs[:, :8], pairs[:, 8:]
        upper = jnp.where(low, first, pltpu.roll(second, 4, 1))
        lower = jnp.where(low, pltpu.roll(first, 4, 1), second)
        return upper.reshape(take // 2, x.shape[1]), lower.reshape(take // 2, x.shape[1])

    for i in range(parts):
        x_copy(i).wait()

        @pl.loop(i * step_rows // take, (i + 1) * step_rows // take)
        def _(r):
            src = pl.ds(pl.multiple_of(r * take, take), take)
            dst = pl.ds(pl.multiple_of(r * (take // 2), take // 2), take // 2)
            upper, lower = split(x_buf[src, :features])
            n_buf[dst, :] = upper.astype(BF)
            c_buf[dst, :] = lower.astype(BF)
            ident, _ = split(x_buf[src, features:])
            id_buf[dst, :] = ident

    kept = [pltpu.make_async_copy(n_buf, n_hbm, o_sem.at[0]), pltpu.make_async_copy(c_buf, c_hbm, o_sem.at[1])]
    for copy in kept:
        copy.start()

    for j in range(parts):
        f_copy(j).wait()
        v_copy(j).wait()
        scores = nn(n_buf[...], fold_buf[j]) * scale
        cot_scores = nt(c_buf[...], val_buf[j * step_cols : (j + 1) * step_cols, :])
        sig = 1.0 / (1.0 + jnp.exp(-scores))
        block_of = (lax.broadcasted_iota(jnp.int32, (1, step_cols), 1) // BLOCK + j * (step_cols // BLOCK)).astype(F32)
        mine = id_buf[:, :1] == block_of
        g_buf[j] = jnp.where(mine, sig, 0.0).astype(BF)
        s_buf[j] = jnp.where(mine, cot_scores * sig * (1.0 - sig) * scale, 0.0).astype(BF)
        at = pl.ds(j * step_cols, step_cols)
        kept.append(pltpu.make_async_copy(g_buf.at[j], g_hbm.at[:, at], o_sem.at[2 + j]))
        kept.append(pltpu.make_async_copy(s_buf.at[j], s_hbm.at[:, at], o_sem.at[2 + parts + j]))
        kept[-2].start()
        kept[-1].start()

    tiles = y_sem.shape[0]
    width = features // tiles
    lows = lax.broadcasted_iota(jnp.int32, (slots // 8, 8, 1), 1) < SLOTS

    def y_copy(i):
        at = pl.ds(pl.multiple_of(i * width, width), width)
        return pltpu.make_async_copy(y_buf.at[i], y_hbm.at[:, at], y_sem.at[i])

    @pl.loop(0, tiles)
    def _(i):
        at = pl.ds(pl.multiple_of(i * width, width), width)
        read = nn(g_buf[0], val_buf[0:step_cols, at])
        grad = nt(s_buf[0], fold_buf[0, at, :])
        for j in range(1, parts):
            read += nn(g_buf[j], val_buf[j * step_cols : (j + 1) * step_cols, at])
            grad += nt(s_buf[j], fold_buf[j, at, :])
        read = read.reshape(slots // 8, 8, width)
        grad = grad.reshape(slots // 8, 8, width)
        first = jnp.where(lows, read, pltpu.roll(grad, 4, 1))
        second = jnp.where(lows, pltpu.roll(read, 4, 1), grad)
        y_buf[i] = jnp.concatenate([first, second], axis=1).reshape(rows, width).astype(BF)
        y_copy(i).start()

    for copy in kept:
        copy.wait()
    for i in range(tiles):
        y_copy(i).wait()


def serve(x, fold, values, features):
    rows = x.shape[0]
    slots = rows // 2
    value_rows = values.shape[0]
    parts, tiles = 4, 8
    step_cols = value_rows // parts
    any_spec = pl.BlockSpec(memory_space=pl.ANY)
    return pl.pallas_call(
        functools.partial(serve_kernel, float(features) ** (-0.5)),
        out_shape=(
            jax.ShapeDtypeStruct((rows, features), BF),
            jax.ShapeDtypeStruct((slots, features), BF),
            jax.ShapeDtypeStruct((slots, features), BF),
            jax.ShapeDtypeStruct((slots, value_rows), BF),
            jax.ShapeDtypeStruct((slots, value_rows), BF),
        ),
        in_specs=[any_spec] * 3,
        out_specs=(any_spec,) * 5,
        scratch_shapes=[
            pltpu.VMEM(x.shape, BF),
            pltpu.VMEM((parts, features, step_cols), BF),
            pltpu.VMEM(values.shape, BF),
            pltpu.VMEM((slots, features), BF),
            pltpu.VMEM((slots, features), BF),
            pltpu.VMEM((slots, LANES), F32),
            pltpu.VMEM((parts, slots, step_cols), BF),
            pltpu.VMEM((parts, slots, step_cols), BF),
            pltpu.VMEM((tiles, rows, features // tiles), BF),
            pltpu.SemaphoreType.DMA((parts,)),
            pltpu.SemaphoreType.DMA((parts,)),
            pltpu.SemaphoreType.DMA((parts,)),
            pltpu.SemaphoreType.DMA((tiles,)),
            pltpu.SemaphoreType.DMA((2 + 2 * parts,)),
        ],
        compiler_params=params(MB),
        cost_estimate=cost(4 * rows * value_rows * features, 20 << 20),
    )(x, fold, values)


def grad_kernel(at_ref, own_ref, sib_ref, n_ref, c_ref, g_ref, s_ref, out_ref, gt_ref, st_ref):
    slots = n_ref.shape[0]
    tile = 256

    @pl.when(pl.program_id(0) == 0)
    def _():
        for i in range(0, slots, tile):
            gt_ref[:, i : i + tile] = g_ref[i : i + tile, :].T
            st_ref[:, i : i + tile] = s_ref[i : i + tile, :].T

    weight = jnp.where(pl.program_id(0) < 4, own_ref[0], sib_ref[0])
    queries = nn(n_ref[...], weight).astype(BF)
    for i in range(0, out_ref.shape[0], tile):
        total = nn(gt_ref[i : i + tile, :], c_ref[...]) + nn(st_ref[i : i + tile, :], queries)
        out_ref[i : i + tile, :] = total.astype(BF)


def value_grads(at, own, sib, n, c, g, s):
    half, features, width = own.shape
    slots, value_rows = g.shape
    return pl.pallas_call(
        grad_kernel,
        out_shape=jax.ShapeDtypeStruct((value_rows, features), BF),
        grid_spec=pltpu.PrefetchScalarGridSpec(
            num_scalar_prefetch=1,
            grid=(2 * half,),
            in_specs=[
                pl.BlockSpec((1, features, width), lambda a, x: (jnp.minimum(a, half - 1), 0, 0)),
                pl.BlockSpec((1, features, width), lambda a, x: (jnp.maximum(a - half, 0), 0, 0)),
                whole(n.shape),
                pl.BlockSpec((slots, width), lambda a, x: (0, slice_at(a, x))),
                whole(g.shape),
                whole(s.shape),
            ],
            out_specs=pl.BlockSpec((value_rows, width), lambda a, x: (0, slice_at(a, x))),
            scratch_shapes=[pltpu.VMEM((value_rows, slots), BF), pltpu.VMEM((value_rows, slots), BF)],
        ),
        compiler_params=params(MB),
        cost_estimate=cost(6 * slots * value_rows * features, 24 << 20),
    )(at, own, sib, n, c, g, s)


def home_kernel(back_ref, tgt_ref, wgt_ref, tok_ref, cot_ref, gain_ref, out_ref, grad_ref, pick_ref, acc_ref, rms_ref, sum_ref):
    step = pl.program_id(0)
    count, features = tok_ref.shape
    rows, width = back_ref.shape

    @pl.when(step == 0)
    def _():
        number = lax.broadcasted_iota(jnp.int32, (count, rows), 1)
        targets = tgt_ref[...]
        t0, t1 = targets[:, :1], targets[:, 1:]
        one = lambda hit: jnp.where(hit, 1.0, 0.0).astype(BF)
        pick_ref[:count, :] = one(number == t0)
        pick_ref[count : 2 * count, :] = one(number == t1)
        pick_ref[2 * count :, :] = one((number == t0 + SLOTS) | (number == t1 + SLOTS))
        exact = tok_ref[...].astype(F32)
        rms_ref[...] = lax.rsqrt(jnp.mean(exact * exact, axis=1, keepdims=True) + 1e-06)
        sum_ref[...] = jnp.zeros_like(sum_ref)

    at = pl.ds(pl.multiple_of(step * width, width), width)
    weights = wgt_ref[...]
    got = nn(pick_ref[...], back_ref[...])
    exact = tok_ref[:, at].astype(F32)
    out_ref[...] = exact + (weights[:, :1] * got[:count] + weights[:, 1:] * got[count : 2 * count])
    unit_grad = got[2 * count :] * gain_ref[:, at]
    acc_ref[:, at] = unit_grad
    rms = rms_ref[...]
    sum_ref[...] += jnp.sum(unit_grad * (exact * rms), axis=1, keepdims=True)

    @pl.when(step == pl.num_programs(0) - 1)
    def _():
        mean = sum_ref[...] * (1.0 / features)
        for i in range(0, features, width):
            cols = slice(i, i + width)
            unit = tok_ref[:, cols].astype(F32) * rms
            grad_ref[:, cols] = cot_ref[:, cols].astype(F32) + rms * (acc_ref[:, cols] - unit * mean)


def finish(back, targets, weights, tokens, cot, gain):
    count, features = tokens.shape
    rows = back.shape[0]
    steps = 4
    width = features // steps
    return pl.pallas_call(
        home_kernel,
        out_shape=(
            jax.ShapeDtypeStruct((count, features), F32),
            jax.ShapeDtypeStruct((count, features), F32),
        ),
        grid=(steps,),
        in_specs=[
            pl.BlockSpec((rows, width), lambda i: (0, i)),
            whole((count, 2)),
            whole((count, 2)),
            whole(tokens.shape),
            whole(cot.shape),
            whole((1, features)),
        ],
        out_specs=(pl.BlockSpec((count, width), lambda i: (0, i)), whole((count, features))),
        scratch_shapes=[
            pltpu.VMEM((3 * count, rows), BF),
            pltpu.VMEM((count, features), F32),
            pltpu.VMEM((count, 1), F32),
            pltpu.VMEM((count, 1), F32),
        ],
        compiler_params=params(MB),
        cost_estimate=cost(6 * count * rows * features, 10 << 20),
    )(back, targets, weights, tokens, cot, gain)


def exchange(rows):
    return lax.all_to_all(rows, ALL, split_axis=0, concat_axis=0, tiled=True)


def body(tokens, norm_gain, query_weight, values, blocks, weights, out_cotangent):
    features = tokens.shape[1]
    owners = lax.axis_size(ALL)
    at = jnp.stack([lax.axis_index("x"), lax.axis_index("core")]).astype(jnp.int32)
    gain = norm_gain.reshape(1, features)
    place = line_place()
    quarter = features // 4
    part = along_x(lax.dynamic_slice_in_dim(query_weight, place * quarter, quarter, axis=0))
    payload, targets = build_payload(
        tokens, gain, blocks, weights, out_cotangent, owners, values.shape[0] // BLOCK
    )
    joined = jnp.concatenate(part, axis=1)
    joined, payload = lax.optimization_barrier((joined, payload))
    own = assemble(place, query_weight, part, along_line(joined))
    sib = lax.ppermute(own, "core", [(0, 1), (1, 0)])
    got = exchange(payload)
    fold = fold_weight(at, own, sib, values)
    answers, n, c, g, s = serve(got, fold, values, features)
    back = exchange(answers)
    grad_values = value_grads(at, own, sib, n, c, g, s)
    layer_out, grad_tokens = finish(back, targets, weights, tokens, out_cotangent, gain)
    return layer_out, grad_tokens, grad_values


def solution(mesh):
    fine = Mesh(np.asarray(mesh.devices).reshape(4, 2, 4, 4), ALL)
    rows = P(ALL, None)
    return jax.shard_map(
        body,
        mesh=fine,
        in_specs=(rows, P(), P(None, ("x", "core")), rows, rows, rows, rows),
        out_specs=(rows, rows, rows),
        check_vma=False,
    )
```

```python
import functools

import jax
import jax.numpy as jnp
import numpy as np
from jax import lax
from jax.experimental import pallas as pl
from jax.experimental.pallas import tpu as pltpu
from jax.sharding import Mesh
from jax.sharding import PartitionSpec as P

BLOCK = 64
SLOTS = 4
CHUNK = 2 * SLOTS
LANES = 128
ALL = ("x", "core", "z", "y")
BF = jnp.bfloat16
F32 = jnp.float32
MB = 60


def params(megabytes):
    return pltpu.CompilerParams(vmem_limit_bytes=megabytes << 20)


def cost(flops, bytes_accessed):
    return pl.CostEstimate(
        flops=int(flops), bytes_accessed=int(bytes_accessed), transcendentals=0
    )


def whole(shape):
    return pl.BlockSpec(shape, lambda *_: (0,) * len(shape))


def nt(left, right):
    return lax.dot_general(left, right, (((1,), (1,)), ((), ())), preferred_element_type=F32)


def nn(left, right):
    return jnp.dot(left, right, preferred_element_type=F32)


def send_kernel(span, tok_ref, gain_ref, blk_ref, wgt_ref, cot_ref, x_ref, tgt_ref, rows_ref, route_ref):
    step = pl.program_id(0)
    count, features = tok_ref.shape
    step_rows = x_ref.shape[0]

    @pl.when(step == 0)
    def _():
        exact = tok_ref[...].astype(F32)
        rms = lax.rsqrt(jnp.mean(exact * exact, axis=1, keepdims=True) + 1e-06)
        rows_ref[:count, :] = ((exact * rms) * gain_ref[...]).astype(BF)
        rows_ref[count:, :] = cot_ref[...]
        square = (count, count)
        sub = lax.broadcasted_iota(jnp.int32, square, 0)
        lane = lax.broadcasted_iota(jnp.int32, square, 1)
        blocks = blk_ref[...]
        weights = wgt_ref[...]
        col = [jnp.broadcast_to(blocks[:, k : k + 1], square) for k in range(2)]
        row = [c.astype(F32).T.astype(jnp.int32) for c in col]
        wrow = [jnp.broadcast_to(weights[:, k : k + 1], square).T for k in range(2)]
        own_col = [c // span for c in col]
        own_row = [r // span for r in row]
        one = lambda hit: jnp.where(hit, 1, 0)
        before = [
            [one((own_col[0] == own_row[0]) & (sub < lane))],
            [one(own_col[0] == own_row[1]), one((own_col[1] == own_row[1]) & (sub < lane))],
        ]
        before_t = [
            [one((own_row[0] == own_col[0]) & (lane < sub))],
            [one(own_row[0] == own_col[1]), one((own_row[1] == own_col[1]) & (lane < sub))],
        ]
        for k in range(2):
            slot_row = sum(jnp.sum(e, axis=0, keepdims=True) for e in before[k])
            slot_col = sum(jnp.sum(e, axis=1, keepdims=True) for e in before_t[k])
            target = own_row[k][:1, :] * CHUNK + slot_row
            route_ref[k : k + 1, :] = target.astype(F32)
            route_ref[2 + k : 3 + k, :] = (row[k][:1, :] % span).astype(F32) + 1.0
            route_ref[4 + k : 5 + k, :] = wrow[k][:1, :]
            tgt_ref[:, k : k + 1] = own_col[k][:, :1] * CHUNK + slot_col

    route = route_ref[...]
    shape = (step_rows, count)
    number = (lax.broadcasted_iota(jnp.int32, shape, 0) + step * step_rows).astype(F32)
    t0, t1 = route[0:1, :], route[1:2, :]
    n0, n1 = number == t0, number == t1
    c0, c1 = number == t0 + SLOTS, number == t1 + SLOTS
    scale = jnp.sum(jnp.where(c0, route[4:5, :], 0.0) + jnp.where(c1, route[5:6, :], 0.0), axis=1, keepdims=True)
    ident = jnp.sum(
        jnp.where(n0 | c0, route[2:3, :], 0.0) + jnp.where(n1 | c1, route[3:4, :], 0.0),
        axis=1,
        keepdims=True,
    )
    is_cot = (lax.broadcasted_iota(jnp.int32, (step_rows, 1), 0) % CHUNK) >= SLOTS
    scale = jnp.where(is_cot, scale, 1.0)
    pick = jnp.concatenate(
        [jnp.where(n0 | n1, 1.0, 0.0), jnp.where(c0 | c1, 1.0, 0.0)], axis=1
    ).astype(BF)
    width = 512
    for at in range(0, features, width):
        rows = nn(pick, rows_ref[:, at : at + width])
        x_ref[:, at : at + width] = (rows * scale).astype(BF)
    x_ref[:, features:] = jnp.broadcast_to(ident - 1.0, (step_rows, LANES)).astype(BF)


def build_payload(tokens, gain, blocks, weights, cot, owners, span):
    count, features = tokens.shape
    rows = owners * CHUNK
    steps = 4
    return pl.pallas_call(
        functools.partial(send_kernel, span),
        out_shape=(
            jax.ShapeDtypeStruct((rows, features + LANES), BF),
            jax.ShapeDtypeStruct((count, 2), jnp.int32),
        ),
        grid=(steps,),
        in_specs=[
            whole((count, features)),
            whole((1, features)),
            whole((count, 2)),
            whole((count, 2)),
            whole((count, features)),
        ],
        out_specs=(
            pl.BlockSpec((rows // steps, features + LANES), lambda i: (i, 0)),
            whole((count, 2)),
        ),
        scratch_shapes=[pltpu.VMEM((2 * count, features), BF), pltpu.VMEM((8, count), F32)],
        compiler_params=params(MB),
        cost_estimate=cost(2 * rows * 2 * count * features, 6 << 20),
    )(tokens, gain, blocks, weights, cot)


def turn(rows, by):
    return lax.ppermute(rows, "x", [(i, (i + by) % 4) for i in range(4)])


def gather_weight(weight, before, after):
    half = weight.shape[0] // 2
    across = jnp.concatenate([turn(before[:half], 1), turn(after[half:], -1)], axis=0)
    own = jnp.stack([weight, before, after, across])
    return own, lax.ppermute(own, "core", [(0, 1), (1, 0)])


def slice_at(step, at):
    turn = jnp.where(step % 4 == 0, 0, jnp.where(step % 4 == 1, 3, step % 4 - 1))
    return 2 * ((at[0] + turn) % 4) + jnp.where(step < 4, at[1], 1 - at[1])


def fold_kernel(at_ref, own_ref, sib_ref, val_ref, out_ref, vt_ref, left_ref):
    half, _, width = own_ref.shape
    tile = 256

    @pl.when(pl.program_id(0) == 0)
    def _():
        for a in range(2 * half):
            turn = (0, 3, 1, 2)[a % half]
            parity = at_ref[1] if a < half else 1 - at_ref[1]
            column = 2 * lax.rem(at_ref[0] + turn, 4) + parity
            at = pl.ds(pl.multiple_of(column * width, width), width)
            vt_ref[a * width : (a + 1) * width, :] = val_ref[:, at].T

    for a in range(half):
        left_ref[:, a * width : (a + 1) * width] = own_ref[a]
        left_ref[:, (half + a) * width : (half + a + 1) * width] = sib_ref[a]
    for i in range(0, out_ref.shape[1], tile):
        at = slice(i, i + tile)
        out_ref[:, at] = nn(left_ref[...], vt_ref[:, at]).astype(BF)


def fold_weight(at, own, sib, values):
    value_rows, features = values.shape
    half, _, width = own.shape
    steps = 4
    rows = features // steps
    block = pl.BlockSpec((half, rows, width), lambda i, at: (0, i, 0))
    return pl.pallas_call(
        fold_kernel,
        out_shape=jax.ShapeDtypeStruct((features, value_rows), BF),
        grid_spec=pltpu.PrefetchScalarGridSpec(
            num_scalar_prefetch=1,
            grid=(steps,),
            in_specs=[block, block, whole(values.shape)],
            out_specs=pl.BlockSpec((rows, value_rows), lambda i, at: (i, 0)),
            scratch_shapes=[pltpu.VMEM((features, value_rows), BF), pltpu.VMEM((rows, features), BF)],
        ),
        compiler_params=params(MB),
        cost_estimate=cost(1, 1),
    )(at, own, sib, values)


def serve_kernel(scale, x_hbm, fold_hbm, val_hbm, y_hbm, n_hbm, c_hbm, g_hbm, s_hbm,
                 x_buf, fold_buf, val_buf, n_buf, c_buf, id_buf, g_buf, s_buf, y_buf, score_buf, cot_buf,
                 x_sem, f_sem, v_sem, y_sem, o_sem):
    rows = x_buf.shape[0]
    features = n_buf.shape[1]
    value_rows = val_buf.shape[0]
    parts = x_sem.shape[0]
    step_rows = rows // parts
    step_cols = value_rows // parts
    slots = rows // 2

    def x_copy(i):
        at = pl.ds(i * step_rows, step_rows)
        return pltpu.make_async_copy(x_hbm.at[at, :], x_buf.at[at, :], x_sem.at[i])

    def f_copy(i):
        return pltpu.make_async_copy(
            fold_hbm.at[:, pl.ds(i * step_cols, step_cols)], fold_buf.at[i], f_sem.at[i]
        )

    def v_copy(i):
        at = pl.ds(i * step_cols, step_cols)
        return pltpu.make_async_copy(val_hbm.at[at, :], val_buf.at[at, :], v_sem.at[i])

    for i in range(parts):
        x_copy(i).start()
    def load(i):
        if i < parts:
            f_copy(i).start()
            v_copy(i).start()

    take = 32
    low = lax.broadcasted_iota(jnp.int32, (take // 16, 8, 1), 1) < SLOTS

    def split(x):
        pairs = x.astype(F32).reshape(take // 16, 16, x.shape[1])
        first, second = pairs[:, :8], pairs[:, 8:]
        upper = jnp.where(low, first, pltpu.roll(second, 4, 1))
        lower = jnp.where(low, pltpu.roll(first, 4, 1), second)
        return upper.reshape(take // 2, x.shape[1]), lower.reshape(take // 2, x.shape[1])

    for i in range(parts):
        x_copy(i).wait()
        if i == parts - 2:
            load(0)

        @pl.loop(i * step_rows // take, (i + 1) * step_rows // take)
        def _(r):
            src = pl.ds(pl.multiple_of(r * take, take), take)
            dst = pl.ds(pl.multiple_of(r * (take // 2), take // 2), take // 2)
            upper, lower = split(x_buf[src, :features])
            n_buf[dst, :] = upper.astype(BF)
            c_buf[dst, :] = lower.astype(BF)
            ident, _ = split(x_buf[src, features:])
            id_buf[dst, :] = ident

    kept = [pltpu.make_async_copy(n_buf, n_hbm, o_sem.at[0]), pltpu.make_async_copy(c_buf, c_hbm, o_sem.at[1])]
    def products(j):
        f_copy(j).wait()
        v_copy(j).wait()
        load(j + 1)
        score_buf[j % 2] = nn(n_buf[...], fold_buf[j])
        cot_buf[j % 2] = nt(c_buf[...], val_buf[j * step_cols : (j + 1) * step_cols, :])

    def gate(j):
        block_of = (lax.broadcasted_iota(jnp.int32, (1, step_cols), 1) // BLOCK + j * (step_cols // BLOCK)).astype(F32)
        mine = id_buf[:, :1] == block_of
        sig = 1.0 / (1.0 + jnp.exp(score_buf[j % 2] * -scale))
        g_buf[j] = jnp.where(mine, sig, 0.0).astype(BF)
        s_buf[j] = jnp.where(mine, cot_buf[j % 2] * sig * (1.0 - sig) * scale, 0.0).astype(BF)

    products(0)
    for j in range(parts):
        if j + 1 < parts:
            products(j + 1)
        gate(j)
    for copy in kept:
        copy.start()
    for j in range(parts):
        at = pl.ds(j * step_cols, step_cols)
        kept.append(pltpu.make_async_copy(g_buf.at[j], g_hbm.at[:, at], o_sem.at[2 + j]))
        kept.append(pltpu.make_async_copy(s_buf.at[j], s_hbm.at[:, at], o_sem.at[2 + parts + j]))
        kept[-2].start()
        kept[-1].start()

    tiles = y_sem.shape[0]
    width = features // tiles
    lows = lax.broadcasted_iota(jnp.int32, (slots // 8, 8, 1), 1) < SLOTS

    def y_copy(i):
        at = pl.ds(pl.multiple_of(i * width, width), width)
        return pltpu.make_async_copy(y_buf.at[i], y_hbm.at[:, at], y_sem.at[i])

    @pl.loop(0, tiles)
    def _(i):
        at = pl.ds(pl.multiple_of(i * width, width), width)
        read = nn(g_buf[0], val_buf[0:step_cols, at])
        grad = nt(s_buf[0], fold_buf[0, at, :])
        for j in range(1, parts):
            read += nn(g_buf[j], val_buf[j * step_cols : (j + 1) * step_cols, at])
            grad += nt(s_buf[j], fold_buf[j, at, :])
        read = read.reshape(slots // 8, 8, width)
        grad = grad.reshape(slots // 8, 8, width)
        first = jnp.where(lows, read, pltpu.roll(grad, 4, 1))
        second = jnp.where(lows, pltpu.roll(read, 4, 1), grad)
        y_buf[i] = jnp.concatenate([first, second], axis=1).reshape(rows, width).astype(BF)
        y_copy(i).start()

    for copy in kept:
        copy.wait()
    for i in range(tiles):
        y_copy(i).wait()


def serve(x, fold, values, features):
    rows = x.shape[0]
    slots = rows // 2
    value_rows = values.shape[0]
    parts, tiles = 4, 4
    step_cols = value_rows // parts
    any_spec = pl.BlockSpec(memory_space=pl.ANY)
    return pl.pallas_call(
        functools.partial(serve_kernel, float(features) ** (-0.5)),
        out_shape=(
            jax.ShapeDtypeStruct((rows, features), BF),
            jax.ShapeDtypeStruct((slots, features), BF),
            jax.ShapeDtypeStruct((slots, features), BF),
            jax.ShapeDtypeStruct((slots, value_rows), BF),
            jax.ShapeDtypeStruct((slots, value_rows), BF),
        ),
        in_specs=[any_spec] * 3,
        out_specs=(any_spec,) * 5,
        scratch_shapes=[
            pltpu.VMEM(x.shape, BF),
            pltpu.VMEM((parts, features, step_cols), BF),
            pltpu.VMEM(values.shape, BF),
            pltpu.VMEM((slots, features), BF),
            pltpu.VMEM((slots, features), BF),
            pltpu.VMEM((slots, LANES), F32),
            pltpu.VMEM((parts, slots, step_cols), BF),
            pltpu.VMEM((parts, slots, step_cols), BF),
            pltpu.VMEM((tiles, rows, features // tiles), BF),
            pltpu.VMEM((2, slots, step_cols), F32),
            pltpu.VMEM((2, slots, step_cols), F32),
            pltpu.SemaphoreType.DMA((parts,)),
            pltpu.SemaphoreType.DMA((parts,)),
            pltpu.SemaphoreType.DMA((parts,)),
            pltpu.SemaphoreType.DMA((tiles,)),
            pltpu.SemaphoreType.DMA((2 + 2 * parts,)),
        ],
        compiler_params=params(MB),
        cost_estimate=cost(4 * rows * value_rows * features, 20 << 20),
    )(x, fold, values)


def grad_kernel(at_ref, own_ref, sib_ref, n_ref, c_ref, g_ref, s_ref, out_ref, gt_ref, st_ref):
    slots = n_ref.shape[0]
    tile = 256

    @pl.when(pl.program_id(0) == 0)
    def _():
        for i in range(0, slots, tile):
            gt_ref[:, i : i + tile] = g_ref[i : i + tile, :].T
            st_ref[:, i : i + tile] = s_ref[i : i + tile, :].T

    weight = jnp.where(pl.program_id(0) < 4, own_ref[0], sib_ref[0])
    queries = nn(n_ref[...], weight).astype(BF)
    for i in range(0, out_ref.shape[0], tile):
        total = nn(gt_ref[i : i + tile, :], c_ref[...]) + nn(st_ref[i : i + tile, :], queries)
        out_ref[i : i + tile, :] = total.astype(BF)


def value_grads(at, own, sib, n, c, g, s):
    half, features, width = own.shape
    slots, value_rows = g.shape
    return pl.pallas_call(
        grad_kernel,
        out_shape=jax.ShapeDtypeStruct((value_rows, features), BF),
        grid_spec=pltpu.PrefetchScalarGridSpec(
            num_scalar_prefetch=1,
            grid=(2 * half,),
            in_specs=[
                pl.BlockSpec((1, features, width), lambda a, x: (jnp.minimum(a, half - 1), 0, 0)),
                pl.BlockSpec((1, features, width), lambda a, x: (jnp.maximum(a - half, 0), 0, 0)),
                whole(n.shape),
                pl.BlockSpec((slots, width), lambda a, x: (0, slice_at(a, x))),
                whole(g.shape),
                whole(s.shape),
            ],
            out_specs=pl.BlockSpec((value_rows, width), lambda a, x: (0, slice_at(a, x))),
            scratch_shapes=[pltpu.VMEM((value_rows, slots), BF), pltpu.VMEM((value_rows, slots), BF)],
        ),
        compiler_params=params(MB),
        cost_estimate=cost(6 * slots * value_rows * features, 24 << 20),
    )(at, own, sib, n, c, g, s)


def home_kernel(back_ref, tgt_ref, wgt_ref, tok_ref, cot_ref, gain_ref, out_ref, grad_ref, pick_ref, acc_ref, rms_ref, sum_ref):
    step = pl.program_id(0)
    count, features = tok_ref.shape
    rows, width = back_ref.shape

    @pl.when(step == 0)
    def _():
        number = lax.broadcasted_iota(jnp.int32, (count, rows), 1)
        targets = tgt_ref[...]
        t0, t1 = targets[:, :1], targets[:, 1:]
        one = lambda hit: jnp.where(hit, 1.0, 0.0).astype(BF)
        pick_ref[:count, :] = one(number == t0)
        pick_ref[count : 2 * count, :] = one(number == t1)
        pick_ref[2 * count :, :] = one((number == t0 + SLOTS) | (number == t1 + SLOTS))
        exact = tok_ref[...].astype(F32)
        rms_ref[...] = lax.rsqrt(jnp.mean(exact * exact, axis=1, keepdims=True) + 1e-06)
        sum_ref[...] = jnp.zeros_like(sum_ref)

    at = pl.ds(pl.multiple_of(step * width, width), width)
    weights = wgt_ref[...]
    got = nn(pick_ref[...], back_ref[...])
    exact = tok_ref[:, at].astype(F32)
    out_ref[...] = exact + (weights[:, :1] * got[:count] + weights[:, 1:] * got[count : 2 * count])
    unit_grad = got[2 * count :] * gain_ref[:, at]
    acc_ref[:, at] = unit_grad
    rms = rms_ref[...]
    sum_ref[...] += jnp.sum(unit_grad * (exact * rms), axis=1, keepdims=True)

    @pl.when(step == pl.num_programs(0) - 1)
    def _():
        mean = sum_ref[...] * (1.0 / features)
        for i in range(0, features, width):
            cols = slice(i, i + width)
            unit = tok_ref[:, cols].astype(F32) * rms
            grad_ref[:, cols] = cot_ref[:, cols].astype(F32) + rms * (acc_ref[:, cols] - unit * mean)


def finish(back, targets, weights, tokens, cot, gain):
    count, features = tokens.shape
    rows = back.shape[0]
    steps = 4
    width = features // steps
    return pl.pallas_call(
        home_kernel,
        out_shape=(
            jax.ShapeDtypeStruct((count, features), F32),
            jax.ShapeDtypeStruct((count, features), F32),
        ),
        grid=(steps,),
        in_specs=[
            pl.BlockSpec((rows, width), lambda i: (0, i)),
            whole((count, 2)),
            whole((count, 2)),
            whole(tokens.shape),
            whole(cot.shape),
            whole((1, features)),
        ],
        out_specs=(pl.BlockSpec((count, width), lambda i: (0, i)), whole((count, features))),
        scratch_shapes=[
            pltpu.VMEM((3 * count, rows), BF),
            pltpu.VMEM((count, features), F32),
            pltpu.VMEM((count, 1), F32),
            pltpu.VMEM((count, 1), F32),
        ],
        compiler_params=params(MB),
        cost_estimate=cost(6 * count * rows * features, 10 << 20),
    )(back, targets, weights, tokens, cot, gain)


def exchange(rows):
    return lax.all_to_all(rows, ALL, split_axis=0, concat_axis=0, tiled=True)


def body(tokens, norm_gain, query_weight, values, blocks, weights, out_cotangent):
    features = tokens.shape[1]
    owners = lax.axis_size(ALL)
    at = jnp.stack([lax.axis_index("x"), lax.axis_index("core")]).astype(jnp.int32)
    gain = norm_gain.reshape(1, features)
    before, after = turn(query_weight, 1), turn(query_weight, -1)
    payload, targets = build_payload(
        tokens, gain, blocks, weights, out_cotangent, owners, values.shape[0] // BLOCK
    )
    before, after, payload = lax.optimization_barrier((before, after, payload))
    own, sib = gather_weight(query_weight, before, after)
    got = exchange(payload)
    fold = fold_weight(at, own, sib, values)
    answers, n, c, g, s = serve(got, fold, values, features)
    back = exchange(answers)
    grad_values = value_grads(at, own, sib, n, c, g, s)
    layer_out, grad_tokens = finish(back, targets, weights, tokens, out_cotangent, gain)
    return layer_out, grad_tokens, grad_values


def solution(mesh):
    fine = Mesh(np.asarray(mesh.devices).reshape(4, 2, 4, 4), ALL)
    rows = P(ALL, None)
    return jax.shard_map(
        body,
        mesh=fine,
        in_specs=(rows, P(), P(None, ("x", "core")), rows, rows, rows, rows),
        out_specs=(rows, rows, rows),
        check_vma=False,
    )
```

```python
import functools

import jax
import jax.numpy as jnp
import numpy as np
from jax import lax
from jax.experimental import pallas as pl
from jax.experimental.pallas import tpu as pltpu
from jax.sharding import Mesh
from jax.sharding import PartitionSpec as P

BLOCK = 64
SLOTS = 4
CHUNK = 2 * SLOTS
LANES = 128
ALL = ("x", "core", "z", "y")
BF = jnp.bfloat16
F32 = jnp.float32
MB = 60


def params(megabytes):
    return pltpu.CompilerParams(vmem_limit_bytes=megabytes << 20)


def cost(flops, bytes_accessed):
    return pl.CostEstimate(
        flops=int(flops), bytes_accessed=int(bytes_accessed), transcendentals=0
    )


def whole(shape):
    return pl.BlockSpec(shape, lambda *_: (0,) * len(shape))


def nt(left, right):
    return lax.dot_general(left, right, (((1,), (1,)), ((), ())), preferred_element_type=F32)


def nn(left, right):
    return jnp.dot(left, right, preferred_element_type=F32)


def send_kernel(span, tok_ref, gain_ref, blk_ref, wgt_ref, cot_ref, x_ref, tgt_ref, rows_ref, route_ref):
    step = pl.program_id(0)
    count, features = tok_ref.shape
    step_rows = x_ref.shape[0]

    @pl.when(step == 0)
    def _():
        exact = tok_ref[...].astype(F32)
        rms = lax.rsqrt(jnp.mean(exact * exact, axis=1, keepdims=True) + 1e-06)
        rows_ref[:count, :] = ((exact * rms) * gain_ref[...]).astype(BF)
        rows_ref[count:, :] = cot_ref[...]
        square = (count, count)
        sub = lax.broadcasted_iota(jnp.int32, square, 0)
        lane = lax.broadcasted_iota(jnp.int32, square, 1)
        blocks = blk_ref[...]
        weights = wgt_ref[...]
        col = [jnp.broadcast_to(blocks[:, k : k + 1], square) for k in range(2)]
        row = [c.astype(F32).T.astype(jnp.int32) for c in col]
        wrow = [jnp.broadcast_to(weights[:, k : k + 1], square).T for k in range(2)]
        own_col = [c // span for c in col]
        own_row = [r // span for r in row]
        one = lambda hit: jnp.where(hit, 1, 0)
        before = [
            [one((own_col[0] == own_row[0]) & (sub < lane))],
            [one(own_col[0] == own_row[1]), one((own_col[1] == own_row[1]) & (sub < lane))],
        ]
        before_t = [
            [one((own_row[0] == own_col[0]) & (lane < sub))],
            [one(own_row[0] == own_col[1]), one((own_row[1] == own_col[1]) & (lane < sub))],
        ]
        for k in range(2):
            slot_row = sum(jnp.sum(e, axis=0, keepdims=True) for e in before[k])
            slot_col = sum(jnp.sum(e, axis=1, keepdims=True) for e in before_t[k])
            target = own_row[k][:1, :] * CHUNK + slot_row
            route_ref[k : k + 1, :] = target.astype(F32)
            route_ref[2 + k : 3 + k, :] = (row[k][:1, :] % span).astype(F32) + 1.0
            route_ref[4 + k : 5 + k, :] = wrow[k][:1, :]
            tgt_ref[:, k : k + 1] = own_col[k][:, :1] * CHUNK + slot_col

    route = route_ref[...]
    shape = (step_rows, count)
    number = (lax.broadcasted_iota(jnp.int32, shape, 0) + step * step_rows).astype(F32)
    t0, t1 = route[0:1, :], route[1:2, :]
    n0, n1 = number == t0, number == t1
    c0, c1 = number == t0 + SLOTS, number == t1 + SLOTS
    scale = jnp.sum(jnp.where(c0, route[4:5, :], 0.0) + jnp.where(c1, route[5:6, :], 0.0), axis=1, keepdims=True)
    ident = jnp.sum(
        jnp.where(n0 | c0, route[2:3, :], 0.0) + jnp.where(n1 | c1, route[3:4, :], 0.0),
        axis=1,
        keepdims=True,
    )
    is_cot = (lax.broadcasted_iota(jnp.int32, (step_rows, 1), 0) % CHUNK) >= SLOTS
    scale = jnp.where(is_cot, scale, 1.0)
    pick = jnp.concatenate(
        [jnp.where(n0 | n1, 1.0, 0.0), jnp.where(c0 | c1, 1.0, 0.0)], axis=1
    ).astype(BF)
    width = 512
    for at in range(0, features, width):
        rows = nn(pick, rows_ref[:, at : at + width])
        x_ref[:, at : at + width] = (rows * scale).astype(BF)
    x_ref[:, features:] = jnp.broadcast_to(ident - 1.0, (step_rows, LANES)).astype(BF)


def build_payload(tokens, gain, blocks, weights, cot, owners, span):
    count, features = tokens.shape
    rows = owners * CHUNK
    steps = 4
    return pl.pallas_call(
        functools.partial(send_kernel, span),
        out_shape=(
            jax.ShapeDtypeStruct((rows, features + LANES), BF),
            jax.ShapeDtypeStruct((count, 2), jnp.int32),
        ),
        grid=(steps,),
        in_specs=[
            whole((count, features)),
            whole((1, features)),
            whole((count, 2)),
            whole((count, 2)),
            whole((count, features)),
        ],
        out_specs=(
            pl.BlockSpec((rows // steps, features + LANES), lambda i: (i, 0)),
            whole((count, 2)),
        ),
        scratch_shapes=[pltpu.VMEM((2 * count, features), BF), pltpu.VMEM((8, count), F32)],
        compiler_params=params(MB),
        cost_estimate=cost(2 * rows * 2 * count * features, 6 << 20),
    )(tokens, gain, blocks, weights, cot)


def turn(rows, by):
    return lax.ppermute(rows, "x", [(i, (i + by) % 4) for i in range(4)])


def gather_weight(weight, before, after):
    across = jnp.concatenate([turn(before[0], 1), turn(after[1], -1)], axis=0)
    own = jnp.stack([weight, jnp.concatenate(before, axis=0), jnp.concatenate(after, axis=0), across])
    return own, lax.ppermute(own, "core", [(0, 1), (1, 0)])


def slice_at(step, at):
    turn = jnp.where(step % 4 == 0, 0, jnp.where(step % 4 == 1, 3, step % 4 - 1))
    return 2 * ((at[0] + turn) % 4) + jnp.where(step < 4, at[1], 1 - at[1])


def fold_kernel(at_ref, own_ref, sib_ref, val_ref, out_ref, vt_ref, left_ref):
    half, _, width = own_ref.shape
    tile = 256

    @pl.when(pl.program_id(0) == 0)
    def _():
        for a in range(2 * half):
            turn = (0, 3, 1, 2)[a % half]
            parity = at_ref[1] if a < half else 1 - at_ref[1]
            column = 2 * lax.rem(at_ref[0] + turn, 4) + parity
            at = pl.ds(pl.multiple_of(column * width, width), width)
            vt_ref[a * width : (a + 1) * width, :] = val_ref[:, at].T

    for a in range(half):
        left_ref[:, a * width : (a + 1) * width] = own_ref[a]
        left_ref[:, (half + a) * width : (half + a + 1) * width] = sib_ref[a]
    for i in range(0, out_ref.shape[1], tile):
        at = slice(i, i + tile)
        out_ref[:, at] = nn(left_ref[...], vt_ref[:, at]).astype(BF)


def fold_weight(at, own, sib, values):
    value_rows, features = values.shape
    half, _, width = own.shape
    steps = 4
    rows = features // steps
    block = pl.BlockSpec((half, rows, width), lambda i, at: (0, i, 0))
    return pl.pallas_call(
        fold_kernel,
        out_shape=jax.ShapeDtypeStruct((features, value_rows), BF),
        grid_spec=pltpu.PrefetchScalarGridSpec(
            num_scalar_prefetch=1,
            grid=(steps,),
            in_specs=[block, block, whole(values.shape)],
            out_specs=pl.BlockSpec((rows, value_rows), lambda i, at: (i, 0)),
            scratch_shapes=[pltpu.VMEM((features, value_rows), BF), pltpu.VMEM((rows, features), BF)],
        ),
        compiler_params=params(MB),
        cost_estimate=cost(1, 1),
    )(at, own, sib, values)


def serve_kernel(scale, x_hbm, fold_hbm, val_hbm, y_hbm, n_hbm, c_hbm, g_hbm, s_hbm,
                 x_buf, fold_buf, val_buf, n_buf, c_buf, id_buf, g_buf, s_buf, y_buf, score_buf, cot_buf,
                 x_sem, f_sem, v_sem, y_sem, o_sem):
    rows = x_buf.shape[0]
    features = n_buf.shape[1]
    value_rows = val_buf.shape[0]
    parts = x_sem.shape[0]
    step_rows = rows // parts
    step_cols = value_rows // parts
    slots = rows // 2

    def x_copy(i):
        at = pl.ds(i * step_rows, step_rows)
        return pltpu.make_async_copy(x_hbm.at[at, :], x_buf.at[at, :], x_sem.at[i])

    def f_copy(i):
        return pltpu.make_async_copy(
            fold_hbm.at[:, pl.ds(i * step_cols, step_cols)], fold_buf.at[i], f_sem.at[i]
        )

    def v_copy(i):
        at = pl.ds(i * step_cols, step_cols)
        return pltpu.make_async_copy(val_hbm.at[at, :], val_buf.at[at, :], v_sem.at[i])

    for i in range(parts):
        x_copy(i).start()
    def load(i):
        if i < parts:
            f_copy(i).start()
            v_copy(i).start()

    take = 32
    low = lax.broadcasted_iota(jnp.int32, (take // 16, 8, 1), 1) < SLOTS

    def split(x):
        pairs = x.astype(F32).reshape(take // 16, 16, x.shape[1])
        first, second = pairs[:, :8], pairs[:, 8:]
        upper = jnp.where(low, first, pltpu.roll(second, 4, 1))
        lower = jnp.where(low, pltpu.roll(first, 4, 1), second)
        return upper.reshape(take // 2, x.shape[1]), lower.reshape(take // 2, x.shape[1])

    for i in range(parts):
        x_copy(i).wait()
        if i == parts - 2:
            load(0)

        @pl.loop(i * step_rows // take, (i + 1) * step_rows // take)
        def _(r):
            src = pl.ds(pl.multiple_of(r * take, take), take)
            dst = pl.ds(pl.multiple_of(r * (take // 2), take // 2), take // 2)
            upper, lower = split(x_buf[src, :features])
            n_buf[dst, :] = upper.astype(BF)
            c_buf[dst, :] = lower.astype(BF)
            ident, _ = split(x_buf[src, features:])
            id_buf[dst, :] = ident

    kept = [pltpu.make_async_copy(n_buf, n_hbm, o_sem.at[0]), pltpu.make_async_copy(c_buf, c_hbm, o_sem.at[1])]
    def products(j):
        f_copy(j).wait()
        v_copy(j).wait()
        load(j + 1)
        score_buf[j % 2] = nn(n_buf[...], fold_buf[j])
        cot_buf[j % 2] = nt(c_buf[...], val_buf[j * step_cols : (j + 1) * step_cols, :])

    def gate(j):
        block_of = (lax.broadcasted_iota(jnp.int32, (1, step_cols), 1) // BLOCK + j * (step_cols // BLOCK)).astype(F32)
        mine = id_buf[:, :1] == block_of
        sig = 1.0 / (1.0 + jnp.exp(score_buf[j % 2] * -scale))
        g_buf[j] = jnp.where(mine, sig, 0.0).astype(BF)
        s_buf[j] = jnp.where(mine, cot_buf[j % 2] * sig * (1.0 - sig) * scale, 0.0).astype(BF)

    products(0)
    for j in range(parts):
        if j + 1 < parts:
            products(j + 1)
        gate(j)
    for copy in kept:
        copy.start()
    for j in range(parts):
        at = pl.ds(j * step_cols, step_cols)
        kept.append(pltpu.make_async_copy(g_buf.at[j], g_hbm.at[:, at], o_sem.at[2 + j]))
        kept.append(pltpu.make_async_copy(s_buf.at[j], s_hbm.at[:, at], o_sem.at[2 + parts + j]))
        kept[-2].start()
        kept[-1].start()

    tiles = y_sem.shape[0]
    width = features // tiles
    lows = lax.broadcasted_iota(jnp.int32, (slots // 8, 8, 1), 1) < SLOTS

    def y_copy(i):
        at = pl.ds(pl.multiple_of(i * width, width), width)
        return pltpu.make_async_copy(y_buf.at[i], y_hbm.at[:, at], y_sem.at[i])

    @pl.loop(0, tiles)
    def _(i):
        at = pl.ds(pl.multiple_of(i * width, width), width)
        read = nn(g_buf[0], val_buf[0:step_cols, at])
        grad = nt(s_buf[0], fold_buf[0, at, :])
        for j in range(1, parts):
            read += nn(g_buf[j], val_buf[j * step_cols : (j + 1) * step_cols, at])
            grad += nt(s_buf[j], fold_buf[j, at, :])
        read = read.reshape(slots // 8, 8, width)
        grad = grad.reshape(slots // 8, 8, width)
        first = jnp.where(lows, read, pltpu.roll(grad, 4, 1))
        second = jnp.where(lows, pltpu.roll(read, 4, 1), grad)
        y_buf[i] = jnp.concatenate([first, second], axis=1).reshape(rows, width).astype(BF)
        y_copy(i).start()

    for copy in kept:
        copy.wait()
    for i in range(tiles):
        y_copy(i).wait()


def serve(x, fold, values, features):
    rows = x.shape[0]
    slots = rows // 2
    value_rows = values.shape[0]
    parts, tiles = 4, 4
    step_cols = value_rows // parts
    any_spec = pl.BlockSpec(memory_space=pl.ANY)
    return pl.pallas_call(
        functools.partial(serve_kernel, float(features) ** (-0.5)),
        out_shape=(
            jax.ShapeDtypeStruct((rows, features), BF),
            jax.ShapeDtypeStruct((slots, features), BF),
            jax.ShapeDtypeStruct((slots, features), BF),
            jax.ShapeDtypeStruct((slots, value_rows), BF),
            jax.ShapeDtypeStruct((slots, value_rows), BF),
        ),
        in_specs=[any_spec] * 3,
        out_specs=(any_spec,) * 5,
        scratch_shapes=[
            pltpu.VMEM(x.shape, BF),
            pltpu.VMEM((parts, features, step_cols), BF),
            pltpu.VMEM(values.shape, BF),
            pltpu.VMEM((slots, features), BF),
            pltpu.VMEM((slots, features), BF),
            pltpu.VMEM((slots, LANES), F32),
            pltpu.VMEM((parts, slots, step_cols), BF),
            pltpu.VMEM((parts, slots, step_cols), BF),
            pltpu.VMEM((tiles, rows, features // tiles), BF),
            pltpu.VMEM((2, slots, step_cols), F32),
            pltpu.VMEM((2, slots, step_cols), F32),
            pltpu.SemaphoreType.DMA((parts,)),
            pltpu.SemaphoreType.DMA((parts,)),
            pltpu.SemaphoreType.DMA((parts,)),
            pltpu.SemaphoreType.DMA((tiles,)),
            pltpu.SemaphoreType.DMA((2 + 2 * parts,)),
        ],
        compiler_params=params(MB),
        cost_estimate=cost(4 * rows * value_rows * features, 20 << 20),
    )(x, fold, values)


def grad_kernel(at_ref, own_ref, sib_ref, n_ref, c_ref, g_ref, s_ref, out_ref, gt_ref, st_ref):
    slots = n_ref.shape[0]
    tile = 256

    @pl.when(pl.program_id(0) == 0)
    def _():
        for i in range(0, slots, tile):
            gt_ref[:, i : i + tile] = g_ref[i : i + tile, :].T
            st_ref[:, i : i + tile] = s_ref[i : i + tile, :].T

    weight = jnp.where(pl.program_id(0) < 4, own_ref[0], sib_ref[0])
    queries = nn(n_ref[...], weight).astype(BF)
    for i in range(0, out_ref.shape[0], tile):
        total = nn(gt_ref[i : i + tile, :], c_ref[...]) + nn(st_ref[i : i + tile, :], queries)
        out_ref[i : i + tile, :] = total.astype(BF)


def value_grads(at, own, sib, n, c, g, s):
    half, features, width = own.shape
    slots, value_rows = g.shape
    return pl.pallas_call(
        grad_kernel,
        out_shape=jax.ShapeDtypeStruct((value_rows, features), BF),
        grid_spec=pltpu.PrefetchScalarGridSpec(
            num_scalar_prefetch=1,
            grid=(2 * half,),
            in_specs=[
                pl.BlockSpec((1, features, width), lambda a, x: (jnp.minimum(a, half - 1), 0, 0)),
                pl.BlockSpec((1, features, width), lambda a, x: (jnp.maximum(a - half, 0), 0, 0)),
                whole(n.shape),
                pl.BlockSpec((slots, width), lambda a, x: (0, slice_at(a, x))),
                whole(g.shape),
                whole(s.shape),
            ],
            out_specs=pl.BlockSpec((value_rows, width), lambda a, x: (0, slice_at(a, x))),
            scratch_shapes=[pltpu.VMEM((value_rows, slots), BF), pltpu.VMEM((value_rows, slots), BF)],
        ),
        compiler_params=params(MB),
        cost_estimate=cost(6 * slots * value_rows * features, 24 << 20),
    )(at, own, sib, n, c, g, s)


def home_kernel(back_ref, tgt_ref, wgt_ref, tok_ref, cot_ref, gain_ref, out_ref, grad_ref, pick_ref, acc_ref, rms_ref, sum_ref):
    step = pl.program_id(0)
    count, features = tok_ref.shape
    rows, width = back_ref.shape

    @pl.when(step == 0)
    def _():
        number = lax.broadcasted_iota(jnp.int32, (count, rows), 1)
        targets = tgt_ref[...]
        t0, t1 = targets[:, :1], targets[:, 1:]
        one = lambda hit: jnp.where(hit, 1.0, 0.0).astype(BF)
        pick_ref[:count, :] = one(number == t0)
        pick_ref[count : 2 * count, :] = one(number == t1)
        pick_ref[2 * count :, :] = one((number == t0 + SLOTS) | (number == t1 + SLOTS))
        exact = tok_ref[...].astype(F32)
        rms_ref[...] = lax.rsqrt(jnp.mean(exact * exact, axis=1, keepdims=True) + 1e-06)
        sum_ref[...] = jnp.zeros_like(sum_ref)

    at = pl.ds(pl.multiple_of(step * width, width), width)
    weights = wgt_ref[...]
    got = nn(pick_ref[...], back_ref[...])
    exact = tok_ref[:, at].astype(F32)
    out_ref[...] = exact + (weights[:, :1] * got[:count] + weights[:, 1:] * got[count : 2 * count])
    unit_grad = got[2 * count :] * gain_ref[:, at]
    acc_ref[:, at] = unit_grad
    rms = rms_ref[...]
    sum_ref[...] += jnp.sum(unit_grad * (exact * rms), axis=1, keepdims=True)

    @pl.when(step == pl.num_programs(0) - 1)
    def _():
        mean = sum_ref[...] * (1.0 / features)
        for i in range(0, features, width):
            cols = slice(i, i + width)
            unit = tok_ref[:, cols].astype(F32) * rms
            grad_ref[:, cols] = cot_ref[:, cols].astype(F32) + rms * (acc_ref[:, cols] - unit * mean)


def finish(back, targets, weights, tokens, cot, gain):
    count, features = tokens.shape
    rows = back.shape[0]
    steps = 4
    width = features // steps
    return pl.pallas_call(
        home_kernel,
        out_shape=(
            jax.ShapeDtypeStruct((count, features), F32),
            jax.ShapeDtypeStruct((count, features), F32),
        ),
        grid=(steps,),
        in_specs=[
            pl.BlockSpec((rows, width), lambda i: (0, i)),
            whole((count, 2)),
            whole((count, 2)),
            whole(tokens.shape),
            whole(cot.shape),
            whole((1, features)),
        ],
        out_specs=(pl.BlockSpec((count, width), lambda i: (0, i)), whole((count, features))),
        scratch_shapes=[
            pltpu.VMEM((3 * count, rows), BF),
            pltpu.VMEM((count, features), F32),
            pltpu.VMEM((count, 1), F32),
            pltpu.VMEM((count, 1), F32),
        ],
        compiler_params=params(MB),
        cost_estimate=cost(6 * count * rows * features, 10 << 20),
    )(back, targets, weights, tokens, cot, gain)


def exchange(rows):
    return lax.all_to_all(rows, ALL, split_axis=0, concat_axis=0, tiled=True)


def body(tokens, norm_gain, query_weight, values, blocks, weights, out_cotangent):
    features = tokens.shape[1]
    owners = lax.axis_size(ALL)
    at = jnp.stack([lax.axis_index("x"), lax.axis_index("core")]).astype(jnp.int32)
    gain = norm_gain.reshape(1, features)
    top, bottom = query_weight[: features // 2], query_weight[features // 2 :]
    before_top, after_bottom = turn(top, 1), turn(bottom, -1)
    before_bottom, after_top = turn(bottom, 1), turn(top, -1)
    payload, targets = build_payload(
        tokens, gain, blocks, weights, out_cotangent, owners, values.shape[0] // BLOCK
    )
    before_top, after_bottom, payload = lax.optimization_barrier((before_top, after_bottom, payload))
    own, sib = gather_weight(query_weight, [before_top, before_bottom], [after_top, after_bottom])
    got = exchange(payload)
    fold = fold_weight(at, own, sib, values)
    answers, n, c, g, s = serve(got, fold, values, features)
    back = exchange(answers)
    grad_values = value_grads(at, own, sib, n, c, g, s)
    layer_out, grad_tokens = finish(back, targets, weights, tokens, out_cotangent, gain)
    return layer_out, grad_tokens, grad_values


def solution(mesh):
    fine = Mesh(np.asarray(mesh.devices).reshape(4, 2, 4, 4), ALL)
    rows = P(ALL, None)
    return jax.shard_map(
        body,
        mesh=fine,
        in_specs=(rows, P(), P(None, ("x", "core")), rows, rows, rows, rows),
        out_specs=(rows, rows, rows),
        check_vma=False,
    )
```

```python
import functools

import jax
import jax.numpy as jnp
import numpy as np
from jax import lax
from jax.experimental import pallas as pl
from jax.experimental.pallas import tpu as pltpu
from jax.sharding import Mesh
from jax.sharding import PartitionSpec as P

BLOCK = 64
SLOTS = 4
CHUNK = 2 * SLOTS
LANES = 128
ALL = ("x", "core", "z", "y")
BF = jnp.bfloat16
F32 = jnp.float32
MB = 60


def params(megabytes):
    return pltpu.CompilerParams(vmem_limit_bytes=megabytes << 20)


def cost(flops, bytes_accessed):
    return pl.CostEstimate(
        flops=int(flops), bytes_accessed=int(bytes_accessed), transcendentals=0
    )


def whole(shape):
    return pl.BlockSpec(shape, lambda *_: (0,) * len(shape))


def nt(left, right):
    return lax.dot_general(left, right, (((1,), (1,)), ((), ())), preferred_element_type=F32)


def nn(left, right):
    return jnp.dot(left, right, preferred_element_type=F32)


def send_kernel(span, tok_ref, gain_ref, blk_ref, wgt_ref, cot_ref, x_ref, tgt_ref, rows_ref, route_ref):
    step = pl.program_id(0)
    count, features = tok_ref.shape
    step_rows = x_ref.shape[0]

    @pl.when(step == 0)
    def _():
        exact = tok_ref[...].astype(F32)
        rms = lax.rsqrt(jnp.mean(exact * exact, axis=1, keepdims=True) + 1e-06)
        rows_ref[:count, :] = ((exact * rms) * gain_ref[...]).astype(BF)
        rows_ref[count:, :] = cot_ref[...]
        square = (count, count)
        sub = lax.broadcasted_iota(jnp.int32, square, 0)
        lane = lax.broadcasted_iota(jnp.int32, square, 1)
        blocks = blk_ref[...]
        weights = wgt_ref[...]
        col = [jnp.broadcast_to(blocks[:, k : k + 1], square) for k in range(2)]
        row = [c.astype(F32).T.astype(jnp.int32) for c in col]
        wrow = [jnp.broadcast_to(weights[:, k : k + 1], square).T for k in range(2)]
        own_col = [c // span for c in col]
        own_row = [r // span for r in row]
        one = lambda hit: jnp.where(hit, 1, 0)
        before = [
            [one((own_col[0] == own_row[0]) & (sub < lane))],
            [one(own_col[0] == own_row[1]), one((own_col[1] == own_row[1]) & (sub < lane))],
        ]
        before_t = [
            [one((own_row[0] == own_col[0]) & (lane < sub))],
            [one(own_row[0] == own_col[1]), one((own_row[1] == own_col[1]) & (lane < sub))],
        ]
        for k in range(2):
            slot_row = sum(jnp.sum(e, axis=0, keepdims=True) for e in before[k])
            slot_col = sum(jnp.sum(e, axis=1, keepdims=True) for e in before_t[k])
            target = own_row[k][:1, :] * CHUNK + slot_row
            route_ref[k : k + 1, :] = target.astype(F32)
            route_ref[2 + k : 3 + k, :] = (row[k][:1, :] % span).astype(F32) + 1.0
            route_ref[4 + k : 5 + k, :] = wrow[k][:1, :]
            tgt_ref[:, k : k + 1] = own_col[k][:, :1] * CHUNK + slot_col

    route = route_ref[...]
    shape = (step_rows, count)
    number = (lax.broadcasted_iota(jnp.int32, shape, 0) + step * step_rows).astype(F32)
    t0, t1 = route[0:1, :], route[1:2, :]
    n0, n1 = number == t0, number == t1
    c0, c1 = number == t0 + SLOTS, number == t1 + SLOTS
    scale = jnp.sum(jnp.where(c0, route[4:5, :], 0.0) + jnp.where(c1, route[5:6, :], 0.0), axis=1, keepdims=True)
    ident = jnp.sum(
        jnp.where(n0 | c0, route[2:3, :], 0.0) + jnp.where(n1 | c1, route[3:4, :], 0.0),
        axis=1,
        keepdims=True,
    )
    is_cot = (lax.broadcasted_iota(jnp.int32, (step_rows, 1), 0) % CHUNK) >= SLOTS
    scale = jnp.where(is_cot, scale, 1.0)
    pick = jnp.concatenate(
        [jnp.where(n0 | n1, 1.0, 0.0), jnp.where(c0 | c1, 1.0, 0.0)], axis=1
    ).astype(BF)
    width = 512
    for at in range(0, features, width):
        rows = nn(pick, rows_ref[:, at : at + width])
        x_ref[:, at : at + width] = (rows * scale).astype(BF)
    x_ref[:, features:] = jnp.broadcast_to(ident - 1.0, (step_rows, LANES)).astype(BF)


def build_payload(tokens, gain, blocks, weights, cot, owners, span):
    count, features = tokens.shape
    rows = owners * CHUNK
    steps = 4
    return pl.pallas_call(
        functools.partial(send_kernel, span),
        out_shape=(
            jax.ShapeDtypeStruct((rows, features + LANES), BF),
            jax.ShapeDtypeStruct((count, 2), jnp.int32),
        ),
        grid=(steps,),
        in_specs=[
            whole((count, features)),
            whole((1, features)),
            whole((count, 2)),
            whole((count, 2)),
            whole((count, features)),
        ],
        out_specs=(
            pl.BlockSpec((rows // steps, features + LANES), lambda i: (i, 0)),
            whole((count, 2)),
        ),
        scratch_shapes=[pltpu.VMEM((2 * count, features), BF), pltpu.VMEM((8, count), F32)],
        compiler_params=params(MB),
        cost_estimate=cost(2 * rows * 2 * count * features, 6 << 20),
    )(tokens, gain, blocks, weights, cot)


def turn(rows, by):
    return lax.ppermute(rows, "x", [(i, (i + by) % 4) for i in range(4)])


def gather_weight(weight, before, after):
    across = jnp.concatenate([turn(before[0], 1), turn(after[1], -1)], axis=0)
    own = jnp.stack([weight, jnp.concatenate(before, axis=0), jnp.concatenate(after, axis=0), across])
    return own, lax.ppermute(own, "core", [(0, 1), (1, 0)])


def slice_at(step, at):
    turn = jnp.where(step % 4 == 0, 0, jnp.where(step % 4 == 1, 3, step % 4 - 1))
    return 2 * ((at[0] + turn) % 4) + jnp.where(step < 4, at[1], 1 - at[1])


def fold_kernel(at_ref, own_ref, sib_ref, val_ref, out_ref, vt_ref, left_ref):
    half, _, width = own_ref.shape
    tile = 256

    @pl.when(pl.program_id(0) == 0)
    def _():
        for a in range(2 * half):
            turn = (0, 3, 1, 2)[a % half]
            parity = at_ref[1] if a < half else 1 - at_ref[1]
            column = 2 * lax.rem(at_ref[0] + turn, 4) + parity
            at = pl.ds(pl.multiple_of(column * width, width), width)
            vt_ref[a * width : (a + 1) * width, :] = val_ref[:, at].T

    for a in range(half):
        left_ref[:, a * width : (a + 1) * width] = own_ref[a]
        left_ref[:, (half + a) * width : (half + a + 1) * width] = sib_ref[a]
    for i in range(0, out_ref.shape[1], tile):
        at = slice(i, i + tile)
        out_ref[:, at] = nn(left_ref[...], vt_ref[:, at]).astype(BF)


def fold_weight(at, own, sib, values):
    value_rows, features = values.shape
    half, _, width = own.shape
    steps = 4
    rows = features // steps
    block = pl.BlockSpec((half, rows, width), lambda i, at: (0, i, 0))
    return pl.pallas_call(
        fold_kernel,
        out_shape=jax.ShapeDtypeStruct((features, value_rows), BF),
        grid_spec=pltpu.PrefetchScalarGridSpec(
            num_scalar_prefetch=1,
            grid=(steps,),
            in_specs=[block, block, whole(values.shape)],
            out_specs=pl.BlockSpec((rows, value_rows), lambda i, at: (i, 0)),
            scratch_shapes=[pltpu.VMEM((features, value_rows), BF), pltpu.VMEM((rows, features), BF)],
        ),
        compiler_params=params(MB),
        cost_estimate=cost(1, 1),
    )(at, own, sib, values)


def serve_kernel(scale, x_hbm, fold_hbm, val_hbm, y_hbm, n_hbm, c_hbm, g_hbm, s_hbm,
                 x_buf, fold_buf, val_buf, n_buf, c_buf, id_buf, g_buf, s_buf, y_buf, score_buf, cot_buf,
                 x_sem, f_sem, v_sem, y_sem, o_sem):
    rows = x_buf.shape[0]
    features = n_buf.shape[1]
    value_rows = val_buf.shape[0]
    parts = x_sem.shape[0]
    step_rows = rows // parts
    step_cols = value_rows // parts
    slots = rows // 2

    def x_copy(i):
        at = pl.ds(i * step_rows, step_rows)
        return pltpu.make_async_copy(x_hbm.at[at, :], x_buf.at[at, :], x_sem.at[i])

    def f_copy(i):
        return pltpu.make_async_copy(
            fold_hbm.at[:, pl.ds(i * step_cols, step_cols)], fold_buf.at[i], f_sem.at[i]
        )

    def v_copy(i):
        at = pl.ds(i * step_cols, step_cols)
        return pltpu.make_async_copy(val_hbm.at[at, :], val_buf.at[at, :], v_sem.at[i])

    for i in range(parts):
        x_copy(i).start()
    def load(i):
        if i < parts:
            f_copy(i).start()
            v_copy(i).start()

    take = 32
    low = lax.broadcasted_iota(jnp.int32, (take // 16, 8, 1), 1) < SLOTS

    def split(x):
        pairs = x.astype(F32).reshape(take // 16, 16, x.shape[1])
        first, second = pairs[:, :8], pairs[:, 8:]
        upper = jnp.where(low, first, pltpu.roll(second, 4, 1))
        lower = jnp.where(low, pltpu.roll(first, 4, 1), second)
        return upper.reshape(take // 2, x.shape[1]), lower.reshape(take // 2, x.shape[1])

    for i in range(parts):
        x_copy(i).wait()
        if i == parts - 2:
            load(0)

        @pl.loop(i * step_rows // take, (i + 1) * step_rows // take)
        def _(r):
            src = pl.ds(pl.multiple_of(r * take, take), take)
            dst = pl.ds(pl.multiple_of(r * (take // 2), take // 2), take // 2)
            upper, lower = split(x_buf[src, :features])
            n_buf[dst, :] = upper.astype(BF)
            c_buf[dst, :] = lower.astype(BF)
            ident, _ = split(x_buf[src, features:])
            id_buf[dst, :] = ident

    kept = [pltpu.make_async_copy(n_buf, n_hbm, o_sem.at[0]), pltpu.make_async_copy(c_buf, c_hbm, o_sem.at[1])]
    def products(j):
        f_copy(j).wait()
        v_copy(j).wait()
        load(j + 1)
        score_buf[j % 2] = nn(n_buf[...], fold_buf[j])
        cot_buf[j % 2] = nt(c_buf[...], val_buf[j * step_cols : (j + 1) * step_cols, :])

    def gate(j):
        block_of = (lax.broadcasted_iota(jnp.int32, (1, step_cols), 1) // BLOCK + j * (step_cols // BLOCK)).astype(F32)
        mine = id_buf[:, :1] == block_of
        sig = 1.0 / (1.0 + jnp.exp(score_buf[j % 2] * -scale))
        g_buf[j] = jnp.where(mine, sig, 0.0).astype(BF)
        s_buf[j] = jnp.where(mine, cot_buf[j % 2] * sig * (1.0 - sig) * scale, 0.0).astype(BF)

    products(0)
    for j in range(parts):
        if j + 1 < parts:
            products(j + 1)
        gate(j)
    for copy in kept:
        copy.start()
    for j in range(parts):
        at = pl.ds(j * step_cols, step_cols)
        kept.append(pltpu.make_async_copy(g_buf.at[j], g_hbm.at[:, at], o_sem.at[2 + j]))
        kept.append(pltpu.make_async_copy(s_buf.at[j], s_hbm.at[:, at], o_sem.at[2 + parts + j]))
        kept[-2].start()
        kept[-1].start()

    tiles = y_sem.shape[0]
    width = features // tiles
    lows = lax.broadcasted_iota(jnp.int32, (slots // 8, 8, 1), 1) < SLOTS

    def y_copy(i):
        at = pl.ds(pl.multiple_of(i * width, width), width)
        return pltpu.make_async_copy(y_buf.at[i], y_hbm.at[:, at], y_sem.at[i])

    @pl.loop(0, tiles)
    def _(i):
        at = pl.ds(pl.multiple_of(i * width, width), width)
        read = nn(g_buf[0], val_buf[0:step_cols, at])
        grad = nt(s_buf[0], fold_buf[0, at, :])
        for j in range(1, parts):
            read += nn(g_buf[j], val_buf[j * step_cols : (j + 1) * step_cols, at])
            grad += nt(s_buf[j], fold_buf[j, at, :])
        read = read.reshape(slots // 8, 8, width)
        grad = grad.reshape(slots // 8, 8, width)
        first = jnp.where(lows, read, pltpu.roll(grad, 4, 1))
        second = jnp.where(lows, pltpu.roll(read, 4, 1), grad)
        y_buf[i] = jnp.concatenate([first, second], axis=1).reshape(rows, width).astype(BF)
        y_copy(i).start()

    for copy in kept:
        copy.wait()
    for i in range(tiles):
        y_copy(i).wait()


def serve(x, fold, values, features):
    rows = x.shape[0]
    slots = rows // 2
    value_rows = values.shape[0]
    parts, tiles = 4, 4
    step_cols = value_rows // parts
    any_spec = pl.BlockSpec(memory_space=pl.ANY)
    return pl.pallas_call(
        functools.partial(serve_kernel, float(features) ** (-0.5)),
        out_shape=(
            jax.ShapeDtypeStruct((rows, features), BF),
            jax.ShapeDtypeStruct((slots, features), BF),
            jax.ShapeDtypeStruct((slots, features), BF),
            jax.ShapeDtypeStruct((slots, value_rows), BF),
            jax.ShapeDtypeStruct((slots, value_rows), BF),
        ),
        in_specs=[any_spec] * 3,
        out_specs=(any_spec,) * 5,
        scratch_shapes=[
            pltpu.VMEM(x.shape, BF),
            pltpu.VMEM((parts, features, step_cols), BF),
            pltpu.VMEM(values.shape, BF),
            pltpu.VMEM((slots, features), BF),
            pltpu.VMEM((slots, features), BF),
            pltpu.VMEM((slots, LANES), F32),
            pltpu.VMEM((parts, slots, step_cols), BF),
            pltpu.VMEM((parts, slots, step_cols), BF),
            pltpu.VMEM((tiles, rows, features // tiles), BF),
            pltpu.VMEM((2, slots, step_cols), F32),
            pltpu.VMEM((2, slots, step_cols), F32),
            pltpu.SemaphoreType.DMA((parts,)),
            pltpu.SemaphoreType.DMA((parts,)),
            pltpu.SemaphoreType.DMA((parts,)),
            pltpu.SemaphoreType.DMA((tiles,)),
            pltpu.SemaphoreType.DMA((2 + 2 * parts,)),
        ],
        compiler_params=params(MB),
        cost_estimate=cost(4 * rows * value_rows * features, 20 << 20),
    )(x, fold, values)


def grad_kernel(at_ref, own_ref, sib_ref, n_ref, c_ref, g_ref, s_ref, out_ref, gt_ref, st_ref):
    slots = n_ref.shape[0]
    tile = 256

    @pl.when(pl.program_id(0) == 0)
    def _():
        for i in range(0, slots, tile):
            gt_ref[:, i : i + tile] = g_ref[i : i + tile, :].T
            st_ref[:, i : i + tile] = s_ref[i : i + tile, :].T

    weight = jnp.where(pl.program_id(0) < 4, own_ref[0], sib_ref[0])
    queries = nn(n_ref[...], weight).astype(BF)
    for i in range(0, out_ref.shape[0], tile):
        total = nn(gt_ref[i : i + tile, :], c_ref[...]) + nn(st_ref[i : i + tile, :], queries)
        out_ref[i : i + tile, :] = total.astype(BF)


def value_grads(at, own, sib, n, c, g, s):
    half, features, width = own.shape
    slots, value_rows = g.shape
    return pl.pallas_call(
        grad_kernel,
        out_shape=jax.ShapeDtypeStruct((value_rows, features), BF),
        grid_spec=pltpu.PrefetchScalarGridSpec(
            num_scalar_prefetch=1,
            grid=(2 * half,),
            in_specs=[
                pl.BlockSpec((1, features, width), lambda a, x: (jnp.minimum(a, half - 1), 0, 0)),
                pl.BlockSpec((1, features, width), lambda a, x: (jnp.maximum(a - half, 0), 0, 0)),
                whole(n.shape),
                pl.BlockSpec((slots, width), lambda a, x: (0, slice_at(a, x))),
                whole(g.shape),
                whole(s.shape),
            ],
            out_specs=pl.BlockSpec((value_rows, width), lambda a, x: (0, slice_at(a, x))),
            scratch_shapes=[pltpu.VMEM((value_rows, slots), BF), pltpu.VMEM((value_rows, slots), BF)],
        ),
        compiler_params=params(MB),
        cost_estimate=cost(6 * slots * value_rows * features, 24 << 20),
    )(at, own, sib, n, c, g, s)


def home_kernel(back_ref, tgt_ref, wgt_ref, tok_ref, cot_ref, gain_ref, out_ref, grad_ref, pick_ref, acc_ref, rms_ref, sum_ref):
    step = pl.program_id(0)
    count, features = tok_ref.shape
    rows, width = back_ref.shape

    @pl.when(step == 0)
    def _():
        number = lax.broadcasted_iota(jnp.int32, (count, rows), 1)
        targets = tgt_ref[...]
        t0, t1 = targets[:, :1], targets[:, 1:]
        one = lambda hit: jnp.where(hit, 1.0, 0.0).astype(BF)
        pick_ref[:count, :] = one(number == t0)
        pick_ref[count : 2 * count, :] = one(number == t1)
        pick_ref[2 * count :, :] = one((number == t0 + SLOTS) | (number == t1 + SLOTS))
        exact = tok_ref[...].astype(F32)
        rms_ref[...] = lax.rsqrt(jnp.mean(exact * exact, axis=1, keepdims=True) + 1e-06)
        sum_ref[...] = jnp.zeros_like(sum_ref)

    at = pl.ds(pl.multiple_of(step * width, width), width)
    weights = wgt_ref[...]
    got = nn(pick_ref[...], back_ref[...])
    exact = tok_ref[:, at].astype(F32)
    out_ref[...] = exact + (weights[:, :1] * got[:count] + weights[:, 1:] * got[count : 2 * count])
    unit_grad = got[2 * count :] * gain_ref[:, at]
    acc_ref[:, at] = unit_grad
    rms = rms_ref[...]
    sum_ref[...] += jnp.sum(unit_grad * (exact * rms), axis=1, keepdims=True)

    @pl.when(step == pl.num_programs(0) - 1)
    def _():
        mean = sum_ref[...] * (1.0 / features)
        for i in range(0, features, width):
            cols = slice(i, i + width)
            unit = tok_ref[:, cols].astype(F32) * rms
            grad_ref[:, cols] = cot_ref[:, cols].astype(F32) + rms * (acc_ref[:, cols] - unit * mean)


def finish(back, targets, weights, tokens, cot, gain):
    count, features = tokens.shape
    rows = back.shape[0]
    steps = 4
    width = features // steps
    return pl.pallas_call(
        home_kernel,
        out_shape=(
            jax.ShapeDtypeStruct((count, features), F32),
            jax.ShapeDtypeStruct((count, features), F32),
        ),
        grid=(steps,),
        in_specs=[
            pl.BlockSpec((rows, width), lambda i: (0, i)),
            whole((count, 2)),
            whole((count, 2)),
            whole(tokens.shape),
            whole(cot.shape),
            whole((1, features)),
        ],
        out_specs=(pl.BlockSpec((count, width), lambda i: (0, i)), whole((count, features))),
        scratch_shapes=[
            pltpu.VMEM((3 * count, rows), BF),
            pltpu.VMEM((count, features), F32),
            pltpu.VMEM((count, 1), F32),
            pltpu.VMEM((count, 1), F32),
        ],
        compiler_params=params(MB),
        cost_estimate=cost(6 * count * rows * features, 10 << 20),
    )(back, targets, weights, tokens, cot, gain)


def exchange(rows):
    return lax.all_to_all(rows, ALL, split_axis=0, concat_axis=0, tiled=True)


def body(tokens, norm_gain, query_weight, values, blocks, weights, out_cotangent):
    features = tokens.shape[1]
    owners = lax.axis_size(ALL)
    at = jnp.stack([lax.axis_index("x"), lax.axis_index("core")]).astype(jnp.int32)
    gain = norm_gain.reshape(1, features)
    top, bottom = query_weight[: features // 2], query_weight[features // 2 :]
    before_top, after_bottom = turn(top, 1), turn(bottom, -1)
    payload, targets = build_payload(
        tokens, gain, blocks, weights, out_cotangent, owners, values.shape[0] // BLOCK
    )
    before_top, after_bottom, top, bottom, payload = lax.optimization_barrier(
        (before_top, after_bottom, top, bottom, payload)
    )
    before_bottom, after_top = turn(bottom, 1), turn(top, -1)
    own, sib = gather_weight(query_weight, [before_top, before_bottom], [after_top, after_bottom])
    got = exchange(payload)
    fold = fold_weight(at, own, sib, values)
    answers, n, c, g, s = serve(got, fold, values, features)
    back = exchange(answers)
    grad_values = value_grads(at, own, sib, n, c, g, s)
    layer_out, grad_tokens = finish(back, targets, weights, tokens, out_cotangent, gain)
    return layer_out, grad_tokens, grad_values


def solution(mesh):
    fine = Mesh(np.asarray(mesh.devices).reshape(4, 2, 4, 4), ALL)
    rows = P(ALL, None)
    return jax.shard_map(
        body,
        mesh=fine,
        in_specs=(rows, P(), P(None, ("x", "core")), rows, rows, rows, rows),
        out_specs=(rows, rows, rows),
        check_vma=False,
    )
```

```python
import functools

import jax
import jax.numpy as jnp
import numpy as np
from jax import lax
from jax.experimental import pallas as pl
from jax.experimental.pallas import tpu as pltpu
from jax.sharding import Mesh
from jax.sharding import PartitionSpec as P

BLOCK = 64
SLOTS = 4
CHUNK = 2 * SLOTS
LANES = 128
ALL = ("x", "core", "z", "y")
BF = jnp.bfloat16
F32 = jnp.float32
MB = 60


def params(megabytes):
    return pltpu.CompilerParams(vmem_limit_bytes=megabytes << 20)


def cost(flops, bytes_accessed):
    return pl.CostEstimate(
        flops=int(flops), bytes_accessed=int(bytes_accessed), transcendentals=0
    )


def whole(shape):
    return pl.BlockSpec(shape, lambda *_: (0,) * len(shape))


def nt(left, right):
    return lax.dot_general(left, right, (((1,), (1,)), ((), ())), preferred_element_type=F32)


def nn(left, right):
    return jnp.dot(left, right, preferred_element_type=F32)


def send_kernel(span, tok_ref, gain_ref, blk_ref, wgt_ref, cot_ref, x_ref, tgt_ref, rows_ref, route_ref):
    step = pl.program_id(0)
    count, features = tok_ref.shape
    step_rows = x_ref.shape[0]

    @pl.when(step == 0)
    def _():
        exact = tok_ref[...].astype(F32)
        rms = lax.rsqrt(jnp.mean(exact * exact, axis=1, keepdims=True) + 1e-06)
        rows_ref[:count, :] = ((exact * rms) * gain_ref[...]).astype(BF)
        rows_ref[count:, :] = cot_ref[...]
        square = (count, count)
        sub = lax.broadcasted_iota(jnp.int32, square, 0)
        lane = lax.broadcasted_iota(jnp.int32, square, 1)
        blocks = blk_ref[...]
        weights = wgt_ref[...]
        col = [jnp.broadcast_to(blocks[:, k : k + 1], square) for k in range(2)]
        row = [c.astype(F32).T.astype(jnp.int32) for c in col]
        wrow = [jnp.broadcast_to(weights[:, k : k + 1], square).T for k in range(2)]
        own_col = [c // span for c in col]
        own_row = [r // span for r in row]
        one = lambda hit: jnp.where(hit, 1, 0)
        before = [
            [one((own_col[0] == own_row[0]) & (sub < lane))],
            [one(own_col[0] == own_row[1]), one((own_col[1] == own_row[1]) & (sub < lane))],
        ]
        before_t = [
            [one((own_row[0] == own_col[0]) & (lane < sub))],
            [one(own_row[0] == own_col[1]), one((own_row[1] == own_col[1]) & (lane < sub))],
        ]
        for k in range(2):
            slot_row = sum(jnp.sum(e, axis=0, keepdims=True) for e in before[k])
            slot_col = sum(jnp.sum(e, axis=1, keepdims=True) for e in before_t[k])
            target = own_row[k][:1, :] * CHUNK + slot_row
            route_ref[k : k + 1, :] = target.astype(F32)
            route_ref[2 + k : 3 + k, :] = (row[k][:1, :] % span).astype(F32) + 1.0
            route_ref[4 + k : 5 + k, :] = wrow[k][:1, :]
            tgt_ref[:, k : k + 1] = own_col[k][:, :1] * CHUNK + slot_col

    route = route_ref[...]
    shape = (step_rows, count)
    number = (lax.broadcasted_iota(jnp.int32, shape, 0) + step * step_rows).astype(F32)
    t0, t1 = route[0:1, :], route[1:2, :]
    n0, n1 = number == t0, number == t1
    c0, c1 = number == t0 + SLOTS, number == t1 + SLOTS
    scale = jnp.sum(jnp.where(c0, route[4:5, :], 0.0) + jnp.where(c1, route[5:6, :], 0.0), axis=1, keepdims=True)
    ident = jnp.sum(
        jnp.where(n0 | c0, route[2:3, :], 0.0) + jnp.where(n1 | c1, route[3:4, :], 0.0),
        axis=1,
        keepdims=True,
    )
    is_cot = (lax.broadcasted_iota(jnp.int32, (step_rows, 1), 0) % CHUNK) >= SLOTS
    scale = jnp.where(is_cot, scale, 1.0)
    pick = jnp.concatenate(
        [jnp.where(n0 | n1, 1.0, 0.0), jnp.where(c0 | c1, 1.0, 0.0)], axis=1
    ).astype(BF)
    width = 512
    for at in range(0, features, width):
        rows = nn(pick, rows_ref[:, at : at + width])
        x_ref[:, at : at + width] = (rows * scale).astype(BF)
    x_ref[:, features:] = jnp.broadcast_to(ident - 1.0, (step_rows, LANES)).astype(BF)


def build_payload(tokens, gain, blocks, weights, cot, owners, span):
    count, features = tokens.shape
    rows = owners * CHUNK
    steps = 4
    return pl.pallas_call(
        functools.partial(send_kernel, span),
        out_shape=(
            jax.ShapeDtypeStruct((rows, features + LANES), BF),
            jax.ShapeDtypeStruct((count, 2), jnp.int32),
        ),
        grid=(steps,),
        in_specs=[
            whole((count, features)),
            whole((1, features)),
            whole((count, 2)),
            whole((count, 2)),
            whole((count, features)),
        ],
        out_specs=(
            pl.BlockSpec((rows // steps, features + LANES), lambda i: (i, 0)),
            whole((count, 2)),
        ),
        scratch_shapes=[pltpu.VMEM((2 * count, features), BF), pltpu.VMEM((8, count), F32)],
        compiler_params=params(MB),
        cost_estimate=cost(2 * rows * 2 * count * features, 6 << 20),
    )(tokens, gain, blocks, weights, cot)


def turn(rows, by):
    return lax.ppermute(rows, "x", [(i, (i + by) % 4) for i in range(4)])


def gather_weight(weight, before, after):
    across = jnp.concatenate([turn(before[0], 1), turn(after[1], -1)], axis=0)
    own = jnp.stack([weight, jnp.concatenate(before, axis=0), jnp.concatenate(after, axis=0), across])
    return own, lax.ppermute(own, "core", [(0, 1), (1, 0)])


def slice_at(step, at):
    turn = jnp.where(step % 4 == 0, 0, jnp.where(step % 4 == 1, 3, step % 4 - 1))
    return 2 * ((at[0] + turn) % 4) + jnp.where(step < 4, at[1], 1 - at[1])


def fold_kernel(at_ref, own_ref, sib_ref, val_ref, out_ref, vt_ref, left_ref):
    half, _, width = own_ref.shape
    tile = 256

    @pl.when(pl.program_id(0) == 0)
    def _():
        for a in range(2 * half):
            turn = (0, 3, 1, 2)[a % half]
            parity = at_ref[1] if a < half else 1 - at_ref[1]
            column = 2 * lax.rem(at_ref[0] + turn, 4) + parity
            at = pl.ds(pl.multiple_of(column * width, width), width)
            vt_ref[a * width : (a + 1) * width, :] = val_ref[:, at].T

    for a in range(half):
        left_ref[:, a * width : (a + 1) * width] = own_ref[a]
        left_ref[:, (half + a) * width : (half + a + 1) * width] = sib_ref[a]
    for i in range(0, out_ref.shape[1], tile):
        at = slice(i, i + tile)
        out_ref[:, at] = nn(left_ref[...], vt_ref[:, at]).astype(BF)


def fold_weight(at, own, sib, values):
    value_rows, features = values.shape
    half, _, width = own.shape
    steps = 4
    rows = features // steps
    block = pl.BlockSpec((half, rows, width), lambda i, at: (0, i, 0))
    return pl.pallas_call(
        fold_kernel,
        out_shape=jax.ShapeDtypeStruct((features, value_rows), BF),
        grid_spec=pltpu.PrefetchScalarGridSpec(
            num_scalar_prefetch=1,
            grid=(steps,),
            in_specs=[block, block, whole(values.shape)],
            out_specs=pl.BlockSpec((rows, value_rows), lambda i, at: (i, 0)),
            scratch_shapes=[pltpu.VMEM((features, value_rows), BF), pltpu.VMEM((rows, features), BF)],
        ),
        compiler_params=params(MB),
        cost_estimate=cost(1, 1),
    )(at, own, sib, values)


def serve_kernel(scale, x_hbm, fold_hbm, val_hbm, y_hbm, n_hbm, c_hbm, g_hbm, s_hbm,
                 x_buf, fold_buf, val_buf, n_buf, c_buf, id_buf, g_buf, s_buf, y_buf, score_buf, cot_buf,
                 x_sem, f_sem, v_sem, y_sem, o_sem):
    rows = x_buf.shape[0]
    features = n_buf.shape[1]
    value_rows = val_buf.shape[0]
    parts = x_sem.shape[0]
    step_rows = rows // parts
    step_cols = value_rows // parts
    slots = rows // 2

    def x_copy(i):
        at = pl.ds(i * step_rows, step_rows)
        return pltpu.make_async_copy(x_hbm.at[at, :], x_buf.at[at, :], x_sem.at[i])

    def f_copy(i):
        return pltpu.make_async_copy(
            fold_hbm.at[:, pl.ds(i * step_cols, step_cols)], fold_buf.at[i], f_sem.at[i]
        )

    def v_copy(i):
        at = pl.ds(i * step_cols, step_cols)
        return pltpu.make_async_copy(val_hbm.at[at, :], val_buf.at[at, :], v_sem.at[i])

    for i in range(parts):
        x_copy(i).start()
    def load(i):
        if i < parts:
            f_copy(i).start()
            v_copy(i).start()

    take = 32
    low = lax.broadcasted_iota(jnp.int32, (take // 16, 8, 1), 1) < SLOTS

    def split(x):
        pairs = x.astype(F32).reshape(take // 16, 16, x.shape[1])
        first, second = pairs[:, :8], pairs[:, 8:]
        upper = jnp.where(low, first, pltpu.roll(second, 4, 1))
        lower = jnp.where(low, pltpu.roll(first, 4, 1), second)
        return upper.reshape(take // 2, x.shape[1]), lower.reshape(take // 2, x.shape[1])

    for i in range(parts):
        x_copy(i).wait()
        if i == parts - 2:
            load(0)

        @pl.loop(i * step_rows // take, (i + 1) * step_rows // take)
        def _(r):
            src = pl.ds(pl.multiple_of(r * take, take), take)
            dst = pl.ds(pl.multiple_of(r * (take // 2), take // 2), take // 2)
            upper, lower = split(x_buf[src, :features])
            n_buf[dst, :] = upper.astype(BF)
            c_buf[dst, :] = lower.astype(BF)
            ident, _ = split(x_buf[src, features:])
            id_buf[dst, :] = ident

    kept = [pltpu.make_async_copy(n_buf, n_hbm, o_sem.at[0]), pltpu.make_async_copy(c_buf, c_hbm, o_sem.at[1])]
    def products(j):
        f_copy(j).wait()
        v_copy(j).wait()
        load(j + 1)
        score_buf[j % 2] = nn(n_buf[...], fold_buf[j])
        cot_buf[j % 2] = nt(c_buf[...], val_buf[j * step_cols : (j + 1) * step_cols, :])

    def gate(j):
        block_of = (lax.broadcasted_iota(jnp.int32, (1, step_cols), 1) // BLOCK + j * (step_cols // BLOCK)).astype(F32)
        mine = id_buf[:, :1] == block_of
        sig = 1.0 / (1.0 + jnp.exp(score_buf[j % 2] * -scale))
        g_buf[j] = jnp.where(mine, sig, 0.0).astype(BF)
        s_buf[j] = jnp.where(mine, cot_buf[j % 2] * sig * (1.0 - sig) * scale, 0.0).astype(BF)

    products(0)
    for j in range(parts):
        if j + 1 < parts:
            products(j + 1)
        gate(j)
    for copy in kept:
        copy.start()
    for j in range(parts):
        at = pl.ds(j * step_cols, step_cols)
        kept.append(pltpu.make_async_copy(g_buf.at[j], g_hbm.at[:, at], o_sem.at[2 + j]))
        kept.append(pltpu.make_async_copy(s_buf.at[j], s_hbm.at[:, at], o_sem.at[2 + parts + j]))
        kept[-2].start()
        kept[-1].start()

    tiles = y_sem.shape[0]
    width = features // tiles
    lows = lax.broadcasted_iota(jnp.int32, (slots // 8, 8, 1), 1) < SLOTS

    def y_copy(i):
        at = pl.ds(pl.multiple_of(i * width, width), width)
        return pltpu.make_async_copy(y_buf.at[i], y_hbm.at[:, at], y_sem.at[i])

    @pl.loop(0, tiles)
    def _(i):
        at = pl.ds(pl.multiple_of(i * width, width), width)
        read = nn(g_buf[0], val_buf[0:step_cols, at])
        grad = nt(s_buf[0], fold_buf[0, at, :])
        for j in range(1, parts):
            read += nn(g_buf[j], val_buf[j * step_cols : (j + 1) * step_cols, at])
            grad += nt(s_buf[j], fold_buf[j, at, :])
        read = read.reshape(slots // 8, 8, width)
        grad = grad.reshape(slots // 8, 8, width)
        first = jnp.where(lows, read, pltpu.roll(grad, 4, 1))
        second = jnp.where(lows, pltpu.roll(read, 4, 1), grad)
        y_buf[i] = jnp.concatenate([first, second], axis=1).reshape(rows, width).astype(BF)
        y_copy(i).start()

    for copy in kept:
        copy.wait()
    for i in range(tiles):
        y_copy(i).wait()


def serve(x, fold, values, features):
    rows = x.shape[0]
    slots = rows // 2
    value_rows = values.shape[0]
    parts, tiles = 4, 4
    step_cols = value_rows // parts
    any_spec = pl.BlockSpec(memory_space=pl.ANY)
    return pl.pallas_call(
        functools.partial(serve_kernel, float(features) ** (-0.5)),
        out_shape=(
            jax.ShapeDtypeStruct((rows, features), BF),
            jax.ShapeDtypeStruct((slots, features), BF),
            jax.ShapeDtypeStruct((slots, features), BF),
            jax.ShapeDtypeStruct((slots, value_rows), BF),
            jax.ShapeDtypeStruct((slots, value_rows), BF),
        ),
        in_specs=[any_spec] * 3,
        out_specs=(any_spec,) * 5,
        scratch_shapes=[
            pltpu.VMEM(x.shape, BF),
            pltpu.VMEM((parts, features, step_cols), BF),
            pltpu.VMEM(values.shape, BF),
            pltpu.VMEM((slots, features), BF),
            pltpu.VMEM((slots, features), BF),
            pltpu.VMEM((slots, LANES), F32),
            pltpu.VMEM((parts, slots, step_cols), BF),
            pltpu.VMEM((parts, slots, step_cols), BF),
            pltpu.VMEM((tiles, rows, features // tiles), BF),
            pltpu.VMEM((2, slots, step_cols), F32),
            pltpu.VMEM((2, slots, step_cols), F32),
            pltpu.SemaphoreType.DMA((parts,)),
            pltpu.SemaphoreType.DMA((parts,)),
            pltpu.SemaphoreType.DMA((parts,)),
            pltpu.SemaphoreType.DMA((tiles,)),
            pltpu.SemaphoreType.DMA((2 + 2 * parts,)),
        ],
        compiler_params=params(MB),
        cost_estimate=cost(4 * rows * value_rows * features, 20 << 20),
    )(x, fold, values)


def grad_kernel(at_ref, own_ref, sib_ref, n_ref, c_ref, g_ref, s_ref, out_ref, gt_ref, st_ref):
    slots = n_ref.shape[0]
    tile = 256

    @pl.when(pl.program_id(0) == 0)
    def _():
        for i in range(0, slots, tile):
            gt_ref[:, i : i + tile] = g_ref[i : i + tile, :].T
            st_ref[:, i : i + tile] = s_ref[i : i + tile, :].T

    weight = jnp.where(pl.program_id(0) < 4, own_ref[0], sib_ref[0])
    queries = nn(n_ref[...], weight).astype(BF)
    for i in range(0, out_ref.shape[0], tile):
        total = nn(gt_ref[i : i + tile, :], c_ref[...]) + nn(st_ref[i : i + tile, :], queries)
        out_ref[i : i + tile, :] = total.astype(BF)


def value_grads(at, own, sib, n, c, g, s):
    half, features, width = own.shape
    slots, value_rows = g.shape
    return pl.pallas_call(
        grad_kernel,
        out_shape=jax.ShapeDtypeStruct((value_rows, features), BF),
        grid_spec=pltpu.PrefetchScalarGridSpec(
            num_scalar_prefetch=1,
            grid=(2 * half,),
            in_specs=[
                pl.BlockSpec((1, features, width), lambda a, x: (jnp.minimum(a, half - 1), 0, 0)),
                pl.BlockSpec((1, features, width), lambda a, x: (jnp.maximum(a - half, 0), 0, 0)),
                whole(n.shape),
                pl.BlockSpec((slots, width), lambda a, x: (0, slice_at(a, x))),
                whole(g.shape),
                whole(s.shape),
            ],
            out_specs=pl.BlockSpec((value_rows, width), lambda a, x: (0, slice_at(a, x))),
            scratch_shapes=[pltpu.VMEM((value_rows, slots), BF), pltpu.VMEM((value_rows, slots), BF)],
        ),
        compiler_params=params(MB),
        cost_estimate=cost(6 * slots * value_rows * features, 24 << 20),
    )(at, own, sib, n, c, g, s)


def home_kernel(back_ref, tgt_ref, wgt_ref, tok_ref, cot_ref, gain_ref, out_ref, grad_ref, pick_ref, acc_ref, rms_ref, sum_ref):
    step = pl.program_id(0)
    count, features = tok_ref.shape
    rows, width = back_ref.shape

    @pl.when(step == 0)
    def _():
        number = lax.broadcasted_iota(jnp.int32, (count, rows), 1)
        targets = tgt_ref[...]
        t0, t1 = targets[:, :1], targets[:, 1:]
        one = lambda hit: jnp.where(hit, 1.0, 0.0).astype(BF)
        pick_ref[:count, :] = one(number == t0)
        pick_ref[count : 2 * count, :] = one(number == t1)
        pick_ref[2 * count :, :] = one((number == t0 + SLOTS) | (number == t1 + SLOTS))
        exact = tok_ref[...].astype(F32)
        rms_ref[...] = lax.rsqrt(jnp.mean(exact * exact, axis=1, keepdims=True) + 1e-06)
        sum_ref[...] = jnp.zeros_like(sum_ref)

    at = pl.ds(pl.multiple_of(step * width, width), width)
    weights = wgt_ref[...]
    got = nn(pick_ref[...], back_ref[...])
    exact = tok_ref[:, at].astype(F32)
    out_ref[...] = exact + (weights[:, :1] * got[:count] + weights[:, 1:] * got[count : 2 * count])
    unit_grad = got[2 * count :] * gain_ref[:, at]
    acc_ref[:, at] = unit_grad
    rms = rms_ref[...]
    sum_ref[...] += jnp.sum(unit_grad * (exact * rms), axis=1, keepdims=True)

    @pl.when(step == pl.num_programs(0) - 1)
    def _():
        mean = sum_ref[...] * (1.0 / features)
        for i in range(0, features, width):
            cols = slice(i, i + width)
            unit = tok_ref[:, cols].astype(F32) * rms
            grad_ref[:, cols] = cot_ref[:, cols].astype(F32) + rms * (acc_ref[:, cols] - unit * mean)


def finish(back, targets, weights, tokens, cot, gain):
    count, features = tokens.shape
    rows = back.shape[0]
    steps = 8
    width = features // steps
    return pl.pallas_call(
        home_kernel,
        out_shape=(
            jax.ShapeDtypeStruct((count, features), F32),
            jax.ShapeDtypeStruct((count, features), F32),
        ),
        grid=(steps,),
        in_specs=[
            pl.BlockSpec((rows, width), lambda i: (0, i)),
            whole((count, 2)),
            whole((count, 2)),
            whole(tokens.shape),
            whole(cot.shape),
            whole((1, features)),
        ],
        out_specs=(pl.BlockSpec((count, width), lambda i: (0, i)), whole((count, features))),
        scratch_shapes=[
            pltpu.VMEM((3 * count, rows), BF),
            pltpu.VMEM((count, features), F32),
            pltpu.VMEM((count, 1), F32),
            pltpu.VMEM((count, 1), F32),
        ],
        compiler_params=params(MB),
        cost_estimate=cost(6 * count * rows * features, 10 << 20),
    )(back, targets, weights, tokens, cot, gain)


def exchange(rows):
    return lax.all_to_all(rows, ALL, split_axis=0, concat_axis=0, tiled=True)


def body(tokens, norm_gain, query_weight, values, blocks, weights, out_cotangent):
    features = tokens.shape[1]
    owners = lax.axis_size(ALL)
    at = jnp.stack([lax.axis_index("x"), lax.axis_index("core")]).astype(jnp.int32)
    gain = norm_gain.reshape(1, features)
    top, bottom = query_weight[: features // 2], query_weight[features // 2 :]
    before_top, after_bottom = turn(top, 1), turn(bottom, -1)
    before_bottom, after_top = turn(bottom, 1), turn(top, -1)
    payload, targets = build_payload(
        tokens, gain, blocks, weights, out_cotangent, owners, values.shape[0] // BLOCK
    )
    before_top, after_bottom, payload = lax.optimization_barrier((before_top, after_bottom, payload))
    own, sib = gather_weight(query_weight, [before_top, before_bottom], [after_top, after_bottom])
    got = exchange(payload)
    fold = fold_weight(at, own, sib, values)
    answers, n, c, g, s = serve(got, fold, values, features)
    back = exchange(answers)
    grad_values = value_grads(at, own, sib, n, c, g, s)
    layer_out, grad_tokens = finish(back, targets, weights, tokens, out_cotangent, gain)
    return layer_out, grad_tokens, grad_values


def solution(mesh):
    fine = Mesh(np.asarray(mesh.devices).reshape(4, 2, 4, 4), ALL)
    rows = P(ALL, None)
    return jax.shard_map(
        body,
        mesh=fine,
        in_specs=(rows, P(), P(None, ("x", "core")), rows, rows, rows, rows),
        out_specs=(rows, rows, rows),
        check_vma=False,
    )
```
